256 devices in a mesh: gx: 32 (over y, x, core), gy: 8 (over z).
Axes of the slice: x: 4, y: 4, z: 8, core: 2. Of those that a mesh axis runs over, the one named last changes fastest.
Arguments:
- atmos: float32 [5, 48, 256, 1024], P(None, None, 'gx', 'gy'), may hold values from -4 to 4
- level_set: float32 [2048, 8192], P('gx', 'gy'), may hold values from -8 to 8
- fuel_left: float32 [2048, 8192], P('gx', 'gy'), may hold values from 0.3 to 1
- fuel_map: int32 [2048, 8192], P('gx', 'gy'), may hold values from 0 to 12
- spread_rate: float32 [13], replicated, may hold values from 0.04 to 0.15
- wind_factor: float32 [13], replicated, may hold values from 0.1 to 0.5
- burn_time: float32 [13], replicated, may hold values from 3 to 20
- heat_yield: float32 [13], replicated, may hold values from 1 to 4
- burn_tiles: int32 [32, 8, 16], P('gx', 'gy'), may hold values from 0 to 15, as said below
- burn_count: int32 [32, 8], P('gx', 'gy'), may hold values from 1 to 16, as said below
- substep_count: int32 [32, 128], P('gx', 'gy'), may hold values from 1 to 8, as said below
Outputs:
- atmos_next: float32 [5, 48, 256, 1024], P(None, None, 'gx', 'gy')
- level_next: float32 [2048, 8192], P('gx', 'gy')
- fuel_next: float32 [2048, 8192], P('gx', 'gy')
The draws below stay inside these ranges and needn't reach their ends.
Inputs may be any that keep to these rules, and one draw needn't show every extreme that they name: `burn_tiles`: each device's 16 entries are distinct local tile numbers; some device has all 16 entries valid. `burn_count`: some device has 16 burning tiles. `substep_count`: some tile takes 8 substeps.
All inputs are finite; a program needn't handle non-finite values.
Results may differ from the reference program's by a relative error of at most 0.000075.
Values sent between devices are 32-bit elements; how exact they have to be, the bound alone decides.
A program may use at most 64 MiB of HBM per device.

```python
import math
import jax
import jax.numpy as jnp

LEVELS = 48
RF = 8
TILE = 64
SUBSTEPS = 8
BURN = 16
NCAT = 13
NXA = 256
NYA = 1024
NXF = 2048
NYF = 8192
TXD = 1
TYD = 16
NTX = 32
NTY = 128
N_GX = 32
N_GY = 8


def draw_full_one(key, shape_total, most):
    first_key, second_key = jax.random.split(key)
    counts = jax.random.randint(first_key, (shape_total,), 1, most + 1)
    chosen = jax.random.randint(second_key, (), 0, shape_total)
    return jnp.where(jnp.arange(shape_total) == chosen, most, counts).astype(jnp.int32)


def draw_burn_count(key, part):
    return draw_full_one(key, N_GX * N_GY, BURN).reshape(N_GX, N_GY)


def draw_substep_count(key, part):
    return draw_full_one(key, NTX * NTY, SUBSTEPS).reshape(NTX, NTY)


def draw_burn_tiles(key, part):
    tiles_dev = TXD * TYD
    scores = jax.random.randint(key, (N_GX, N_GY, tiles_dev), 0, 65536) * tiles_dev + jnp.arange(tiles_dev)
    ordering = jnp.argsort(scores, axis=-1, stable=True)
    return ordering[..., :BURN].astype(jnp.int32)


def set_ends(result, rng, low, largest):
    place = [jax.random.randint(jax.random.fold_in(rng, axis), (), 0, length) for axis, length in enumerate(result.shape)]
    widest = result.shape.index(max(result.shape))
    next_to = place[:widest] + [(place[widest] + 1) % result.shape[widest]] + place[widest + 1:]
    return result.at[tuple(place)].set(low).at[tuple(next_to)].set(largest)


def steps_of(key, extent, cuts, smallest, largest):
    level = 1.0
    for axis_at, blocks in cuts:
        heights = jax.random.uniform(jax.random.fold_in(jax.random.fold_in(key, 6), axis_at), (blocks,), jnp.float32, smallest / len(cuts), largest / len(cuts))
        level = level * jnp.repeat(jnp.exp(heights), extent[axis_at] // blocks).reshape((-1,) + (1,) * (len(extent) - 1 - axis_at))
    return level


def bell_draw(own_key, shape, deviation, bound, cuts=(), held_as=jnp.bfloat16):
    level = steps_of(own_key, shape, cuts, -0.22, 0.18) if cuts else 1.0
    entries = jax.random.normal(own_key, shape, jnp.float32) * deviation * level
    return jnp.minimum(jnp.maximum(entries, -bound), bound).astype(held_as)


def setup_inputs(seed: int = 0) -> dict:
    splits = jax.random.split(jax.random.key(seed), 12)
    return {
        "atmos": bell_draw(splits[0], (5, LEVELS, NXA, NYA), 1.0, 4.0, ((2, 32), (3, 8)), jnp.float32),
        "level_set": bell_draw(splits[1], (NXF, NYF), 2.0, 8.0, ((0, 32), (1, 8)), jnp.float32),
        "fuel_left": jnp.clip(0.3 + 0.7 * jax.random.uniform(splits[2], (NXF, NYF), jnp.float32) ** steps_of(splits[2], (NXF, NYF), ((0, 32), (1, 8)), -0.2, 0.2), 0.3, 1.0),
        "fuel_map": set_ends(jax.random.randint(splits[3], (NXF, NYF), 0, NCAT), jax.random.fold_in(splits[3], 1), 0, NCAT - 1).astype(jnp.int32),
        "spread_rate": jnp.clip(jnp.exp(jax.random.uniform(splits[4], (NCAT,), jnp.float32, math.log(0.04), math.log(0.15))), 0.04, 0.15),
        "wind_factor": jnp.clip(jnp.exp(jax.random.uniform(splits[5], (NCAT,), jnp.float32, math.log(0.1), math.log(0.5))), 0.1, 0.5),
        "burn_time": jnp.clip(jnp.exp(jax.random.uniform(splits[6], (NCAT,), jnp.float32, math.log(3.0), math.log(20.0))), 3.0, 20.0),
        "heat_yield": jnp.clip(jnp.exp(jax.random.uniform(splits[7], (NCAT,), jnp.float32, math.log(1.0), math.log(4.0))), 1.0, 4.0),
        "burn_tiles": draw_burn_tiles(jax.random.fold_in(splits[11], 71), 0),
        "burn_count": draw_burn_count(jax.random.fold_in(splits[11], 71), 0),
        "substep_count": draw_substep_count(jax.random.fold_in(splits[11], 71), 0),
    }


COURANT = 0.2
DIFFUSE = 0.05

def advance(padded, level, remaining, heating, spread, gain, burnout, yields, wind_u, wind_v, active):
    back_x = level - padded[..., 1:-3, 2:-2]
    ahead_x = padded[..., 3:-1, 2:-2] - level
    back_y = level - padded[..., 2:-2, 1:-3]
    ahead_y = padded[..., 2:-2, 3:-1] - level
    upwind = jnp.sqrt(jnp.maximum(back_x, 0.0) ** 2 + jnp.minimum(ahead_x, 0.0) ** 2 + jnp.maximum(back_y, 0.0) ** 2 + jnp.minimum(ahead_y, 0.0) ** 2)
    slope_x = (padded[..., :-4, 2:-2] - 8.0 * padded[..., 1:-3, 2:-2] + 8.0 * padded[..., 3:-1, 2:-2] - padded[..., 4:, 2:-2]) / 12.0
    slope_y = (padded[..., 2:-2, :-4] - 8.0 * padded[..., 2:-2, 1:-3] + 8.0 * padded[..., 2:-2, 3:-1] - padded[..., 2:-2, 4:]) / 12.0
    pushing = jnp.maximum(wind_u * slope_x + wind_v * slope_y, 0.0)
    advanced = level - spread * (upwind + gain * pushing)
    burned = remaining / (1.0 + jnp.exp(advanced)) / burnout
    return (jnp.where(active, advanced, level), jnp.where(active, remaining - burned, remaining), heating + jnp.where(active, yields * burned, 0.0))

def atmos_step(padded, heat_atm):
    width_x = padded.shape[2] - 6
    width_y = padded.shape[3] - 6

    def shifted(along_x, along_y):
        return padded[:, :, 3 + along_x:3 + along_x + width_x, 3 + along_y:3 + along_y + width_y]
    centre = shifted(0, 0)
    deriv_x = (shifted(3, 0) - 9.0 * shifted(2, 0) + 45.0 * shifted(1, 0) - 45.0 * shifted(-1, 0) + 9.0 * shifted(-2, 0) - shifted(-3, 0)) / 60.0
    deriv_y = (shifted(0, 3) - 9.0 * shifted(0, 2) + 45.0 * shifted(0, 1) - 45.0 * shifted(0, -1) + 9.0 * shifted(0, -2) - shifted(0, -3)) / 60.0
    laplace = shifted(1, 0) + shifted(-1, 0) + shifted(0, 1) + shifted(0, -1) - 4.0 * centre
    updated = centre - COURANT * (centre[0:1] * deriv_x + centre[1:2] * deriv_y) + DIFFUSE * laplace
    depth = padded.shape[1]
    profile = jnp.exp(-4.0 * jnp.arange(depth).astype(jnp.float32) / depth)
    return updated.at[3].add(heat_atm[None, :, :] * profile[:, None, None])

def lower_weights(count, ratio):
    indices = jnp.arange(count).astype(jnp.int32)
    coarse = indices // ratio
    within = indices % ratio
    lower = jnp.where(within < ratio // 2, coarse, coarse + 1).astype(jnp.int32)
    weight = (within.astype(jnp.float32) + 0.5) / ratio + jnp.where(within < ratio // 2, 0.5, -0.5)
    return (lower, weight)

def reference(atmos, level_set, fuel_left, fuel_map, spread_rate, wind_factor, burn_time, heat_yield, burn_tiles, burn_count, substep_count):
    surface = jnp.pad(atmos[0:2, 0], ((0, 0), (1, 1), (1, 1)))
    lower_x, weight_x = lower_weights(NXF, RF)
    lower_y, weight_y = lower_weights(NYF, RF)
    along = (1.0 - weight_x)[None, :, None] * surface[:, lower_x, :] + weight_x[None, :, None] * surface[:, lower_x + 1, :]
    winds = (1.0 - weight_y)[None, None, :] * along[:, :, lower_y] + weight_y[None, None, :] * along[:, :, lower_y + 1]
    spread = spread_rate[fuel_map]
    gain = wind_factor[fuel_map]
    burnout = burn_time[fuel_map]
    yields = heat_yield[fuel_map]
    tiles_dev = TXD * TYD
    slot_valid = jnp.arange(BURN).astype(jnp.int32)[None, None, :] < burn_count[:, :, None]
    matches = (burn_tiles[..., None] == jnp.arange(tiles_dev).astype(jnp.int32)[None, None, None, :]) & slot_valid[..., None]
    tile_on = jnp.any(matches, axis=2).reshape(N_GX, N_GY, TXD, TYD).transpose(0, 2, 1, 3).reshape(NTX, NTY)
    level, remaining = (level_set, fuel_left)
    heating = jnp.zeros_like(level_set)
    for substep in range(SUBSTEPS):
        tile_active = tile_on & (substep < substep_count)
        active = jnp.repeat(jnp.repeat(tile_active, TILE, axis=0), TILE, axis=1)
        padded = jnp.pad(level, 2)
        level, remaining, heating = advance(padded, level, remaining, heating, spread, gain, burnout, yields, winds[0], winds[1], active)
    heat_atm = heating.reshape(NXA, RF, NYA, RF).sum(axis=(1, 3)) / (RF * RF)
    padded_atm = jnp.pad(atmos, ((0, 0), (0, 0), (3, 3), (3, 3)))
    return (atmos_step(padded_atm, heat_atm), level, remaining)
```

```python
import jax
import jax.numpy as jnp
from jax import lax
from jax.sharding import PartitionSpec as P

RF = 8
TILE = 64
SUBSTEPS = 8


COURANT = 0.2
DIFFUSE = 0.05


def extended(cells, sides, width):
    for axis, dim in sides:
        count = lax.axis_size(axis)
        ends = count - 1
        head = lax.slice_in_dim(cells, 0, width, axis=dim)
        tail = lax.slice_in_dim(cells, cells.shape[dim] - width, cells.shape[dim], axis=dim)
        cells = jnp.concatenate(
            [
                lax.ppermute(tail, axis, [(i, (i + 1) % count) for i in range(ends)]),
                cells,
                lax.ppermute(head, axis, [((i + 1) % count, i) for i in range(ends)]),
            ],
            axis=dim,
        )
    return cells


def advance(
    padded, level, remaining, heating, spread, gain, burnout, yields, wind_u, wind_v, active
):
    back_x = level - padded[..., 1:-3, 2:-2]
    ahead_x = padded[..., 3:-1, 2:-2] - level
    back_y = level - padded[..., 2:-2, 1:-3]
    ahead_y = padded[..., 2:-2, 3:-1] - level
    upwind = jnp.sqrt(
        jnp.maximum(back_x, 0.0) ** 2
        + jnp.minimum(ahead_x, 0.0) ** 2
        + jnp.maximum(back_y, 0.0) ** 2
        + jnp.minimum(ahead_y, 0.0) ** 2
    )
    slope_x = (
        padded[..., :-4, 2:-2]
        - 8.0 * padded[..., 1:-3, 2:-2]
        + 8.0 * padded[..., 3:-1, 2:-2]
        - padded[..., 4:, 2:-2]
    ) / 12.0
    slope_y = (
        padded[..., 2:-2, :-4]
        - 8.0 * padded[..., 2:-2, 1:-3]
        + 8.0 * padded[..., 2:-2, 3:-1]
        - padded[..., 2:-2, 4:]
    ) / 12.0
    pushing = jnp.maximum(wind_u * slope_x + wind_v * slope_y, 0.0)
    advanced = level - spread * (upwind + gain * pushing)
    burned = remaining / (1.0 + jnp.exp(advanced)) / burnout
    return (
        jnp.where(active, advanced, level),
        jnp.where(active, remaining - burned, remaining),
        heating + jnp.where(active, yields * burned, 0.0),
    )


def spread_level(padded, level, spread, gain, wind_u, wind_v):
    back_x = level - padded[..., 1:-3, 2:-2]
    ahead_x = padded[..., 3:-1, 2:-2] - level
    back_y = level - padded[..., 2:-2, 1:-3]
    ahead_y = padded[..., 2:-2, 3:-1] - level
    upwind = jnp.sqrt(
        jnp.maximum(back_x, 0.0) ** 2
        + jnp.minimum(ahead_x, 0.0) ** 2
        + jnp.maximum(back_y, 0.0) ** 2
        + jnp.minimum(ahead_y, 0.0) ** 2
    )
    slope_x = (
        padded[..., :-4, 2:-2]
        - 8.0 * padded[..., 1:-3, 2:-2]
        + 8.0 * padded[..., 3:-1, 2:-2]
        - padded[..., 4:, 2:-2]
    ) / 12.0
    slope_y = (
        padded[..., 2:-2, :-4]
        - 8.0 * padded[..., 2:-2, 1:-3]
        + 8.0 * padded[..., 2:-2, 3:-1]
        - padded[..., 2:-2, 4:]
    ) / 12.0
    pushing = jnp.maximum(wind_u * slope_x + wind_v * slope_y, 0.0)
    return level - spread * (upwind + gain * pushing)


def atmos_step(padded, heat_atm):
    width_x = padded.shape[2] - 6
    width_y = padded.shape[3] - 6

    def shifted(along_x, along_y):
        return padded[
            :, :, 3 + along_x : 3 + along_x + width_x, 3 + along_y : 3 + along_y + width_y
        ]

    centre = shifted(0, 0)
    deriv_x = (
        shifted(3, 0)
        - 9.0 * shifted(2, 0)
        + 45.0 * shifted(1, 0)
        - 45.0 * shifted(-1, 0)
        + 9.0 * shifted(-2, 0)
        - shifted(-3, 0)
    ) / 60.0
    deriv_y = (
        shifted(0, 3)
        - 9.0 * shifted(0, 2)
        + 45.0 * shifted(0, 1)
        - 45.0 * shifted(0, -1)
        + 9.0 * shifted(0, -2)
        - shifted(0, -3)
    ) / 60.0
    laplace = shifted(1, 0) + shifted(-1, 0) + shifted(0, 1) + shifted(0, -1) - 4.0 * centre
    updated = centre - COURANT * (centre[0:1] * deriv_x + centre[1:2] * deriv_y) + DIFFUSE * laplace
    depth = padded.shape[1]
    profile = jnp.exp(-4.0 * jnp.arange(depth).astype(jnp.float32) / depth)
    return updated.at[3].add(heat_atm[None, :, :] * profile[:, None, None])


def interp_table(count, ratio, extra):
    indices = jnp.arange(count + 2 * extra) - extra
    coarse = indices // ratio
    within = indices % ratio
    lower = jnp.where(within < ratio // 2, coarse, coarse + 1) + 2
    weight = (within.astype(jnp.float32) + 0.5) / ratio + jnp.where(within < ratio // 2, 0.5, -0.5)
    columns = jnp.arange(count // ratio + 6)
    return (1.0 - weight)[:, None] * (columns[None, :] == lower[:, None]) + weight[:, None] * (
        columns[None, :] == lower[:, None] + 1
    )


def surface_winds(surface, fire_rows, fire_cols, extra):
    table_x = interp_table(fire_rows, RF, extra)
    table_y = interp_table(fire_cols, RF, extra)
    along = jnp.einsum("ia,kab->kib", table_x, surface, precision=lax.Precision.HIGHEST)
    return jnp.einsum("kib,jb->kij", along, table_y, precision=lax.Precision.HIGHEST)


def fire_halo(level):
    return extended(level, (("gx", 0), ("gy", 1)), 2)


def shards(
    atmos,
    level_set,
    fuel_left,
    fuel_map,
    spread_rate,
    wind_factor,
    burn_time,
    heat_yield,
    burn_tiles,
    burn_count,
    substep_count,
):
    fire_rows, fire_cols = level_set.shape
    atmos_rows, atmos_cols = (atmos.shape[2], atmos.shape[3])
    padded_atm = extended(atmos, (("gx", 2), ("gy", 3)), 3)
    surface = padded_atm[0:2, 0]
    spread = jnp.zeros(level_set.shape, jnp.float32)
    gain = jnp.zeros(level_set.shape, jnp.float32)
    burnout = jnp.ones(level_set.shape, jnp.float32)
    yields = jnp.zeros(level_set.shape, jnp.float32)
    for category in range(spread_rate.shape[0]):
        picked = fuel_map == category
        spread = jnp.where(picked, spread_rate[category], spread)
        gain = jnp.where(picked, wind_factor[category], gain)
        burnout = jnp.where(picked, burn_time[category], burnout)
        yields = jnp.where(picked, heat_yield[category], yields)
    slots = burn_tiles.reshape(-1)
    listed = burn_count.reshape(())
    tiles_dev = substep_count.size
    slot_valid = jnp.arange(slots.shape[0]) < listed
    tile_on = jnp.any(
        (slots[:, None] == jnp.arange(tiles_dev)[None, :]) & slot_valid[:, None], axis=0
    )
    tile_on = tile_on.reshape(substep_count.shape)
    tiles_x, tiles_y = substep_count.shape
    halo = 2 * SUBSTEPS
    nsteps = jnp.where(tile_on, substep_count, 0).astype(jnp.float32)
    nsteps = jnp.broadcast_to(nsteps[:, None, :, None], (tiles_x, TILE, tiles_y, TILE)).reshape(
        fire_rows, fire_cols
    )
    stacked = extended(
        jnp.stack([level_set, spread, gain, nsteps]), (("gx", 1), ("gy", 2)), halo
    )
    level, spread_ext, gain_ext, nsteps_ext = stacked[0], stacked[1], stacked[2], stacked[3]
    winds = surface_winds(surface, fire_rows, fire_cols, halo)
    inner = (slice(halo, halo + fire_rows), slice(halo, halo + fire_cols))
    remaining = fuel_left
    heating = jnp.zeros_like(level_set)
    for substep in range(SUBSTEPS):
        active_ext = substep < nsteps_ext
        padded = jnp.pad(level, 2)
        moved = spread_level(padded, level, spread_ext, gain_ext, winds[0], winds[1])
        burned = remaining / (1.0 + jnp.exp(moved[inner])) / burnout
        active = active_ext[inner]
        remaining, heating = (
            jnp.where(active, remaining - burned, remaining),
            heating + jnp.where(active, yields * burned, 0.0),
        )
        level = jnp.where(active_ext, moved, level)
    level = level[inner]
    heat_atm = heating.reshape(atmos_rows, RF, atmos_cols, RF).sum(axis=(1, 3)) / (RF * RF)
    return (atmos_step(padded_atm, heat_atm), level, remaining)


def solution(mesh):
    return jax.shard_map(
        shards,
        mesh=mesh,
        in_specs=(
            P(None, None, "gx", "gy"),
            P("gx", "gy"),
            P("gx", "gy"),
            P("gx", "gy"),
            P(),
            P(),
            P(),
            P(),
            P("gx", "gy", None),
            P("gx", "gy"),
            P("gx", "gy"),
        ),
        out_specs=(P(None, None, "gx", "gy"), P("gx", "gy"), P("gx", "gy")),
        check_vma=False,
    )
```

```python
import jax
import jax.numpy as jnp
from jax import lax
from jax.sharding import PartitionSpec as P
from jax.experimental import pallas as pl
from jax.experimental.pallas import tpu as pltpu

RF = 8
TILE = 64
SUBSTEPS = 8


COURANT = 0.2
DIFFUSE = 0.05


def extended(cells, sides, width):
    for axis, dim in sides:
        count = lax.axis_size(axis)
        ends = count - 1
        head = lax.slice_in_dim(cells, 0, width, axis=dim)
        tail = lax.slice_in_dim(cells, cells.shape[dim] - width, cells.shape[dim], axis=dim)
        cells = jnp.concatenate(
            [
                lax.ppermute(tail, axis, [(i, (i + 1) % count) for i in range(ends)]),
                cells,
                lax.ppermute(head, axis, [((i + 1) % count, i) for i in range(ends)]),
            ],
            axis=dim,
        )
    return cells


def advance(
    padded, level, remaining, heating, spread, gain, burnout, yields, wind_u, wind_v, active
):
    back_x = level - padded[..., 1:-3, 2:-2]
    ahead_x = padded[..., 3:-1, 2:-2] - level
    back_y = level - padded[..., 2:-2, 1:-3]
    ahead_y = padded[..., 2:-2, 3:-1] - level
    upwind = jnp.sqrt(
        jnp.maximum(back_x, 0.0) ** 2
        + jnp.minimum(ahead_x, 0.0) ** 2
        + jnp.maximum(back_y, 0.0) ** 2
        + jnp.minimum(ahead_y, 0.0) ** 2
    )
    slope_x = (
        padded[..., :-4, 2:-2]
        - 8.0 * padded[..., 1:-3, 2:-2]
        + 8.0 * padded[..., 3:-1, 2:-2]
        - padded[..., 4:, 2:-2]
    ) / 12.0
    slope_y = (
        padded[..., 2:-2, :-4]
        - 8.0 * padded[..., 2:-2, 1:-3]
        + 8.0 * padded[..., 2:-2, 3:-1]
        - padded[..., 2:-2, 4:]
    ) / 12.0
    pushing = jnp.maximum(wind_u * slope_x + wind_v * slope_y, 0.0)
    advanced = level - spread * (upwind + gain * pushing)
    burned = remaining / (1.0 + jnp.exp(advanced)) / burnout
    return (
        jnp.where(active, advanced, level),
        jnp.where(active, remaining - burned, remaining),
        heating + jnp.where(active, yields * burned, 0.0),
    )


def spread_level(padded, level, spread, gain, wind_u, wind_v):
    back_x = level - padded[..., 1:-3, 2:-2]
    ahead_x = padded[..., 3:-1, 2:-2] - level
    back_y = level - padded[..., 2:-2, 1:-3]
    ahead_y = padded[..., 2:-2, 3:-1] - level
    upwind = jnp.sqrt(
        jnp.maximum(back_x, 0.0) ** 2
        + jnp.minimum(ahead_x, 0.0) ** 2
        + jnp.maximum(back_y, 0.0) ** 2
        + jnp.minimum(ahead_y, 0.0) ** 2
    )
    slope_x = (
        padded[..., :-4, 2:-2]
        - 8.0 * padded[..., 1:-3, 2:-2]
        + 8.0 * padded[..., 3:-1, 2:-2]
        - padded[..., 4:, 2:-2]
    ) / 12.0
    slope_y = (
        padded[..., 2:-2, :-4]
        - 8.0 * padded[..., 2:-2, 1:-3]
        + 8.0 * padded[..., 2:-2, 3:-1]
        - padded[..., 2:-2, 4:]
    ) / 12.0
    pushing = jnp.maximum(wind_u * slope_x + wind_v * slope_y, 0.0)
    return level - spread * (upwind + gain * pushing)


def atmos_step(padded, heat_atm):
    width_x = padded.shape[2] - 6
    width_y = padded.shape[3] - 6

    def shifted(along_x, along_y):
        return padded[
            :, :, 3 + along_x : 3 + along_x + width_x, 3 + along_y : 3 + along_y + width_y
        ]

    centre = shifted(0, 0)
    deriv_x = (
        shifted(3, 0)
        - 9.0 * shifted(2, 0)
        + 45.0 * shifted(1, 0)
        - 45.0 * shifted(-1, 0)
        + 9.0 * shifted(-2, 0)
        - shifted(-3, 0)
    ) / 60.0
    deriv_y = (
        shifted(0, 3)
        - 9.0 * shifted(0, 2)
        + 45.0 * shifted(0, 1)
        - 45.0 * shifted(0, -1)
        + 9.0 * shifted(0, -2)
        - shifted(0, -3)
    ) / 60.0
    laplace = shifted(1, 0) + shifted(-1, 0) + shifted(0, 1) + shifted(0, -1) - 4.0 * centre
    updated = centre - COURANT * (centre[0:1] * deriv_x + centre[1:2] * deriv_y) + DIFFUSE * laplace
    depth = padded.shape[1]
    profile = jnp.exp(-4.0 * jnp.arange(depth).astype(jnp.float32) / depth)
    return updated.at[3].add(heat_atm[None, :, :] * profile[:, None, None])


def interp_table(count, ratio, extra):
    indices = jnp.arange(count + 2 * extra) - extra
    coarse = indices // ratio
    within = indices % ratio
    lower = jnp.where(within < ratio // 2, coarse, coarse + 1) + 2
    weight = (within.astype(jnp.float32) + 0.5) / ratio + jnp.where(within < ratio // 2, 0.5, -0.5)
    columns = jnp.arange(count // ratio + 6)
    return (1.0 - weight)[:, None] * (columns[None, :] == lower[:, None]) + weight[:, None] * (
        columns[None, :] == lower[:, None] + 1
    )


def surface_winds(surface, fire_rows, fire_cols, extra_x, extra_y):
    table_x = interp_table(fire_rows, RF, extra_x)
    table_y = interp_table(fire_cols, RF, extra_y)
    along = jnp.einsum("ia,kab->kib", table_x, surface, precision=lax.Precision.HIGHEST)
    return jnp.einsum("kib,jb->kij", along, table_y, precision=lax.Precision.HIGHEST)


HALO_Y = 128


def shift(a, d, axis):
    return pltpu.roll(a, (-d) % a.shape[axis], axis)


def lookup(tab_ref, cat, row, default):
    ncat = tab_ref.shape[0] // 4
    out = jnp.full(cat.shape, default, jnp.float32)
    for category in range(ncat):
        out = jnp.where(cat == float(category), tab_ref[row * ncat + category], out)
    return out


def fire_kernel(tab_ref, ext_ref, wind_ref, fuel_ref, level_out, fuel_out, heat_out):
    rows, cols = fuel_ref.shape
    hx = (ext_ref.shape[1] - rows) // 2
    hy = (ext_ref.shape[2] - cols) // 2
    inner = (slice(hx, hx + rows), slice(hy, hy + cols))
    level = ext_ref[0]
    cat = ext_ref[1]
    nsteps = ext_ref[2]
    spread = lookup(tab_ref, cat, 0, 0.0)
    gain = lookup(tab_ref, cat, 1, 0.0)
    cat_in = cat[inner]
    burnout = lookup(tab_ref, cat_in, 2, 1.0)
    yields = lookup(tab_ref, cat_in, 3, 0.0)
    nsteps_in = nsteps[inner]
    wind_u = wind_ref[0]
    wind_v = wind_ref[1]
    remaining = fuel_ref[...]
    heating = jnp.zeros_like(remaining)
    for substep in range(SUBSTEPS):
        xm1 = shift(level, -1, 0)
        xp1 = shift(level, 1, 0)
        ym1 = shift(level, -1, 1)
        yp1 = shift(level, 1, 1)
        back_x = level - xm1
        ahead_x = xp1 - level
        back_y = level - ym1
        ahead_y = yp1 - level
        upwind = jnp.sqrt(
            jnp.maximum(back_x, 0.0) ** 2
            + jnp.minimum(ahead_x, 0.0) ** 2
            + jnp.maximum(back_y, 0.0) ** 2
            + jnp.minimum(ahead_y, 0.0) ** 2
        )
        slope_x = (shift(level, -2, 0) - 8.0 * xm1 + 8.0 * xp1 - shift(level, 2, 0)) / 12.0
        slope_y = (shift(level, -2, 1) - 8.0 * ym1 + 8.0 * yp1 - shift(level, 2, 1)) / 12.0
        pushing = jnp.maximum(wind_u * slope_x + wind_v * slope_y, 0.0)
        moved = level - spread * (upwind + gain * pushing)
        burned = remaining / (1.0 + jnp.exp(moved[inner])) / burnout
        active = float(substep) < nsteps_in
        remaining = jnp.where(active, remaining - burned, remaining)
        heating = heating + jnp.where(active, yields * burned, 0.0)
        level = jnp.where(float(substep) < nsteps, moved, level)
    level_out[...] = level[inner]
    fuel_out[...] = remaining
    heat_out[...] = heating.reshape(rows // RF, RF, cols).sum(axis=1)


def fire_step(tables, ext, winds, fuel_left):
    rows, cols = fuel_left.shape
    vmem = pl.BlockSpec(memory_space=pltpu.VMEM)
    return pl.pallas_call(
        fire_kernel,
        out_shape=(
            jax.ShapeDtypeStruct((rows, cols), jnp.float32),
            jax.ShapeDtypeStruct((rows, cols), jnp.float32),
            jax.ShapeDtypeStruct((rows // RF, cols), jnp.float32),
        ),
        in_specs=[pl.BlockSpec(memory_space=pltpu.SMEM), vmem, vmem, vmem],
        out_specs=(vmem, vmem, vmem),
    )(tables, ext, winds, fuel_left)


def fire_halo(level):
    return extended(level, (("gx", 0), ("gy", 1)), 2)


def shards(
    atmos,
    level_set,
    fuel_left,
    fuel_map,
    spread_rate,
    wind_factor,
    burn_time,
    heat_yield,
    burn_tiles,
    burn_count,
    substep_count,
):
    fire_rows, fire_cols = level_set.shape
    atmos_rows, atmos_cols = (atmos.shape[2], atmos.shape[3])
    padded_atm = extended(atmos, (("gx", 2), ("gy", 3)), 3)
    surface = padded_atm[0:2, 0]
    slots = burn_tiles.reshape(-1)
    listed = burn_count.reshape(())
    tiles_dev = substep_count.size
    slot_valid = jnp.arange(slots.shape[0]) < listed
    tile_on = jnp.any(
        (slots[:, None] == jnp.arange(tiles_dev)[None, :]) & slot_valid[:, None], axis=0
    )
    tile_on = tile_on.reshape(substep_count.shape)
    tiles_x, tiles_y = substep_count.shape
    halo = 2 * SUBSTEPS
    nsteps = jnp.where(tile_on, substep_count, 0).astype(jnp.float32)
    nsteps = jnp.broadcast_to(nsteps[:, None, :, None], (tiles_x, TILE, tiles_y, TILE)).reshape(
        fire_rows, fire_cols
    )
    stacked = jnp.stack([level_set, fuel_map.astype(jnp.float32), nsteps])
    stacked = extended(stacked, (("gx", 1), ("gy", 2)), halo)
    room = jnp.zeros(stacked.shape[:2] + (HALO_Y - halo,), jnp.float32)
    stacked = jnp.concatenate([room, stacked, room], axis=2)
    winds = surface_winds(surface, fire_rows, fire_cols, halo, HALO_Y)
    tables = jnp.concatenate([spread_rate, wind_factor, burn_time, heat_yield]).astype(jnp.float32)
    level, remaining, heat_rows = fire_step(tables, stacked, winds, fuel_left)
    heat_atm = heat_rows.reshape(atmos_rows, atmos_cols, RF).sum(axis=2) / (RF * RF)
    return (atmos_step(padded_atm, heat_atm), level, remaining)


def solution(mesh):
    return jax.shard_map(
        shards,
        mesh=mesh,
        in_specs=(
            P(None, None, "gx", "gy"),
            P("gx", "gy"),
            P("gx", "gy"),
            P("gx", "gy"),
            P(),
            P(),
            P(),
            P(),
            P("gx", "gy", None),
            P("gx", "gy"),
            P("gx", "gy"),
        ),
        out_specs=(P(None, None, "gx", "gy"), P("gx", "gy"), P("gx", "gy")),
        check_vma=False,
    )
```

```python
import jax
import jax.numpy as jnp
from jax import lax
from jax.sharding import PartitionSpec as P
from jax.experimental import pallas as pl
from jax.experimental.pallas import tpu as pltpu

RF = 8
TILE = 64
SUBSTEPS = 8


COURANT = 0.2
DIFFUSE = 0.05


def extended(cells, sides, width):
    for axis, dim in sides:
        count = lax.axis_size(axis)
        ends = count - 1
        head = lax.slice_in_dim(cells, 0, width, axis=dim)
        tail = lax.slice_in_dim(cells, cells.shape[dim] - width, cells.shape[dim], axis=dim)
        cells = jnp.concatenate(
            [
                lax.ppermute(tail, axis, [(i, (i + 1) % count) for i in range(ends)]),
                cells,
                lax.ppermute(head, axis, [((i + 1) % count, i) for i in range(ends)]),
            ],
            axis=dim,
        )
    return cells


def swap_ends(groups, axis):
    count = lax.axis_size(axis)
    ends = count - 1
    heads = [lax.slice_in_dim(a, 0, w, axis=d) for a, d, w in groups]
    tails = [lax.slice_in_dim(a, a.shape[d] - w, a.shape[d], axis=d) for a, d, w in groups]

    def pack(parts):
        return jnp.concatenate([p.reshape(-1) for p in parts])

    def unpack(flat, parts):
        out, at = [], 0
        for p in parts:
            out.append(flat[at : at + p.size].reshape(p.shape))
            at += p.size
        return out

    below = unpack(lax.ppermute(pack(tails), axis, [(i, i + 1) for i in range(ends)]), tails)
    above = unpack(lax.ppermute(pack(heads), axis, [(i + 1, i) for i in range(ends)]), heads)
    return [
        jnp.concatenate([lo, a, hi], axis=d) for (a, d, w), lo, hi in zip(groups, below, above)
    ]


def advance(
    padded, level, remaining, heating, spread, gain, burnout, yields, wind_u, wind_v, active
):
    back_x = level - padded[..., 1:-3, 2:-2]
    ahead_x = padded[..., 3:-1, 2:-2] - level
    back_y = level - padded[..., 2:-2, 1:-3]
    ahead_y = padded[..., 2:-2, 3:-1] - level
    upwind = jnp.sqrt(
        jnp.maximum(back_x, 0.0) ** 2
        + jnp.minimum(ahead_x, 0.0) ** 2
        + jnp.maximum(back_y, 0.0) ** 2
        + jnp.minimum(ahead_y, 0.0) ** 2
    )
    slope_x = (
        padded[..., :-4, 2:-2]
        - 8.0 * padded[..., 1:-3, 2:-2]
        + 8.0 * padded[..., 3:-1, 2:-2]
        - padded[..., 4:, 2:-2]
    ) / 12.0
    slope_y = (
        padded[..., 2:-2, :-4]
        - 8.0 * padded[..., 2:-2, 1:-3]
        + 8.0 * padded[..., 2:-2, 3:-1]
        - padded[..., 2:-2, 4:]
    ) / 12.0
    pushing = jnp.maximum(wind_u * slope_x + wind_v * slope_y, 0.0)
    advanced = level - spread * (upwind + gain * pushing)
    burned = remaining / (1.0 + jnp.exp(advanced)) / burnout
    return (
        jnp.where(active, advanced, level),
        jnp.where(active, remaining - burned, remaining),
        heating + jnp.where(active, yields * burned, 0.0),
    )


def spread_level(padded, level, spread, gain, wind_u, wind_v):
    back_x = level - padded[..., 1:-3, 2:-2]
    ahead_x = padded[..., 3:-1, 2:-2] - level
    back_y = level - padded[..., 2:-2, 1:-3]
    ahead_y = padded[..., 2:-2, 3:-1] - level
    upwind = jnp.sqrt(
        jnp.maximum(back_x, 0.0) ** 2
        + jnp.minimum(ahead_x, 0.0) ** 2
        + jnp.maximum(back_y, 0.0) ** 2
        + jnp.minimum(ahead_y, 0.0) ** 2
    )
    slope_x = (
        padded[..., :-4, 2:-2]
        - 8.0 * padded[..., 1:-3, 2:-2]
        + 8.0 * padded[..., 3:-1, 2:-2]
        - padded[..., 4:, 2:-2]
    ) / 12.0
    slope_y = (
        padded[..., 2:-2, :-4]
        - 8.0 * padded[..., 2:-2, 1:-3]
        + 8.0 * padded[..., 2:-2, 3:-1]
        - padded[..., 2:-2, 4:]
    ) / 12.0
    pushing = jnp.maximum(wind_u * slope_x + wind_v * slope_y, 0.0)
    return level - spread * (upwind + gain * pushing)


def atmos_step(padded, heat_atm):
    width_x = padded.shape[2] - 6
    width_y = padded.shape[3] - 6

    def shifted(along_x, along_y):
        return padded[
            :, :, 3 + along_x : 3 + along_x + width_x, 3 + along_y : 3 + along_y + width_y
        ]

    centre = shifted(0, 0)
    deriv_x = (
        shifted(3, 0)
        - 9.0 * shifted(2, 0)
        + 45.0 * shifted(1, 0)
        - 45.0 * shifted(-1, 0)
        + 9.0 * shifted(-2, 0)
        - shifted(-3, 0)
    ) / 60.0
    deriv_y = (
        shifted(0, 3)
        - 9.0 * shifted(0, 2)
        + 45.0 * shifted(0, 1)
        - 45.0 * shifted(0, -1)
        + 9.0 * shifted(0, -2)
        - shifted(0, -3)
    ) / 60.0
    laplace = shifted(1, 0) + shifted(-1, 0) + shifted(0, 1) + shifted(0, -1) - 4.0 * centre
    updated = centre - COURANT * (centre[0:1] * deriv_x + centre[1:2] * deriv_y) + DIFFUSE * laplace
    depth = padded.shape[1]
    profile = jnp.exp(-4.0 * jnp.arange(depth).astype(jnp.float32) / depth)
    return updated.at[3].add(heat_atm[None, :, :] * profile[:, None, None])


def interp_table(count, ratio, extra):
    indices = jnp.arange(count + 2 * extra) - extra
    coarse = indices // ratio
    within = indices % ratio
    lower = jnp.where(within < ratio // 2, coarse, coarse + 1) + 2
    weight = (within.astype(jnp.float32) + 0.5) / ratio + jnp.where(within < ratio // 2, 0.5, -0.5)
    columns = jnp.arange(count // ratio + 6)
    return (1.0 - weight)[:, None] * (columns[None, :] == lower[:, None]) + weight[:, None] * (
        columns[None, :] == lower[:, None] + 1
    )


def surface_winds(surface, fire_rows, fire_cols, extra_x, extra_y):
    table_x = interp_table(fire_rows, RF, extra_x)
    table_y = interp_table(fire_cols, RF, extra_y)
    along = jnp.einsum("ia,kab->kib", table_x, surface, precision=lax.Precision.HIGHEST)
    return jnp.einsum("kib,jb->kij", along, table_y, precision=lax.Precision.HIGHEST)


HALO_Y = 128


def shift(a, d, axis):
    return pltpu.roll(a, (-d) % a.shape[axis], axis)


def lookup(tab_ref, cat, row, default):
    ncat = tab_ref.shape[0] // 4
    out = jnp.full(cat.shape, default, jnp.float32)
    for category in range(ncat):
        out = jnp.where(cat == float(category), tab_ref[row * ncat + category], out)
    return out


def fire_kernel(tab_ref, ext_ref, wind_ref, fuel_ref, level_out, fuel_out, heat_out):
    rows, cols = fuel_ref.shape
    hx = (ext_ref.shape[1] - rows) // 2
    hy = (ext_ref.shape[2] - cols) // 2
    inner = (slice(hx, hx + rows), slice(hy, hy + cols))
    level = ext_ref[0]
    cat = ext_ref[1]
    nsteps = ext_ref[2]
    spread = lookup(tab_ref, cat, 0, 0.0)
    gain = lookup(tab_ref, cat, 1, 0.0)
    cat_in = cat[inner]
    burnout = lookup(tab_ref, cat_in, 2, 1.0)
    yields = lookup(tab_ref, cat_in, 3, 0.0)
    nsteps_in = nsteps[inner]
    wind_u = wind_ref[0]
    wind_v = wind_ref[1]
    remaining = fuel_ref[...]
    heating = jnp.zeros_like(remaining)
    for substep in range(SUBSTEPS):
        xm1 = shift(level, -1, 0)
        xp1 = shift(level, 1, 0)
        ym1 = shift(level, -1, 1)
        yp1 = shift(level, 1, 1)
        back_x = level - xm1
        ahead_x = xp1 - level
        back_y = level - ym1
        ahead_y = yp1 - level
        upwind = jnp.sqrt(
            jnp.maximum(back_x, 0.0) ** 2
            + jnp.minimum(ahead_x, 0.0) ** 2
            + jnp.maximum(back_y, 0.0) ** 2
            + jnp.minimum(ahead_y, 0.0) ** 2
        )
        slope_x = (shift(level, -2, 0) - 8.0 * xm1 + 8.0 * xp1 - shift(level, 2, 0)) / 12.0
        slope_y = (shift(level, -2, 1) - 8.0 * ym1 + 8.0 * yp1 - shift(level, 2, 1)) / 12.0
        pushing = jnp.maximum(wind_u * slope_x + wind_v * slope_y, 0.0)
        moved = level - spread * (upwind + gain * pushing)
        burned = remaining / (1.0 + jnp.exp(moved[inner])) / burnout
        active = float(substep) < nsteps_in
        remaining = jnp.where(active, remaining - burned, remaining)
        heating = heating + jnp.where(active, yields * burned, 0.0)
        level = jnp.where(float(substep) < nsteps, moved, level)
    level_out[...] = level[inner]
    fuel_out[...] = remaining
    heat_out[...] = heating.reshape(rows // RF, RF, cols).sum(axis=1)


def fire_step(tables, ext, winds, fuel_left):
    rows, cols = fuel_left.shape
    vmem = pl.BlockSpec(memory_space=pltpu.VMEM)
    return pl.pallas_call(
        fire_kernel,
        out_shape=(
            jax.ShapeDtypeStruct((rows, cols), jnp.float32),
            jax.ShapeDtypeStruct((rows, cols), jnp.float32),
            jax.ShapeDtypeStruct((rows // RF, cols), jnp.float32),
        ),
        in_specs=[pl.BlockSpec(memory_space=pltpu.SMEM), vmem, vmem, vmem],
        out_specs=(vmem, vmem, vmem),
    )(tables, ext, winds, fuel_left)


def fire_halo(level):
    return extended(level, (("gx", 0), ("gy", 1)), 2)


def shards(
    atmos,
    level_set,
    fuel_left,
    fuel_map,
    spread_rate,
    wind_factor,
    burn_time,
    heat_yield,
    burn_tiles,
    burn_count,
    substep_count,
):
    fire_rows, fire_cols = level_set.shape
    atmos_rows, atmos_cols = (atmos.shape[2], atmos.shape[3])
    slots = burn_tiles.reshape(-1)
    listed = burn_count.reshape(())
    tiles_dev = substep_count.size
    slot_valid = jnp.arange(slots.shape[0]) < listed
    tile_on = jnp.any(
        (slots[:, None] == jnp.arange(tiles_dev)[None, :]) & slot_valid[:, None], axis=0
    )
    tile_on = tile_on.reshape(substep_count.shape)
    tiles_x, tiles_y = substep_count.shape
    halo = 2 * SUBSTEPS
    nsteps = jnp.where(tile_on, substep_count, 0).astype(jnp.float32)
    nsteps = jnp.broadcast_to(nsteps[:, None, :, None], (tiles_x, TILE, tiles_y, TILE)).reshape(
        fire_rows, fire_cols
    )
    stacked = jnp.stack([level_set, fuel_map.astype(jnp.float32), nsteps])
    stacked, padded_atm = swap_ends(((stacked, 1, halo), (atmos, 2, 3)), "gx")
    stacked, padded_atm = swap_ends(((stacked, 2, halo), (padded_atm, 3, 3)), "gy")
    surface = padded_atm[0:2, 0]
    room = jnp.zeros(stacked.shape[:2] + (HALO_Y - halo,), jnp.float32)
    stacked = jnp.concatenate([room, stacked, room], axis=2)
    winds = surface_winds(surface, fire_rows, fire_cols, halo, HALO_Y)
    tables = jnp.concatenate([spread_rate, wind_factor, burn_time, heat_yield]).astype(jnp.float32)
    level, remaining, heat_rows = fire_step(tables, stacked, winds, fuel_left)
    heat_atm = heat_rows.reshape(atmos_rows, atmos_cols, RF).sum(axis=2) / (RF * RF)
    return (atmos_step(padded_atm, heat_atm), level, remaining)


def solution(mesh):
    return jax.shard_map(
        shards,
        mesh=mesh,
        in_specs=(
            P(None, None, "gx", "gy"),
            P("gx", "gy"),
            P("gx", "gy"),
            P("gx", "gy"),
            P(),
            P(),
            P(),
            P(),
            P("gx", "gy", None),
            P("gx", "gy"),
            P("gx", "gy"),
        ),
        out_specs=(P(None, None, "gx", "gy"), P("gx", "gy"), P("gx", "gy")),
        check_vma=False,
    )
```

```python
import jax
import jax.numpy as jnp
from jax import lax
from jax.sharding import PartitionSpec as P
from jax.experimental import pallas as pl
from jax.experimental.pallas import tpu as pltpu

RF = 8
TILE = 64
SUBSTEPS = 8


COURANT = 0.2
DIFFUSE = 0.05


def extended(cells, sides, width):
    for axis, dim in sides:
        count = lax.axis_size(axis)
        ends = count - 1
        head = lax.slice_in_dim(cells, 0, width, axis=dim)
        tail = lax.slice_in_dim(cells, cells.shape[dim] - width, cells.shape[dim], axis=dim)
        cells = jnp.concatenate(
            [
                lax.ppermute(tail, axis, [(i, (i + 1) % count) for i in range(ends)]),
                cells,
                lax.ppermute(head, axis, [((i + 1) % count, i) for i in range(ends)]),
            ],
            axis=dim,
        )
    return cells


def advance(
    padded, level, remaining, heating, spread, gain, burnout, yields, wind_u, wind_v, active
):
    back_x = level - padded[..., 1:-3, 2:-2]
    ahead_x = padded[..., 3:-1, 2:-2] - level
    back_y = level - padded[..., 2:-2, 1:-3]
    ahead_y = padded[..., 2:-2, 3:-1] - level
    upwind = jnp.sqrt(
        jnp.maximum(back_x, 0.0) ** 2
        + jnp.minimum(ahead_x, 0.0) ** 2
        + jnp.maximum(back_y, 0.0) ** 2
        + jnp.minimum(ahead_y, 0.0) ** 2
    )
    slope_x = (
        padded[..., :-4, 2:-2]
        - 8.0 * padded[..., 1:-3, 2:-2]
        + 8.0 * padded[..., 3:-1, 2:-2]
        - padded[..., 4:, 2:-2]
    ) / 12.0
    slope_y = (
        padded[..., 2:-2, :-4]
        - 8.0 * padded[..., 2:-2, 1:-3]
        + 8.0 * padded[..., 2:-2, 3:-1]
        - padded[..., 2:-2, 4:]
    ) / 12.0
    pushing = jnp.maximum(wind_u * slope_x + wind_v * slope_y, 0.0)
    advanced = level - spread * (upwind + gain * pushing)
    burned = remaining / (1.0 + jnp.exp(advanced)) / burnout
    return (
        jnp.where(active, advanced, level),
        jnp.where(active, remaining - burned, remaining),
        heating + jnp.where(active, yields * burned, 0.0),
    )


def spread_level(padded, level, spread, gain, wind_u, wind_v):
    back_x = level - padded[..., 1:-3, 2:-2]
    ahead_x = padded[..., 3:-1, 2:-2] - level
    back_y = level - padded[..., 2:-2, 1:-3]
    ahead_y = padded[..., 2:-2, 3:-1] - level
    upwind = jnp.sqrt(
        jnp.maximum(back_x, 0.0) ** 2
        + jnp.minimum(ahead_x, 0.0) ** 2
        + jnp.maximum(back_y, 0.0) ** 2
        + jnp.minimum(ahead_y, 0.0) ** 2
    )
    slope_x = (
        padded[..., :-4, 2:-2]
        - 8.0 * padded[..., 1:-3, 2:-2]
        + 8.0 * padded[..., 3:-1, 2:-2]
        - padded[..., 4:, 2:-2]
    ) / 12.0
    slope_y = (
        padded[..., 2:-2, :-4]
        - 8.0 * padded[..., 2:-2, 1:-3]
        + 8.0 * padded[..., 2:-2, 3:-1]
        - padded[..., 2:-2, 4:]
    ) / 12.0
    pushing = jnp.maximum(wind_u * slope_x + wind_v * slope_y, 0.0)
    return level - spread * (upwind + gain * pushing)


def atmos_step(padded, heat_atm):
    width_x = padded.shape[2] - 6
    width_y = padded.shape[3] - 6

    def shifted(along_x, along_y):
        return padded[
            :, :, 3 + along_x : 3 + along_x + width_x, 3 + along_y : 3 + along_y + width_y
        ]

    centre = shifted(0, 0)
    deriv_x = (
        shifted(3, 0)
        - 9.0 * shifted(2, 0)
        + 45.0 * shifted(1, 0)
        - 45.0 * shifted(-1, 0)
        + 9.0 * shifted(-2, 0)
        - shifted(-3, 0)
    ) / 60.0
    deriv_y = (
        shifted(0, 3)
        - 9.0 * shifted(0, 2)
        + 45.0 * shifted(0, 1)
        - 45.0 * shifted(0, -1)
        + 9.0 * shifted(0, -2)
        - shifted(0, -3)
    ) / 60.0
    laplace = shifted(1, 0) + shifted(-1, 0) + shifted(0, 1) + shifted(0, -1) - 4.0 * centre
    updated = centre - COURANT * (centre[0:1] * deriv_x + centre[1:2] * deriv_y) + DIFFUSE * laplace
    depth = padded.shape[1]
    profile = jnp.exp(-4.0 * jnp.arange(depth).astype(jnp.float32) / depth)
    return updated.at[3].add(heat_atm[None, :, :] * profile[:, None, None])


def interp_table(count, ratio, extra):
    indices = jnp.arange(count + 2 * extra) - extra
    coarse = indices // ratio
    within = indices % ratio
    lower = jnp.where(within < ratio // 2, coarse, coarse + 1) + 2
    weight = (within.astype(jnp.float32) + 0.5) / ratio + jnp.where(within < ratio // 2, 0.5, -0.5)
    columns = jnp.arange(count // ratio + 6)
    return (1.0 - weight)[:, None] * (columns[None, :] == lower[:, None]) + weight[:, None] * (
        columns[None, :] == lower[:, None] + 1
    )


def surface_winds(surface, fire_rows, fire_cols, extra_x, extra_y):
    table_x = interp_table(fire_rows, RF, extra_x)
    table_y = interp_table(fire_cols, RF, extra_y)
    along = jnp.einsum("ia,kab->kib", table_x, surface, precision=lax.Precision.HIGHEST)
    return jnp.einsum("kib,jb->kij", along, table_y, precision=lax.Precision.HIGHEST)


HALO_Y = 128


def shift(a, d, axis):
    return pltpu.roll(a, (-d) % a.shape[axis], axis)


def lookup(tab_ref, cat, row, default):
    ncat = tab_ref.shape[0] // 4
    out = jnp.full(cat.shape, default, jnp.float32)
    for category in range(ncat):
        out = jnp.where(cat == float(category), tab_ref[row * ncat + category], out)
    return out


def fire_kernel(tab_ref, ext_ref, wind_ref, fuel_ref, level_out, fuel_out, heat_out):
    rows, cols = fuel_ref.shape
    hx = (ext_ref.shape[1] - rows) // 2
    hy = (ext_ref.shape[2] - cols) // 2
    inner = (slice(hx, hx + rows), slice(hy, hy + cols))
    level = ext_ref[0]
    cat = ext_ref[1]
    nsteps = ext_ref[2]
    spread = lookup(tab_ref, cat, 0, 0.0)
    gain = lookup(tab_ref, cat, 1, 0.0)
    cat_in = cat[inner]
    burnout = lookup(tab_ref, cat_in, 2, 1.0)
    yields = lookup(tab_ref, cat_in, 3, 0.0)
    nsteps_in = nsteps[inner]
    wind_u = wind_ref[0]
    wind_v = wind_ref[1]
    remaining = fuel_ref[...]
    heating = jnp.zeros_like(remaining)
    for substep in range(SUBSTEPS):
        xm1 = shift(level, -1, 0)
        xp1 = shift(level, 1, 0)
        ym1 = shift(level, -1, 1)
        yp1 = shift(level, 1, 1)
        back_x = level - xm1
        ahead_x = xp1 - level
        back_y = level - ym1
        ahead_y = yp1 - level
        upwind = jnp.sqrt(
            jnp.maximum(back_x, 0.0) ** 2
            + jnp.minimum(ahead_x, 0.0) ** 2
            + jnp.maximum(back_y, 0.0) ** 2
            + jnp.minimum(ahead_y, 0.0) ** 2
        )
        slope_x = (shift(level, -2, 0) - 8.0 * xm1 + 8.0 * xp1 - shift(level, 2, 0)) / 12.0
        slope_y = (shift(level, -2, 1) - 8.0 * ym1 + 8.0 * yp1 - shift(level, 2, 1)) / 12.0
        pushing = jnp.maximum(wind_u * slope_x + wind_v * slope_y, 0.0)
        moved = level - spread * (upwind + gain * pushing)
        burned = remaining / (1.0 + jnp.exp(moved[inner])) / burnout
        active = float(substep) < nsteps_in
        remaining = jnp.where(active, remaining - burned, remaining)
        heating = heating + jnp.where(active, yields * burned, 0.0)
        level = jnp.where(float(substep) < nsteps, moved, level)
    level_out[...] = level[inner]
    fuel_out[...] = remaining
    heat_rows = heating.reshape(rows // RF, RF, cols).sum(axis=1)
    lane_in = lax.broadcasted_iota(jnp.int32, (cols, cols // RF), 0) // RF
    lane_out = lax.broadcasted_iota(jnp.int32, (cols, cols // RF), 1)
    blocks = (lane_in == lane_out).astype(jnp.float32)
    heat_out[...] = jnp.dot(
        heat_rows, blocks, precision=lax.Precision.HIGHEST, preferred_element_type=jnp.float32
    ) / (RF * RF)


def fire_step(tables, ext, winds, fuel_left):
    rows, cols = fuel_left.shape
    vmem = pl.BlockSpec(memory_space=pltpu.VMEM)
    return pl.pallas_call(
        fire_kernel,
        out_shape=(
            jax.ShapeDtypeStruct((rows, cols), jnp.float32),
            jax.ShapeDtypeStruct((rows, cols), jnp.float32),
            jax.ShapeDtypeStruct((rows // RF, cols // RF), jnp.float32),
        ),
        in_specs=[pl.BlockSpec(memory_space=pltpu.SMEM), vmem, vmem, vmem],
        out_specs=(vmem, vmem, vmem),
    )(tables, ext, winds, fuel_left)


def atmos_kernel(q_ref, u_ref, v_ref, h_ref, o_ref):
    rows, cols = o_ref.shape[2], o_ref.shape[3]
    width = q_ref.shape[3]

    def at(ref, dx, dy):
        band = ref[0, :, 3 + dx : 3 + dx + rows, :]
        return pltpu.roll(band, (width - 3 - dy) % width, 2)[:, :, :cols]

    centre = at(q_ref, 0, 0)
    deriv_x = (
        at(q_ref, 3, 0)
        - 9.0 * at(q_ref, 2, 0)
        + 45.0 * at(q_ref, 1, 0)
        - 45.0 * at(q_ref, -1, 0)
        + 9.0 * at(q_ref, -2, 0)
        - at(q_ref, -3, 0)
    ) / 60.0
    deriv_y = (
        at(q_ref, 0, 3)
        - 9.0 * at(q_ref, 0, 2)
        + 45.0 * at(q_ref, 0, 1)
        - 45.0 * at(q_ref, 0, -1)
        + 9.0 * at(q_ref, 0, -2)
        - at(q_ref, 0, -3)
    ) / 60.0
    laplace = at(q_ref, 1, 0) + at(q_ref, -1, 0) + at(q_ref, 0, 1) + at(q_ref, 0, -1) - 4.0 * centre
    updated = (
        centre
        - COURANT * (at(u_ref, 0, 0) * deriv_x + at(v_ref, 0, 0) * deriv_y)
        + DIFFUSE * laplace
    )
    o_ref[0] = jnp.where(pl.program_id(0) == 3, updated + h_ref[...], updated)


def atmos_call(padded, heat_atm):
    fields, depth, ext_rows, width = padded.shape
    rows, cols = heat_atm.shape
    profile = jnp.exp(-4.0 * jnp.arange(depth).astype(jnp.float32) / depth)
    heat = heat_atm[None, :, :] * profile[:, None, None]
    block = (1, depth, ext_rows, width)
    return pl.pallas_call(
        atmos_kernel,
        grid=(fields,),
        out_shape=jax.ShapeDtypeStruct((fields, depth, rows, cols), jnp.float32),
        in_specs=[
            pl.BlockSpec(block, lambda f: (f, 0, 0, 0)),
            pl.BlockSpec(block, lambda f: (0, 0, 0, 0)),
            pl.BlockSpec(block, lambda f: (1, 0, 0, 0)),
            pl.BlockSpec((depth, rows, cols), lambda f: (0, 0, 0)),
        ],
        out_specs=pl.BlockSpec((1, depth, rows, cols), lambda f: (f, 0, 0, 0)),
    )(padded, padded, padded, heat)


def fire_halo(level):
    return extended(level, (("gx", 0), ("gy", 1)), 2)


def shards(
    atmos,
    level_set,
    fuel_left,
    fuel_map,
    spread_rate,
    wind_factor,
    burn_time,
    heat_yield,
    burn_tiles,
    burn_count,
    substep_count,
):
    fire_rows, fire_cols = level_set.shape
    atmos_rows, atmos_cols = (atmos.shape[2], atmos.shape[3])
    padded_atm = extended(atmos, (("gx", 2), ("gy", 3)), 3)
    surface = padded_atm[0:2, 0]
    lanes = -(-padded_atm.shape[3] // 128) * 128
    padded_atm = jnp.pad(padded_atm, ((0, 0), (0, 0), (0, 0), (0, lanes - padded_atm.shape[3])))
    slots = burn_tiles.reshape(-1)
    listed = burn_count.reshape(())
    tiles_dev = substep_count.size
    slot_valid = jnp.arange(slots.shape[0]) < listed
    tile_on = jnp.any(
        (slots[:, None] == jnp.arange(tiles_dev)[None, :]) & slot_valid[:, None], axis=0
    )
    tile_on = tile_on.reshape(substep_count.shape)
    tiles_x, tiles_y = substep_count.shape
    halo = 2 * SUBSTEPS
    nsteps = jnp.where(tile_on, substep_count, 0).astype(jnp.float32)
    nsteps = jnp.broadcast_to(nsteps[:, None, :, None], (tiles_x, TILE, tiles_y, TILE)).reshape(
        fire_rows, fire_cols
    )
    stacked = jnp.stack([level_set, fuel_map.astype(jnp.float32), nsteps])
    stacked = extended(stacked, (("gx", 1), ("gy", 2)), halo)
    room = jnp.zeros(stacked.shape[:2] + (HALO_Y - halo,), jnp.float32)
    stacked = jnp.concatenate([room, stacked, room], axis=2)
    winds = surface_winds(surface, fire_rows, fire_cols, halo, HALO_Y)
    tables = jnp.concatenate([spread_rate, wind_factor, burn_time, heat_yield]).astype(jnp.float32)
    level, remaining, heat_atm = fire_step(tables, stacked, winds, fuel_left)
    return (atmos_call(padded_atm, heat_atm), level, remaining)


def solution(mesh):
    return jax.shard_map(
        shards,
        mesh=mesh,
        in_specs=(
            P(None, None, "gx", "gy"),
            P("gx", "gy"),
            P("gx", "gy"),
            P("gx", "gy"),
            P(),
            P(),
            P(),
            P(),
            P("gx", "gy", None),
            P("gx", "gy"),
            P("gx", "gy"),
        ),
        out_specs=(P(None, None, "gx", "gy"), P("gx", "gy"), P("gx", "gy")),
        check_vma=False,
    )
```

```python
import jax
import jax.numpy as jnp
from jax import lax
from jax.sharding import PartitionSpec as P
from jax.experimental import pallas as pl
from jax.experimental.pallas import tpu as pltpu

RF = 8
TILE = 64
SUBSTEPS = 8


COURANT = 0.2
DIFFUSE = 0.05


def extended(cells, sides, width):
    for axis, dim in sides:
        count = lax.axis_size(axis)
        ends = count - 1
        head = lax.slice_in_dim(cells, 0, width, axis=dim)
        tail = lax.slice_in_dim(cells, cells.shape[dim] - width, cells.shape[dim], axis=dim)
        cells = jnp.concatenate(
            [
                lax.ppermute(tail, axis, [(i, (i + 1) % count) for i in range(ends)]),
                cells,
                lax.ppermute(head, axis, [((i + 1) % count, i) for i in range(ends)]),
            ],
            axis=dim,
        )
    return cells


def advance(
    padded, level, remaining, heating, spread, gain, burnout, yields, wind_u, wind_v, active
):
    back_x = level - padded[..., 1:-3, 2:-2]
    ahead_x = padded[..., 3:-1, 2:-2] - level
    back_y = level - padded[..., 2:-2, 1:-3]
    ahead_y = padded[..., 2:-2, 3:-1] - level
    upwind = jnp.sqrt(
        jnp.maximum(back_x, 0.0) ** 2
        + jnp.minimum(ahead_x, 0.0) ** 2
        + jnp.maximum(back_y, 0.0) ** 2
        + jnp.minimum(ahead_y, 0.0) ** 2
    )
    slope_x = (
        padded[..., :-4, 2:-2]
        - 8.0 * padded[..., 1:-3, 2:-2]
        + 8.0 * padded[..., 3:-1, 2:-2]
        - padded[..., 4:, 2:-2]
    ) / 12.0
    slope_y = (
        padded[..., 2:-2, :-4]
        - 8.0 * padded[..., 2:-2, 1:-3]
        + 8.0 * padded[..., 2:-2, 3:-1]
        - padded[..., 2:-2, 4:]
    ) / 12.0
    pushing = jnp.maximum(wind_u * slope_x + wind_v * slope_y, 0.0)
    advanced = level - spread * (upwind + gain * pushing)
    burned = remaining / (1.0 + jnp.exp(advanced)) / burnout
    return (
        jnp.where(active, advanced, level),
        jnp.where(active, remaining - burned, remaining),
        heating + jnp.where(active, yields * burned, 0.0),
    )


def spread_level(padded, level, spread, gain, wind_u, wind_v):
    back_x = level - padded[..., 1:-3, 2:-2]
    ahead_x = padded[..., 3:-1, 2:-2] - level
    back_y = level - padded[..., 2:-2, 1:-3]
    ahead_y = padded[..., 2:-2, 3:-1] - level
    upwind = jnp.sqrt(
        jnp.maximum(back_x, 0.0) ** 2
        + jnp.minimum(ahead_x, 0.0) ** 2
        + jnp.maximum(back_y, 0.0) ** 2
        + jnp.minimum(ahead_y, 0.0) ** 2
    )
    slope_x = (
        padded[..., :-4, 2:-2]
        - 8.0 * padded[..., 1:-3, 2:-2]
        + 8.0 * padded[..., 3:-1, 2:-2]
        - padded[..., 4:, 2:-2]
    ) / 12.0
    slope_y = (
        padded[..., 2:-2, :-4]
        - 8.0 * padded[..., 2:-2, 1:-3]
        + 8.0 * padded[..., 2:-2, 3:-1]
        - padded[..., 2:-2, 4:]
    ) / 12.0
    pushing = jnp.maximum(wind_u * slope_x + wind_v * slope_y, 0.0)
    return level - spread * (upwind + gain * pushing)


def atmos_step(padded, heat_atm):
    width_x = padded.shape[2] - 6
    width_y = padded.shape[3] - 6

    def shifted(along_x, along_y):
        return padded[
            :, :, 3 + along_x : 3 + along_x + width_x, 3 + along_y : 3 + along_y + width_y
        ]

    centre = shifted(0, 0)
    deriv_x = (
        shifted(3, 0)
        - 9.0 * shifted(2, 0)
        + 45.0 * shifted(1, 0)
        - 45.0 * shifted(-1, 0)
        + 9.0 * shifted(-2, 0)
        - shifted(-3, 0)
    ) / 60.0
    deriv_y = (
        shifted(0, 3)
        - 9.0 * shifted(0, 2)
        + 45.0 * shifted(0, 1)
        - 45.0 * shifted(0, -1)
        + 9.0 * shifted(0, -2)
        - shifted(0, -3)
    ) / 60.0
    laplace = shifted(1, 0) + shifted(-1, 0) + shifted(0, 1) + shifted(0, -1) - 4.0 * centre
    updated = centre - COURANT * (centre[0:1] * deriv_x + centre[1:2] * deriv_y) + DIFFUSE * laplace
    depth = padded.shape[1]
    profile = jnp.exp(-4.0 * jnp.arange(depth).astype(jnp.float32) / depth)
    return updated.at[3].add(heat_atm[None, :, :] * profile[:, None, None])


def interp_table(count, ratio, extra):
    indices = jnp.arange(count + 2 * extra) - extra
    coarse = indices // ratio
    within = indices % ratio
    lower = jnp.where(within < ratio // 2, coarse, coarse + 1) + 2
    weight = (within.astype(jnp.float32) + 0.5) / ratio + jnp.where(within < ratio // 2, 0.5, -0.5)
    columns = jnp.arange(count // ratio + 6)
    return (1.0 - weight)[:, None] * (columns[None, :] == lower[:, None]) + weight[:, None] * (
        columns[None, :] == lower[:, None] + 1
    )


def surface_winds(surface, fire_rows, fire_cols, extra_x, extra_y):
    table_x = interp_table(fire_rows, RF, extra_x)
    table_y = interp_table(fire_cols, RF, extra_y)
    along = jnp.einsum("ia,kab->kib", table_x, surface, precision=lax.Precision.HIGHEST)
    return jnp.einsum("kib,jb->kij", along, table_y, precision=lax.Precision.HIGHEST)


HALO_Y = 128


def shift(a, d, axis):
    return pltpu.roll(a, (-d) % a.shape[axis], axis)


def lookup(tab_ref, cat, row, default):
    ncat = tab_ref.shape[0] // 4
    out = jnp.full(cat.shape, default, jnp.float32)
    for category in range(ncat):
        out = jnp.where(cat == float(category), tab_ref[row * ncat + category], out)
    return out


def fire_kernel(tab_ref, ext_ref, wind_ref, fuel_ref, level_out, fuel_out, heat_out):
    rows, cols = fuel_ref.shape
    hx = (ext_ref.shape[1] - rows) // 2
    hy = (ext_ref.shape[2] - cols) // 2
    inner = (slice(hx, hx + rows), slice(hy, hy + cols))
    level = ext_ref[0]
    cat = ext_ref[1]
    nsteps = ext_ref[2]
    spread = lookup(tab_ref, cat, 0, 0.0)
    gain = lookup(tab_ref, cat, 1, 0.0)
    cat_in = cat[inner]
    burnout = lookup(tab_ref, cat_in, 2, 1.0)
    yields = lookup(tab_ref, cat_in, 3, 0.0)
    nsteps_in = nsteps[inner]
    wind_u = wind_ref[0]
    wind_v = wind_ref[1]
    remaining = fuel_ref[...]
    heating = jnp.zeros_like(remaining)
    for substep in range(SUBSTEPS):
        xm1 = shift(level, -1, 0)
        xp1 = shift(level, 1, 0)
        ym1 = shift(level, -1, 1)
        yp1 = shift(level, 1, 1)
        back_x = level - xm1
        ahead_x = xp1 - level
        back_y = level - ym1
        ahead_y = yp1 - level
        upwind = jnp.sqrt(
            jnp.maximum(back_x, 0.0) ** 2
            + jnp.minimum(ahead_x, 0.0) ** 2
            + jnp.maximum(back_y, 0.0) ** 2
            + jnp.minimum(ahead_y, 0.0) ** 2
        )
        slope_x = (shift(level, -2, 0) - 8.0 * xm1 + 8.0 * xp1 - shift(level, 2, 0)) / 12.0
        slope_y = (shift(level, -2, 1) - 8.0 * ym1 + 8.0 * yp1 - shift(level, 2, 1)) / 12.0
        pushing = jnp.maximum(wind_u * slope_x + wind_v * slope_y, 0.0)
        moved = level - spread * (upwind + gain * pushing)
        burned = remaining / (1.0 + jnp.exp(moved[inner])) / burnout
        active = float(substep) < nsteps_in
        remaining = jnp.where(active, remaining - burned, remaining)
        heating = heating + jnp.where(active, yields * burned, 0.0)
        level = jnp.where(float(substep) < nsteps, moved, level)
    level_out[...] = level[inner]
    fuel_out[...] = remaining
    heat_rows = heating.reshape(rows // RF, RF, cols).sum(axis=1)
    lane_in = lax.broadcasted_iota(jnp.int32, (cols, cols // RF), 0) // RF
    lane_out = lax.broadcasted_iota(jnp.int32, (cols, cols // RF), 1)
    blocks = (lane_in == lane_out).astype(jnp.float32)
    heat_out[...] = jnp.dot(
        heat_rows, blocks, precision=lax.Precision.HIGHEST, preferred_element_type=jnp.float32
    ) / (RF * RF)


def fire_step(tables, ext, winds, fuel_left):
    rows, cols = fuel_left.shape
    vmem = pl.BlockSpec(memory_space=pltpu.VMEM)
    return pl.pallas_call(
        fire_kernel,
        out_shape=(
            jax.ShapeDtypeStruct((rows, cols), jnp.float32),
            jax.ShapeDtypeStruct((rows, cols), jnp.float32),
            jax.ShapeDtypeStruct((rows // RF, cols // RF), jnp.float32),
        ),
        in_specs=[pl.BlockSpec(memory_space=pltpu.SMEM), vmem, vmem, vmem],
        out_specs=(vmem, vmem, vmem),
    )(tables, ext, winds, fuel_left)


def fire_halo(level):
    return extended(level, (("gx", 0), ("gy", 1)), 2)


def shards(
    atmos,
    level_set,
    fuel_left,
    fuel_map,
    spread_rate,
    wind_factor,
    burn_time,
    heat_yield,
    burn_tiles,
    burn_count,
    substep_count,
):
    fire_rows, fire_cols = level_set.shape
    atmos_rows, atmos_cols = (atmos.shape[2], atmos.shape[3])
    padded_atm = extended(atmos, (("gx", 2), ("gy", 3)), 3)
    surface = padded_atm[0:2, 0]
    slots = burn_tiles.reshape(-1)
    listed = burn_count.reshape(())
    tiles_dev = substep_count.size
    slot_valid = jnp.arange(slots.shape[0]) < listed
    tile_on = jnp.any(
        (slots[:, None] == jnp.arange(tiles_dev)[None, :]) & slot_valid[:, None], axis=0
    )
    tile_on = tile_on.reshape(substep_count.shape)
    tiles_x, tiles_y = substep_count.shape
    halo = 2 * SUBSTEPS
    nsteps = jnp.where(tile_on, substep_count, 0).astype(jnp.float32)
    nsteps = jnp.broadcast_to(nsteps[:, None, :, None], (tiles_x, TILE, tiles_y, TILE)).reshape(
        fire_rows, fire_cols
    )
    stacked = jnp.stack([level_set, fuel_map.astype(jnp.float32), nsteps])
    stacked = extended(stacked, (("gx", 1), ("gy", 2)), halo)
    room = jnp.zeros(stacked.shape[:2] + (HALO_Y - halo,), jnp.float32)
    stacked = jnp.concatenate([room, stacked, room], axis=2)
    winds = surface_winds(surface, fire_rows, fire_cols, halo, HALO_Y)
    tables = jnp.concatenate([spread_rate, wind_factor, burn_time, heat_yield]).astype(jnp.float32)
    level, remaining, heat_atm = fire_step(tables, stacked, winds, fuel_left)
    return (atmos_step(padded_atm, heat_atm), level, remaining)


def solution(mesh):
    return jax.shard_map(
        shards,
        mesh=mesh,
        in_specs=(
            P(None, None, "gx", "gy"),
            P("gx", "gy"),
            P("gx", "gy"),
            P("gx", "gy"),
            P(),
            P(),
            P(),
            P(),
            P("gx", "gy", None),
            P("gx", "gy"),
            P("gx", "gy"),
        ),
        out_specs=(P(None, None, "gx", "gy"), P("gx", "gy"), P("gx", "gy")),
        check_vma=False,
    )
```

```python
import jax
import jax.numpy as jnp
from jax import lax
from jax.sharding import PartitionSpec as P
from jax.experimental import pallas as pl
from jax.experimental.pallas import tpu as pltpu

RF = 8
TILE = 64
SUBSTEPS = 8


COURANT = 0.2
DIFFUSE = 0.05


def extended(cells, sides, width):
    for axis, dim in sides:
        count = lax.axis_size(axis)
        ends = count - 1
        head = lax.slice_in_dim(cells, 0, width, axis=dim)
        tail = lax.slice_in_dim(cells, cells.shape[dim] - width, cells.shape[dim], axis=dim)
        cells = jnp.concatenate(
            [
                lax.ppermute(tail, axis, [(i, (i + 1) % count) for i in range(ends)]),
                cells,
                lax.ppermute(head, axis, [((i + 1) % count, i) for i in range(ends)]),
            ],
            axis=dim,
        )
    return cells


def advance(
    padded, level, remaining, heating, spread, gain, burnout, yields, wind_u, wind_v, active
):
    back_x = level - padded[..., 1:-3, 2:-2]
    ahead_x = padded[..., 3:-1, 2:-2] - level
    back_y = level - padded[..., 2:-2, 1:-3]
    ahead_y = padded[..., 2:-2, 3:-1] - level
    upwind = jnp.sqrt(
        jnp.maximum(back_x, 0.0) ** 2
        + jnp.minimum(ahead_x, 0.0) ** 2
        + jnp.maximum(back_y, 0.0) ** 2
        + jnp.minimum(ahead_y, 0.0) ** 2
    )
    slope_x = (
        padded[..., :-4, 2:-2]
        - 8.0 * padded[..., 1:-3, 2:-2]
        + 8.0 * padded[..., 3:-1, 2:-2]
        - padded[..., 4:, 2:-2]
    ) / 12.0
    slope_y = (
        padded[..., 2:-2, :-4]
        - 8.0 * padded[..., 2:-2, 1:-3]
        + 8.0 * padded[..., 2:-2, 3:-1]
        - padded[..., 2:-2, 4:]
    ) / 12.0
    pushing = jnp.maximum(wind_u * slope_x + wind_v * slope_y, 0.0)
    advanced = level - spread * (upwind + gain * pushing)
    burned = remaining / (1.0 + jnp.exp(advanced)) / burnout
    return (
        jnp.where(active, advanced, level),
        jnp.where(active, remaining - burned, remaining),
        heating + jnp.where(active, yields * burned, 0.0),
    )


def spread_level(padded, level, spread, gain, wind_u, wind_v):
    back_x = level - padded[..., 1:-3, 2:-2]
    ahead_x = padded[..., 3:-1, 2:-2] - level
    back_y = level - padded[..., 2:-2, 1:-3]
    ahead_y = padded[..., 2:-2, 3:-1] - level
    upwind = jnp.sqrt(
        jnp.maximum(back_x, 0.0) ** 2
        + jnp.minimum(ahead_x, 0.0) ** 2
        + jnp.maximum(back_y, 0.0) ** 2
        + jnp.minimum(ahead_y, 0.0) ** 2
    )
    slope_x = (
        padded[..., :-4, 2:-2]
        - 8.0 * padded[..., 1:-3, 2:-2]
        + 8.0 * padded[..., 3:-1, 2:-2]
        - padded[..., 4:, 2:-2]
    ) / 12.0
    slope_y = (
        padded[..., 2:-2, :-4]
        - 8.0 * padded[..., 2:-2, 1:-3]
        + 8.0 * padded[..., 2:-2, 3:-1]
        - padded[..., 2:-2, 4:]
    ) / 12.0
    pushing = jnp.maximum(wind_u * slope_x + wind_v * slope_y, 0.0)
    return level - spread * (upwind + gain * pushing)


def atmos_step(padded, heat_atm):
    width_x = padded.shape[2] - 6
    width_y = padded.shape[3] - 6

    def shifted(along_x, along_y):
        return padded[
            :, :, 3 + along_x : 3 + along_x + width_x, 3 + along_y : 3 + along_y + width_y
        ]

    centre = shifted(0, 0)
    deriv_x = (
        shifted(3, 0)
        - 9.0 * shifted(2, 0)
        + 45.0 * shifted(1, 0)
        - 45.0 * shifted(-1, 0)
        + 9.0 * shifted(-2, 0)
        - shifted(-3, 0)
    ) / 60.0
    deriv_y = (
        shifted(0, 3)
        - 9.0 * shifted(0, 2)
        + 45.0 * shifted(0, 1)
        - 45.0 * shifted(0, -1)
        + 9.0 * shifted(0, -2)
        - shifted(0, -3)
    ) / 60.0
    laplace = shifted(1, 0) + shifted(-1, 0) + shifted(0, 1) + shifted(0, -1) - 4.0 * centre
    updated = centre - COURANT * (centre[0:1] * deriv_x + centre[1:2] * deriv_y) + DIFFUSE * laplace
    depth = padded.shape[1]
    profile = jnp.exp(-4.0 * jnp.arange(depth).astype(jnp.float32) / depth)
    return updated.at[3].add(heat_atm[None, :, :] * profile[:, None, None])


def interp_table(count, ratio, extra):
    indices = jnp.arange(count + 2 * extra) - extra
    coarse = indices // ratio
    within = indices % ratio
    lower = jnp.where(within < ratio // 2, coarse, coarse + 1) + 2
    weight = (within.astype(jnp.float32) + 0.5) / ratio + jnp.where(within < ratio // 2, 0.5, -0.5)
    columns = jnp.arange(count // ratio + 6)
    return (1.0 - weight)[:, None] * (columns[None, :] == lower[:, None]) + weight[:, None] * (
        columns[None, :] == lower[:, None] + 1
    )


def surface_winds(surface, fire_rows, fire_cols, extra_x, extra_y):
    table_x = interp_table(fire_rows, RF, extra_x)
    table_y = interp_table(fire_cols, RF, extra_y)
    along = jnp.einsum("ia,kab->kib", table_x, surface, precision=lax.Precision.HIGHEST)
    return jnp.einsum("kib,jb->kij", along, table_y, precision=lax.Precision.HIGHEST)


HALO_Y = 128


def shift(a, d, axis):
    return pltpu.roll(a, (-d) % a.shape[axis], axis)


def lookup(tab_ref, cat, row, default):
    ncat = tab_ref.shape[0] // 4
    out = jnp.full(cat.shape, default, jnp.float32)
    for category in range(ncat):
        out = jnp.where(cat == float(category), tab_ref[row * ncat + category], out)
    return out


def fire_kernel(tab_ref, ext_ref, wind_ref, fuel_ref, level_out, fuel_out, heat_out):
    rows, cols = fuel_ref.shape
    hx = (ext_ref.shape[1] - rows) // 2
    hy = (ext_ref.shape[2] - cols) // 2
    inner = (slice(hx, hx + rows), slice(hy, hy + cols))
    level = ext_ref[0]
    cat = ext_ref[1]
    nsteps = ext_ref[2]
    spread = lookup(tab_ref, cat, 0, 0.0)
    gain = lookup(tab_ref, cat, 1, 0.0)
    cat_in = cat[inner]
    burnout = lookup(tab_ref, cat_in, 2, 1.0)
    yields = lookup(tab_ref, cat_in, 3, 0.0)
    nsteps_in = nsteps[inner]
    wind_u = wind_ref[0]
    wind_v = wind_ref[1]
    remaining = fuel_ref[...]
    heating = jnp.zeros_like(remaining)
    for substep in range(SUBSTEPS):
        xm1 = shift(level, -1, 0)
        xp1 = shift(level, 1, 0)
        ym1 = shift(level, -1, 1)
        yp1 = shift(level, 1, 1)
        back_x = level - xm1
        ahead_x = xp1 - level
        back_y = level - ym1
        ahead_y = yp1 - level
        upwind = jnp.sqrt(
            jnp.maximum(back_x, 0.0) ** 2
            + jnp.minimum(ahead_x, 0.0) ** 2
            + jnp.maximum(back_y, 0.0) ** 2
            + jnp.minimum(ahead_y, 0.0) ** 2
        )
        slope_x = (shift(level, -2, 0) - 8.0 * xm1 + 8.0 * xp1 - shift(level, 2, 0)) / 12.0
        slope_y = (shift(level, -2, 1) - 8.0 * ym1 + 8.0 * yp1 - shift(level, 2, 1)) / 12.0
        pushing = jnp.maximum(wind_u * slope_x + wind_v * slope_y, 0.0)
        moved = level - spread * (upwind + gain * pushing)
        burned = remaining / (1.0 + jnp.exp(moved[inner])) / burnout
        active = float(substep) < nsteps_in
        remaining = jnp.where(active, remaining - burned, remaining)
        heating = heating + jnp.where(active, yields * burned, 0.0)
        level = jnp.where(float(substep) < nsteps, moved, level)
    level_out[...] = level[inner]
    fuel_out[...] = remaining
    heat_rows = heating.reshape(rows // RF, RF, cols).sum(axis=1)
    lane_in = lax.broadcasted_iota(jnp.int32, (cols, cols // RF), 0) // RF
    lane_out = lax.broadcasted_iota(jnp.int32, (cols, cols // RF), 1)
    blocks = (lane_in == lane_out).astype(jnp.float32)
    heat_out[...] = jnp.dot(
        heat_rows, blocks, precision=lax.Precision.HIGHEST, preferred_element_type=jnp.float32
    ) / (RF * RF)


def fire_step(tables, ext, winds, fuel_left):
    rows, cols = fuel_left.shape
    vmem = pl.BlockSpec(memory_space=pltpu.VMEM)
    return pl.pallas_call(
        fire_kernel,
        out_shape=(
            jax.ShapeDtypeStruct((rows, cols), jnp.float32),
            jax.ShapeDtypeStruct((rows, cols), jnp.float32),
            jax.ShapeDtypeStruct((rows // RF, cols // RF), jnp.float32),
        ),
        in_specs=[pl.BlockSpec(memory_space=pltpu.SMEM), vmem, vmem, vmem],
        out_specs=(vmem, vmem, vmem),
    )(tables, ext, winds, fuel_left)


def atmos_kernel(q_ref, u_ref, v_ref, h_ref, o_ref):
    rows, cols = o_ref.shape[2], o_ref.shape[3]
    width = q_ref.shape[3]

    def at(ref, dx, dy):
        band = ref[0, :, 3 + dx : 3 + dx + rows, :]
        if dy == 0:
            return band[:, :, :cols]
        return pltpu.roll(band, (width - dy) % width, 2)[:, :, :cols]

    centre = at(q_ref, 0, 0)
    deriv_x = (
        at(q_ref, 3, 0)
        - 9.0 * at(q_ref, 2, 0)
        + 45.0 * at(q_ref, 1, 0)
        - 45.0 * at(q_ref, -1, 0)
        + 9.0 * at(q_ref, -2, 0)
        - at(q_ref, -3, 0)
    ) / 60.0
    deriv_y = (
        at(q_ref, 0, 3)
        - 9.0 * at(q_ref, 0, 2)
        + 45.0 * at(q_ref, 0, 1)
        - 45.0 * at(q_ref, 0, -1)
        + 9.0 * at(q_ref, 0, -2)
        - at(q_ref, 0, -3)
    ) / 60.0
    laplace = at(q_ref, 1, 0) + at(q_ref, -1, 0) + at(q_ref, 0, 1) + at(q_ref, 0, -1) - 4.0 * centre
    updated = (
        centre
        - COURANT * (at(u_ref, 0, 0) * deriv_x + at(v_ref, 0, 0) * deriv_y)
        + DIFFUSE * laplace
    )
    o_ref[0] = jnp.where(pl.program_id(0) == 3, updated + h_ref[...], updated)


def atmos_call(padded, heat_atm):
    fields, depth, ext_rows, width = padded.shape
    rows, cols = heat_atm.shape
    profile = jnp.exp(-4.0 * jnp.arange(depth).astype(jnp.float32) / depth)
    heat = heat_atm[None, :, :] * profile[:, None, None]
    block = (1, depth, ext_rows, width)
    return pl.pallas_call(
        atmos_kernel,
        grid=(fields,),
        out_shape=jax.ShapeDtypeStruct((fields, depth, rows, cols), jnp.float32),
        in_specs=[
            pl.BlockSpec(block, lambda f: (f, 0, 0, 0)),
            pl.BlockSpec(block, lambda f: (0, 0, 0, 0)),
            pl.BlockSpec(block, lambda f: (1, 0, 0, 0)),
            pl.BlockSpec((depth, rows, cols), lambda f: (0, 0, 0)),
        ],
        out_specs=pl.BlockSpec((1, depth, rows, cols), lambda f: (f, 0, 0, 0)),
    )(padded, padded, padded, heat)


def fire_halo(level):
    return extended(level, (("gx", 0), ("gy", 1)), 2)


def shards(
    atmos,
    level_set,
    fuel_left,
    fuel_map,
    spread_rate,
    wind_factor,
    burn_time,
    heat_yield,
    burn_tiles,
    burn_count,
    substep_count,
):
    fire_rows, fire_cols = level_set.shape
    atmos_rows, atmos_cols = (atmos.shape[2], atmos.shape[3])
    along_x = extended(atmos, (("gx", 2),), 3)
    count = lax.axis_size("gy")
    from_lo = lax.ppermute(along_x[..., -3:], "gy", [(i, i + 1) for i in range(count - 1)])
    from_hi = lax.ppermute(along_x[..., :3], "gy", [(i + 1, i) for i in range(count - 1)])
    lanes = 2 * (-(-atmos_cols // 128) * 128)
    room = jnp.zeros(along_x.shape[:3] + (lanes - atmos_cols - 6,), jnp.float32)
    padded_atm = jnp.concatenate([along_x, from_hi, room, from_lo], axis=3)
    surface = jnp.concatenate([from_lo[0:2, 0], along_x[0:2, 0], from_hi[0:2, 0]], axis=2)
    slots = burn_tiles.reshape(-1)
    listed = burn_count.reshape(())
    tiles_dev = substep_count.size
    slot_valid = jnp.arange(slots.shape[0]) < listed
    tile_on = jnp.any(
        (slots[:, None] == jnp.arange(tiles_dev)[None, :]) & slot_valid[:, None], axis=0
    )
    tile_on = tile_on.reshape(substep_count.shape)
    tiles_x, tiles_y = substep_count.shape
    halo = 2 * SUBSTEPS
    nsteps = jnp.where(tile_on, substep_count, 0).astype(jnp.float32)
    nsteps = jnp.broadcast_to(nsteps[:, None, :, None], (tiles_x, TILE, tiles_y, TILE)).reshape(
        fire_rows, fire_cols
    )
    stacked = jnp.stack([level_set, fuel_map.astype(jnp.float32), nsteps])
    stacked = extended(stacked, (("gx", 1), ("gy", 2)), halo)
    room = jnp.zeros(stacked.shape[:2] + (HALO_Y - halo,), jnp.float32)
    stacked = jnp.concatenate([room, stacked, room], axis=2)
    winds = surface_winds(surface, fire_rows, fire_cols, halo, HALO_Y)
    tables = jnp.concatenate([spread_rate, wind_factor, burn_time, heat_yield]).astype(jnp.float32)
    level, remaining, heat_atm = fire_step(tables, stacked, winds, fuel_left)
    return (atmos_call(padded_atm, heat_atm), level, remaining)


def solution(mesh):
    return jax.shard_map(
        shards,
        mesh=mesh,
        in_specs=(
            P(None, None, "gx", "gy"),
            P("gx", "gy"),
            P("gx", "gy"),
            P("gx", "gy"),
            P(),
            P(),
            P(),
            P(),
            P("gx", "gy", None),
            P("gx", "gy"),
            P("gx", "gy"),
        ),
        out_specs=(P(None, None, "gx", "gy"), P("gx", "gy"), P("gx", "gy")),
        check_vma=False,
    )
```

```python
import jax
import jax.numpy as jnp
from jax import lax
from jax.sharding import PartitionSpec as P
from jax.experimental import pallas as pl
from jax.experimental.pallas import tpu as pltpu

RF = 8
TILE = 64
SUBSTEPS = 8


COURANT = 0.2
DIFFUSE = 0.05


def extended(cells, sides, width):
    for axis, dim in sides:
        count = lax.axis_size(axis)
        ends = count - 1
        head = lax.slice_in_dim(cells, 0, width, axis=dim)
        tail = lax.slice_in_dim(cells, cells.shape[dim] - width, cells.shape[dim], axis=dim)
        cells = jnp.concatenate(
            [
                lax.ppermute(tail, axis, [(i, (i + 1) % count) for i in range(ends)]),
                cells,
                lax.ppermute(head, axis, [((i + 1) % count, i) for i in range(ends)]),
            ],
            axis=dim,
        )
    return cells


def advance(
    padded, level, remaining, heating, spread, gain, burnout, yields, wind_u, wind_v, active
):
    back_x = level - padded[..., 1:-3, 2:-2]
    ahead_x = padded[..., 3:-1, 2:-2] - level
    back_y = level - padded[..., 2:-2, 1:-3]
    ahead_y = padded[..., 2:-2, 3:-1] - level
    upwind = jnp.sqrt(
        jnp.maximum(back_x, 0.0) ** 2
        + jnp.minimum(ahead_x, 0.0) ** 2
        + jnp.maximum(back_y, 0.0) ** 2
        + jnp.minimum(ahead_y, 0.0) ** 2
    )
    slope_x = (
        padded[..., :-4, 2:-2]
        - 8.0 * padded[..., 1:-3, 2:-2]
        + 8.0 * padded[..., 3:-1, 2:-2]
        - padded[..., 4:, 2:-2]
    ) / 12.0
    slope_y = (
        padded[..., 2:-2, :-4]
        - 8.0 * padded[..., 2:-2, 1:-3]
        + 8.0 * padded[..., 2:-2, 3:-1]
        - padded[..., 2:-2, 4:]
    ) / 12.0
    pushing = jnp.maximum(wind_u * slope_x + wind_v * slope_y, 0.0)
    advanced = level - spread * (upwind + gain * pushing)
    burned = remaining / (1.0 + jnp.exp(advanced)) / burnout
    return (
        jnp.where(active, advanced, level),
        jnp.where(active, remaining - burned, remaining),
        heating + jnp.where(active, yields * burned, 0.0),
    )


def spread_level(padded, level, spread, gain, wind_u, wind_v):
    back_x = level - padded[..., 1:-3, 2:-2]
    ahead_x = padded[..., 3:-1, 2:-2] - level
    back_y = level - padded[..., 2:-2, 1:-3]
    ahead_y = padded[..., 2:-2, 3:-1] - level
    upwind = jnp.sqrt(
        jnp.maximum(back_x, 0.0) ** 2
        + jnp.minimum(ahead_x, 0.0) ** 2
        + jnp.maximum(back_y, 0.0) ** 2
        + jnp.minimum(ahead_y, 0.0) ** 2
    )
    slope_x = (
        padded[..., :-4, 2:-2]
        - 8.0 * padded[..., 1:-3, 2:-2]
        + 8.0 * padded[..., 3:-1, 2:-2]
        - padded[..., 4:, 2:-2]
    ) / 12.0
    slope_y = (
        padded[..., 2:-2, :-4]
        - 8.0 * padded[..., 2:-2, 1:-3]
        + 8.0 * padded[..., 2:-2, 3:-1]
        - padded[..., 2:-2, 4:]
    ) / 12.0
    pushing = jnp.maximum(wind_u * slope_x + wind_v * slope_y, 0.0)
    return level - spread * (upwind + gain * pushing)


def atmos_step(padded, heat_atm):
    width_x = padded.shape[2] - 6
    width_y = padded.shape[3] - 6

    def shifted(along_x, along_y):
        return padded[
            :, :, 3 + along_x : 3 + along_x + width_x, 3 + along_y : 3 + along_y + width_y
        ]

    centre = shifted(0, 0)
    deriv_x = (
        shifted(3, 0)
        - 9.0 * shifted(2, 0)
        + 45.0 * shifted(1, 0)
        - 45.0 * shifted(-1, 0)
        + 9.0 * shifted(-2, 0)
        - shifted(-3, 0)
    ) / 60.0
    deriv_y = (
        shifted(0, 3)
        - 9.0 * shifted(0, 2)
        + 45.0 * shifted(0, 1)
        - 45.0 * shifted(0, -1)
        + 9.0 * shifted(0, -2)
        - shifted(0, -3)
    ) / 60.0
    laplace = shifted(1, 0) + shifted(-1, 0) + shifted(0, 1) + shifted(0, -1) - 4.0 * centre
    updated = centre - COURANT * (centre[0:1] * deriv_x + centre[1:2] * deriv_y) + DIFFUSE * laplace
    depth = padded.shape[1]
    profile = jnp.exp(-4.0 * jnp.arange(depth).astype(jnp.float32) / depth)
    return updated.at[3].add(heat_atm[None, :, :] * profile[:, None, None])


def interp_table(count, ratio, extra):
    indices = jnp.arange(count + 2 * extra) - extra
    coarse = indices // ratio
    within = indices % ratio
    lower = jnp.where(within < ratio // 2, coarse, coarse + 1) + 2
    weight = (within.astype(jnp.float32) + 0.5) / ratio + jnp.where(within < ratio // 2, 0.5, -0.5)
    columns = jnp.arange(count // ratio + 6)
    return (1.0 - weight)[:, None] * (columns[None, :] == lower[:, None]) + weight[:, None] * (
        columns[None, :] == lower[:, None] + 1
    )


def surface_winds(surface, fire_rows, fire_cols, extra_x, extra_y):
    table_x = interp_table(fire_rows, RF, extra_x)
    table_y = interp_table(fire_cols, RF, extra_y)
    along = jnp.einsum("ia,kab->kib", table_x, surface, precision=lax.Precision.HIGHEST)
    return jnp.einsum("kib,jb->kij", along, table_y, precision=lax.Precision.HIGHEST)


HALO_Y = 128


def shift(a, d, axis):
    return pltpu.roll(a, (-d) % a.shape[axis], axis)


def lookup(tab_ref, cat, row, default):
    ncat = tab_ref.shape[0] // 4
    out = jnp.full(cat.shape, default, jnp.float32)
    for category in range(ncat):
        out = jnp.where(cat == float(category), tab_ref[row * ncat + category], out)
    return out


def fire_kernel(tab_ref, ext_ref, wind_ref, fuel_ref, level_out, fuel_out, heat_out):
    rows, cols = fuel_ref.shape
    hx = (ext_ref.shape[1] - rows) // 2
    hy = (ext_ref.shape[2] - cols) // 2
    inner = (slice(hx, hx + rows), slice(hy, hy + cols))
    level = ext_ref[0]
    cat = ext_ref[1]
    nsteps = ext_ref[2]
    spread = lookup(tab_ref, cat, 0, 0.0)
    gain = lookup(tab_ref, cat, 1, 0.0)
    cat_in = cat[inner]
    burnout = lookup(tab_ref, cat_in, 2, 1.0)
    yields = lookup(tab_ref, cat_in, 3, 0.0)
    nsteps_in = nsteps[inner]
    wind_u = wind_ref[0]
    wind_v = wind_ref[1]
    remaining = fuel_ref[...]
    heating = jnp.zeros_like(remaining)
    for substep in range(SUBSTEPS):
        xm1 = shift(level, -1, 0)
        xp1 = shift(level, 1, 0)
        ym1 = shift(level, -1, 1)
        yp1 = shift(level, 1, 1)
        back_x = level - xm1
        ahead_x = xp1 - level
        back_y = level - ym1
        ahead_y = yp1 - level
        upwind = jnp.sqrt(
            jnp.maximum(back_x, 0.0) ** 2
            + jnp.minimum(ahead_x, 0.0) ** 2
            + jnp.maximum(back_y, 0.0) ** 2
            + jnp.minimum(ahead_y, 0.0) ** 2
        )
        slope_x = (shift(level, -2, 0) - 8.0 * xm1 + 8.0 * xp1 - shift(level, 2, 0)) / 12.0
        slope_y = (shift(level, -2, 1) - 8.0 * ym1 + 8.0 * yp1 - shift(level, 2, 1)) / 12.0
        pushing = jnp.maximum(wind_u * slope_x + wind_v * slope_y, 0.0)
        moved = level - spread * (upwind + gain * pushing)
        burned = remaining / (1.0 + jnp.exp(moved[inner])) / burnout
        active = float(substep) < nsteps_in
        remaining = jnp.where(active, remaining - burned, remaining)
        heating = heating + jnp.where(active, yields * burned, 0.0)
        level = jnp.where(float(substep) < nsteps, moved, level)
    level_out[...] = level[inner]
    fuel_out[...] = remaining
    heat_rows = heating.reshape(rows // RF, RF, cols).sum(axis=1)
    lane_in = lax.broadcasted_iota(jnp.int32, (cols, cols // RF), 0) // RF
    lane_out = lax.broadcasted_iota(jnp.int32, (cols, cols // RF), 1)
    blocks = (lane_in == lane_out).astype(jnp.float32)
    heat_out[...] = jnp.dot(
        heat_rows, blocks, precision=lax.Precision.HIGHEST, preferred_element_type=jnp.float32
    ) / (RF * RF)


def fire_step(tables, ext, winds, fuel_left):
    rows, cols = fuel_left.shape
    vmem = pl.BlockSpec(memory_space=pltpu.VMEM)
    return pl.pallas_call(
        fire_kernel,
        out_shape=(
            jax.ShapeDtypeStruct((rows, cols), jnp.float32),
            jax.ShapeDtypeStruct((rows, cols), jnp.float32),
            jax.ShapeDtypeStruct((rows // RF, cols // RF), jnp.float32),
        ),
        in_specs=[pl.BlockSpec(memory_space=pltpu.SMEM), vmem, vmem, vmem],
        out_specs=(vmem, vmem, vmem),
    )(tables, ext, winds, fuel_left)


def atmos_kernel(q_ref, u_ref, v_ref, h_ref, o_ref):
    rows, cols = o_ref.shape[2], o_ref.shape[3]
    width = q_ref.shape[3]

    def at(ref, dx, dy):
        band = ref[0, :, 3 + dx : 3 + dx + rows, :]
        if dy == 0:
            return band[:, :, :cols]
        return pltpu.roll(band, (width - dy) % width, 2)[:, :, :cols]

    centre = at(q_ref, 0, 0)
    deriv_x = (
        at(q_ref, 3, 0)
        - 9.0 * at(q_ref, 2, 0)
        + 45.0 * at(q_ref, 1, 0)
        - 45.0 * at(q_ref, -1, 0)
        + 9.0 * at(q_ref, -2, 0)
        - at(q_ref, -3, 0)
    ) / 60.0
    deriv_y = (
        at(q_ref, 0, 3)
        - 9.0 * at(q_ref, 0, 2)
        + 45.0 * at(q_ref, 0, 1)
        - 45.0 * at(q_ref, 0, -1)
        + 9.0 * at(q_ref, 0, -2)
        - at(q_ref, 0, -3)
    ) / 60.0
    laplace = at(q_ref, 1, 0) + at(q_ref, -1, 0) + at(q_ref, 0, 1) + at(q_ref, 0, -1) - 4.0 * centre
    updated = (
        centre
        - COURANT * (at(u_ref, 0, 0) * deriv_x + at(v_ref, 0, 0) * deriv_y)
        + DIFFUSE * laplace
    )
    o_ref[0] = jnp.where(pl.program_id(0) == 3, updated + h_ref[...], updated)


def atmos_call(padded, heat_atm):
    fields, depth, ext_rows, width = padded.shape
    rows, cols = heat_atm.shape
    profile = jnp.exp(-4.0 * jnp.arange(depth).astype(jnp.float32) / depth)
    heat = heat_atm[None, :, :] * profile[:, None, None]
    block = (1, depth, ext_rows, width)
    return pl.pallas_call(
        atmos_kernel,
        grid=(fields,),
        out_shape=jax.ShapeDtypeStruct((fields, depth, rows, cols), jnp.float32),
        in_specs=[
            pl.BlockSpec(block, lambda f: (f, 0, 0, 0)),
            pl.BlockSpec(block, lambda f: (0, 0, 0, 0)),
            pl.BlockSpec(block, lambda f: (1, 0, 0, 0)),
            pl.BlockSpec((depth, rows, cols), lambda f: (0, 0, 0)),
        ],
        out_specs=pl.BlockSpec((1, depth, rows, cols), lambda f: (f, 0, 0, 0)),
    )(padded, padded, padded, heat)


def fire_halo(level):
    return extended(level, (("gx", 0), ("gy", 1)), 2)


def shards(
    atmos,
    level_set,
    fuel_left,
    fuel_map,
    spread_rate,
    wind_factor,
    burn_time,
    heat_yield,
    burn_tiles,
    burn_count,
    substep_count,
):
    fire_rows, fire_cols = level_set.shape
    atmos_rows, atmos_cols = (atmos.shape[2], atmos.shape[3])
    along_x = extended(atmos, (("gx", 2),), 3)
    count = lax.axis_size("gy")
    from_lo = lax.ppermute(atmos[..., -3:], "gy", [(i, i + 1) for i in range(count - 1)])
    from_hi = lax.ppermute(atmos[..., :3], "gy", [(i + 1, i) for i in range(count - 1)])
    rows_pad = ((0, 0), (0, 0), (3, 3), (0, 0))
    lanes = 2 * (-(-atmos_cols // 128) * 128)
    room = jnp.zeros(along_x.shape[:3] + (lanes - atmos_cols - 6,), jnp.float32)
    padded_atm = jnp.concatenate(
        [along_x, jnp.pad(from_hi, rows_pad), room, jnp.pad(from_lo, rows_pad)], axis=3
    )
    surface = extended(along_x[0:2, 0], (("gy", 2),), 3)
    slots = burn_tiles.reshape(-1)
    listed = burn_count.reshape(())
    tiles_dev = substep_count.size
    slot_valid = jnp.arange(slots.shape[0]) < listed
    tile_on = jnp.any(
        (slots[:, None] == jnp.arange(tiles_dev)[None, :]) & slot_valid[:, None], axis=0
    )
    tile_on = tile_on.reshape(substep_count.shape)
    tiles_x, tiles_y = substep_count.shape
    halo = 2 * SUBSTEPS
    nsteps = jnp.where(tile_on, substep_count, 0).astype(jnp.float32)
    nsteps = jnp.broadcast_to(nsteps[:, None, :, None], (tiles_x, TILE, tiles_y, TILE)).reshape(
        fire_rows, fire_cols
    )
    stacked = jnp.stack([level_set, fuel_map.astype(jnp.float32), nsteps])
    stacked = extended(stacked, (("gx", 1), ("gy", 2)), halo)
    room = jnp.zeros(stacked.shape[:2] + (HALO_Y - halo,), jnp.float32)
    stacked = jnp.concatenate([room, stacked, room], axis=2)
    winds = surface_winds(surface, fire_rows, fire_cols, halo, HALO_Y)
    tables = jnp.concatenate([spread_rate, wind_factor, burn_time, heat_yield]).astype(jnp.float32)
    level, remaining, heat_atm = fire_step(tables, stacked, winds, fuel_left)
    return (atmos_call(padded_atm, heat_atm), level, remaining)


def solution(mesh):
    return jax.shard_map(
        shards,
        mesh=mesh,
        in_specs=(
            P(None, None, "gx", "gy"),
            P("gx", "gy"),
            P("gx", "gy"),
            P("gx", "gy"),
            P(),
            P(),
            P(),
            P(),
            P("gx", "gy", None),
            P("gx", "gy"),
            P("gx", "gy"),
        ),
        out_specs=(P(None, None, "gx", "gy"), P("gx", "gy"), P("gx", "gy")),
        check_vma=False,
    )
```

```python
import jax
import jax.numpy as jnp
from jax import lax
from jax.sharding import PartitionSpec as P
from jax.experimental import pallas as pl
from jax.experimental.pallas import tpu as pltpu

RF = 8
TILE = 64
SUBSTEPS = 8


COURANT = 0.2
DIFFUSE = 0.05


def extended(cells, sides, width):
    for axis, dim in sides:
        count = lax.axis_size(axis)
        ends = count - 1
        head = lax.slice_in_dim(cells, 0, width, axis=dim)
        tail = lax.slice_in_dim(cells, cells.shape[dim] - width, cells.shape[dim], axis=dim)
        cells = jnp.concatenate(
            [
                lax.ppermute(tail, axis, [(i, (i + 1) % count) for i in range(ends)]),
                cells,
                lax.ppermute(head, axis, [((i + 1) % count, i) for i in range(ends)]),
            ],
            axis=dim,
        )
    return cells


def advance(
    padded, level, remaining, heating, spread, gain, burnout, yields, wind_u, wind_v, active
):
    back_x = level - padded[..., 1:-3, 2:-2]
    ahead_x = padded[..., 3:-1, 2:-2] - level
    back_y = level - padded[..., 2:-2, 1:-3]
    ahead_y = padded[..., 2:-2, 3:-1] - level
    upwind = jnp.sqrt(
        jnp.maximum(back_x, 0.0) ** 2
        + jnp.minimum(ahead_x, 0.0) ** 2
        + jnp.maximum(back_y, 0.0) ** 2
        + jnp.minimum(ahead_y, 0.0) ** 2
    )
    slope_x = (
        padded[..., :-4, 2:-2]
        - 8.0 * padded[..., 1:-3, 2:-2]
        + 8.0 * padded[..., 3:-1, 2:-2]
        - padded[..., 4:, 2:-2]
    ) / 12.0
    slope_y = (
        padded[..., 2:-2, :-4]
        - 8.0 * padded[..., 2:-2, 1:-3]
        + 8.0 * padded[..., 2:-2, 3:-1]
        - padded[..., 2:-2, 4:]
    ) / 12.0
    pushing = jnp.maximum(wind_u * slope_x + wind_v * slope_y, 0.0)
    advanced = level - spread * (upwind + gain * pushing)
    burned = remaining / (1.0 + jnp.exp(advanced)) / burnout
    return (
        jnp.where(active, advanced, level),
        jnp.where(active, remaining - burned, remaining),
        heating + jnp.where(active, yields * burned, 0.0),
    )


def spread_level(padded, level, spread, gain, wind_u, wind_v):
    back_x = level - padded[..., 1:-3, 2:-2]
    ahead_x = padded[..., 3:-1, 2:-2] - level
    back_y = level - padded[..., 2:-2, 1:-3]
    ahead_y = padded[..., 2:-2, 3:-1] - level
    upwind = jnp.sqrt(
        jnp.maximum(back_x, 0.0) ** 2
        + jnp.minimum(ahead_x, 0.0) ** 2
        + jnp.maximum(back_y, 0.0) ** 2
        + jnp.minimum(ahead_y, 0.0) ** 2
    )
    slope_x = (
        padded[..., :-4, 2:-2]
        - 8.0 * padded[..., 1:-3, 2:-2]
        + 8.0 * padded[..., 3:-1, 2:-2]
        - padded[..., 4:, 2:-2]
    ) / 12.0
    slope_y = (
        padded[..., 2:-2, :-4]
        - 8.0 * padded[..., 2:-2, 1:-3]
        + 8.0 * padded[..., 2:-2, 3:-1]
        - padded[..., 2:-2, 4:]
    ) / 12.0
    pushing = jnp.maximum(wind_u * slope_x + wind_v * slope_y, 0.0)
    return level - spread * (upwind + gain * pushing)


def atmos_step(padded, heat_atm):
    width_x = padded.shape[2] - 6
    width_y = padded.shape[3] - 6

    def shifted(along_x, along_y):
        return padded[
            :, :, 3 + along_x : 3 + along_x + width_x, 3 + along_y : 3 + along_y + width_y
        ]

    centre = shifted(0, 0)
    deriv_x = (
        shifted(3, 0)
        - 9.0 * shifted(2, 0)
        + 45.0 * shifted(1, 0)
        - 45.0 * shifted(-1, 0)
        + 9.0 * shifted(-2, 0)
        - shifted(-3, 0)
    ) / 60.0
    deriv_y = (
        shifted(0, 3)
        - 9.0 * shifted(0, 2)
        + 45.0 * shifted(0, 1)
        - 45.0 * shifted(0, -1)
        + 9.0 * shifted(0, -2)
        - shifted(0, -3)
    ) / 60.0
    laplace = shifted(1, 0) + shifted(-1, 0) + shifted(0, 1) + shifted(0, -1) - 4.0 * centre
    updated = centre - COURANT * (centre[0:1] * deriv_x + centre[1:2] * deriv_y) + DIFFUSE * laplace
    depth = padded.shape[1]
    profile = jnp.exp(-4.0 * jnp.arange(depth).astype(jnp.float32) / depth)
    return updated.at[3].add(heat_atm[None, :, :] * profile[:, None, None])


def interp_table(count, ratio, extra):
    indices = jnp.arange(count + 2 * extra) - extra
    coarse = indices // ratio
    within = indices % ratio
    lower = jnp.where(within < ratio // 2, coarse, coarse + 1) + 2
    weight = (within.astype(jnp.float32) + 0.5) / ratio + jnp.where(within < ratio // 2, 0.5, -0.5)
    columns = jnp.arange(count // ratio + 6)
    return (1.0 - weight)[:, None] * (columns[None, :] == lower[:, None]) + weight[:, None] * (
        columns[None, :] == lower[:, None] + 1
    )


def surface_winds(surface, fire_rows, fire_cols, extra_x, extra_y):
    table_x = interp_table(fire_rows, RF, extra_x)
    table_y = interp_table(fire_cols, RF, extra_y)
    along = jnp.einsum("ia,kab->kib", table_x, surface, precision=lax.Precision.HIGHEST)
    return jnp.einsum("kib,jb->kij", along, table_y, precision=lax.Precision.HIGHEST)


HALO_Y = 128


def shift(a, d, axis):
    return pltpu.roll(a, (-d) % a.shape[axis], axis)


def lookup(tab_ref, cat, row, default):
    ncat = tab_ref.shape[0] // 4
    out = jnp.full(cat.shape, default, jnp.float32)
    for category in range(ncat):
        out = jnp.where(cat == float(category), tab_ref[row * ncat + category], out)
    return out


def fire_kernel(tab_ref, ext_ref, wind_ref, fuel_ref, level_out, fuel_out, heat_out):
    rows, cols = fuel_ref.shape
    hx = (ext_ref.shape[1] - rows) // 2
    hy = (ext_ref.shape[2] - cols) // 2
    inner = (slice(hx, hx + rows), slice(hy, hy + cols))
    level = ext_ref[0]
    cat = ext_ref[1]
    nsteps = ext_ref[2]
    spread = lookup(tab_ref, cat, 0, 0.0)
    gain = lookup(tab_ref, cat, 1, 0.0)
    cat_in = cat[inner]
    burnout = lookup(tab_ref, cat_in, 2, 1.0)
    yields = lookup(tab_ref, cat_in, 3, 0.0)
    nsteps_in = nsteps[inner]
    wind_u = wind_ref[0]
    wind_v = wind_ref[1]
    remaining = fuel_ref[...]
    heating = jnp.zeros_like(remaining)
    for substep in range(SUBSTEPS):
        xm1 = shift(level, -1, 0)
        xp1 = shift(level, 1, 0)
        ym1 = shift(level, -1, 1)
        yp1 = shift(level, 1, 1)
        back_x = level - xm1
        ahead_x = xp1 - level
        back_y = level - ym1
        ahead_y = yp1 - level
        upwind = jnp.sqrt(
            jnp.maximum(back_x, 0.0) ** 2
            + jnp.minimum(ahead_x, 0.0) ** 2
            + jnp.maximum(back_y, 0.0) ** 2
            + jnp.minimum(ahead_y, 0.0) ** 2
        )
        slope_x = (shift(level, -2, 0) - 8.0 * xm1 + 8.0 * xp1 - shift(level, 2, 0)) / 12.0
        slope_y = (shift(level, -2, 1) - 8.0 * ym1 + 8.0 * yp1 - shift(level, 2, 1)) / 12.0
        pushing = jnp.maximum(wind_u * slope_x + wind_v * slope_y, 0.0)
        moved = level - spread * (upwind + gain * pushing)
        burned = remaining / (1.0 + jnp.exp(moved[inner])) / burnout
        active = float(substep) < nsteps_in
        remaining = jnp.where(active, remaining - burned, remaining)
        heating = heating + jnp.where(active, yields * burned, 0.0)
        level = jnp.where(float(substep) < nsteps, moved, level)
    level_out[...] = level[inner]
    fuel_out[...] = remaining
    heat_rows = heating.reshape(rows // RF, RF, cols).sum(axis=1)
    lane_in = lax.broadcasted_iota(jnp.int32, (cols, cols // RF), 0) // RF
    lane_out = lax.broadcasted_iota(jnp.int32, (cols, cols // RF), 1)
    blocks = (lane_in == lane_out).astype(jnp.float32)
    heat_out[...] = jnp.dot(
        heat_rows, blocks, precision=lax.Precision.HIGHEST, preferred_element_type=jnp.float32
    ) / (RF * RF)


def fire_step(tables, ext, winds, fuel_left):
    rows, cols = fuel_left.shape
    vmem = pl.BlockSpec(memory_space=pltpu.VMEM)
    return pl.pallas_call(
        fire_kernel,
        out_shape=(
            jax.ShapeDtypeStruct((rows, cols), jnp.float32),
            jax.ShapeDtypeStruct((rows, cols), jnp.float32),
            jax.ShapeDtypeStruct((rows // RF, cols // RF), jnp.float32),
        ),
        in_specs=[pl.BlockSpec(memory_space=pltpu.SMEM), vmem, vmem, vmem],
        out_specs=(vmem, vmem, vmem),
    )(tables, ext, winds, fuel_left)


def atmos_kernel(p_ref, q_ref, u_ref, v_ref, h_ref, o_ref):
    rows, cols = o_ref.shape[2], o_ref.shape[3]
    width = q_ref.shape[3]

    def at(ref, dx, dy):
        band = ref[0, :, 3 + dx : 3 + dx + rows, :]
        if dy == 0:
            return band[:, :, :cols]
        return pltpu.roll(band, (width - dy) % width, 2)[:, :, :cols]

    centre = at(q_ref, 0, 0)
    deriv_x = (
        at(q_ref, 3, 0)
        - 9.0 * at(q_ref, 2, 0)
        + 45.0 * at(q_ref, 1, 0)
        - 45.0 * at(q_ref, -1, 0)
        + 9.0 * at(q_ref, -2, 0)
        - at(q_ref, -3, 0)
    ) / 60.0
    deriv_y = (
        at(q_ref, 0, 3)
        - 9.0 * at(q_ref, 0, 2)
        + 45.0 * at(q_ref, 0, 1)
        - 45.0 * at(q_ref, 0, -1)
        + 9.0 * at(q_ref, 0, -2)
        - at(q_ref, 0, -3)
    ) / 60.0
    laplace = at(q_ref, 1, 0) + at(q_ref, -1, 0) + at(q_ref, 0, 1) + at(q_ref, 0, -1) - 4.0 * centre
    updated = (
        centre
        - COURANT * (at(u_ref, 0, 0) * deriv_x + at(v_ref, 0, 0) * deriv_y)
        + DIFFUSE * laplace
    )
    heat = h_ref[...]
    profile_heat = jnp.stack([heat * p_ref[k] for k in range(updated.shape[0])])
    o_ref[0] = jnp.where(pl.program_id(0) == 3, updated + profile_heat, updated)


def atmos_call(padded, heat_atm):
    fields, depth, ext_rows, width = padded.shape
    rows, cols = heat_atm.shape
    profile = jnp.exp(-4.0 * jnp.arange(depth).astype(jnp.float32) / depth)
    block = (1, depth, ext_rows, width)
    return pl.pallas_call(
        atmos_kernel,
        grid=(fields,),
        out_shape=jax.ShapeDtypeStruct((fields, depth, rows, cols), jnp.float32),
        in_specs=[
            pl.BlockSpec(memory_space=pltpu.SMEM),
            pl.BlockSpec(block, lambda f: (f, 0, 0, 0)),
            pl.BlockSpec(block, lambda f: (0, 0, 0, 0)),
            pl.BlockSpec(block, lambda f: (1, 0, 0, 0)),
            pl.BlockSpec((rows, cols), lambda f: (0, 0)),
        ],
        out_specs=pl.BlockSpec((1, depth, rows, cols), lambda f: (f, 0, 0, 0)),
    )(profile, padded, padded, padded, heat_atm)


def fire_halo(level):
    return extended(level, (("gx", 0), ("gy", 1)), 2)


def shards(
    atmos,
    level_set,
    fuel_left,
    fuel_map,
    spread_rate,
    wind_factor,
    burn_time,
    heat_yield,
    burn_tiles,
    burn_count,
    substep_count,
):
    fire_rows, fire_cols = level_set.shape
    atmos_rows, atmos_cols = (atmos.shape[2], atmos.shape[3])
    along_x = extended(atmos, (("gx", 2),), 3)
    count = lax.axis_size("gy")
    from_lo = lax.ppermute(atmos[..., -3:], "gy", [(i, i + 1) for i in range(count - 1)])
    from_hi = lax.ppermute(atmos[..., :3], "gy", [(i + 1, i) for i in range(count - 1)])
    rows_pad = ((0, 0), (0, 0), (3, 3), (0, 0))
    lanes = 2 * (-(-atmos_cols // 128) * 128)
    room = jnp.zeros(along_x.shape[:3] + (lanes - atmos_cols - 6,), jnp.float32)
    padded_atm = jnp.concatenate(
        [along_x, jnp.pad(from_hi, rows_pad), room, jnp.pad(from_lo, rows_pad)], axis=3
    )
    surface = extended(along_x[0:2, 0], (("gy", 2),), 3)
    slots = burn_tiles.reshape(-1)
    listed = burn_count.reshape(())
    tiles_dev = substep_count.size
    slot_valid = jnp.arange(slots.shape[0]) < listed
    tile_on = jnp.any(
        (slots[:, None] == jnp.arange(tiles_dev)[None, :]) & slot_valid[:, None], axis=0
    )
    tile_on = tile_on.reshape(substep_count.shape)
    tiles_x, tiles_y = substep_count.shape
    halo = 2 * SUBSTEPS
    nsteps = jnp.where(tile_on, substep_count, 0).astype(jnp.float32)
    nsteps = jnp.broadcast_to(nsteps[:, None, :, None], (tiles_x, TILE, tiles_y, TILE)).reshape(
        fire_rows, fire_cols
    )
    stacked = jnp.stack([level_set, fuel_map.astype(jnp.float32), nsteps])
    stacked = extended(stacked, (("gx", 1), ("gy", 2)), halo)
    room = jnp.zeros(stacked.shape[:2] + (HALO_Y - halo,), jnp.float32)
    stacked = jnp.concatenate([room, stacked, room], axis=2)
    winds = surface_winds(surface, fire_rows, fire_cols, halo, HALO_Y)
    tables = jnp.concatenate([spread_rate, wind_factor, burn_time, heat_yield]).astype(jnp.float32)
    level, remaining, heat_atm = fire_step(tables, stacked, winds, fuel_left)
    return (atmos_call(padded_atm, heat_atm), level, remaining)


def solution(mesh):
    return jax.shard_map(
        shards,
        mesh=mesh,
        in_specs=(
            P(None, None, "gx", "gy"),
            P("gx", "gy"),
            P("gx", "gy"),
            P("gx", "gy"),
            P(),
            P(),
            P(),
            P(),
            P("gx", "gy", None),
            P("gx", "gy"),
            P("gx", "gy"),
        ),
        out_specs=(P(None, None, "gx", "gy"), P("gx", "gy"), P("gx", "gy")),
        check_vma=False,
    )
```

```python
import jax
import jax.numpy as jnp
from jax import lax
from jax.sharding import PartitionSpec as P
from jax.experimental import pallas as pl
from jax.experimental.pallas import tpu as pltpu

RF = 8
TILE = 64
SUBSTEPS = 8


COURANT = 0.2
DIFFUSE = 0.05


def extended(cells, sides, width):
    for axis, dim in sides:
        count = lax.axis_size(axis)
        ends = count - 1
        head = lax.slice_in_dim(cells, 0, width, axis=dim)
        tail = lax.slice_in_dim(cells, cells.shape[dim] - width, cells.shape[dim], axis=dim)
        cells = jnp.concatenate(
            [
                lax.ppermute(tail, axis, [(i, (i + 1) % count) for i in range(ends)]),
                cells,
                lax.ppermute(head, axis, [((i + 1) % count, i) for i in range(ends)]),
            ],
            axis=dim,
        )
    return cells


def advance(
    padded, level, remaining, heating, spread, gain, burnout, yields, wind_u, wind_v, active
):
    back_x = level - padded[..., 1:-3, 2:-2]
    ahead_x = padded[..., 3:-1, 2:-2] - level
    back_y = level - padded[..., 2:-2, 1:-3]
    ahead_y = padded[..., 2:-2, 3:-1] - level
    upwind = jnp.sqrt(
        jnp.maximum(back_x, 0.0) ** 2
        + jnp.minimum(ahead_x, 0.0) ** 2
        + jnp.maximum(back_y, 0.0) ** 2
        + jnp.minimum(ahead_y, 0.0) ** 2
    )
    slope_x = (
        padded[..., :-4, 2:-2]
        - 8.0 * padded[..., 1:-3, 2:-2]
        + 8.0 * padded[..., 3:-1, 2:-2]
        - padded[..., 4:, 2:-2]
    ) / 12.0
    slope_y = (
        padded[..., 2:-2, :-4]
        - 8.0 * padded[..., 2:-2, 1:-3]
        + 8.0 * padded[..., 2:-2, 3:-1]
        - padded[..., 2:-2, 4:]
    ) / 12.0
    pushing = jnp.maximum(wind_u * slope_x + wind_v * slope_y, 0.0)
    advanced = level - spread * (upwind + gain * pushing)
    burned = remaining / (1.0 + jnp.exp(advanced)) / burnout
    return (
        jnp.where(active, advanced, level),
        jnp.where(active, remaining - burned, remaining),
        heating + jnp.where(active, yields * burned, 0.0),
    )


def spread_level(padded, level, spread, gain, wind_u, wind_v):
    back_x = level - padded[..., 1:-3, 2:-2]
    ahead_x = padded[..., 3:-1, 2:-2] - level
    back_y = level - padded[..., 2:-2, 1:-3]
    ahead_y = padded[..., 2:-2, 3:-1] - level
    upwind = jnp.sqrt(
        jnp.maximum(back_x, 0.0) ** 2
        + jnp.minimum(ahead_x, 0.0) ** 2
        + jnp.maximum(back_y, 0.0) ** 2
        + jnp.minimum(ahead_y, 0.0) ** 2
    )
    slope_x = (
        padded[..., :-4, 2:-2]
        - 8.0 * padded[..., 1:-3, 2:-2]
        + 8.0 * padded[..., 3:-1, 2:-2]
        - padded[..., 4:, 2:-2]
    ) / 12.0
    slope_y = (
        padded[..., 2:-2, :-4]
        - 8.0 * padded[..., 2:-2, 1:-3]
        + 8.0 * padded[..., 2:-2, 3:-1]
        - padded[..., 2:-2, 4:]
    ) / 12.0
    pushing = jnp.maximum(wind_u * slope_x + wind_v * slope_y, 0.0)
    return level - spread * (upwind + gain * pushing)


def atmos_step(padded, heat_atm):
    width_x = padded.shape[2] - 6
    width_y = padded.shape[3] - 6

    def shifted(along_x, along_y):
        return padded[
            :, :, 3 + along_x : 3 + along_x + width_x, 3 + along_y : 3 + along_y + width_y
        ]

    centre = shifted(0, 0)
    deriv_x = (
        shifted(3, 0)
        - 9.0 * shifted(2, 0)
        + 45.0 * shifted(1, 0)
        - 45.0 * shifted(-1, 0)
        + 9.0 * shifted(-2, 0)
        - shifted(-3, 0)
    ) / 60.0
    deriv_y = (
        shifted(0, 3)
        - 9.0 * shifted(0, 2)
        + 45.0 * shifted(0, 1)
        - 45.0 * shifted(0, -1)
        + 9.0 * shifted(0, -2)
        - shifted(0, -3)
    ) / 60.0
    laplace = shifted(1, 0) + shifted(-1, 0) + shifted(0, 1) + shifted(0, -1) - 4.0 * centre
    updated = centre - COURANT * (centre[0:1] * deriv_x + centre[1:2] * deriv_y) + DIFFUSE * laplace
    depth = padded.shape[1]
    profile = jnp.exp(-4.0 * jnp.arange(depth).astype(jnp.float32) / depth)
    return updated.at[3].add(heat_atm[None, :, :] * profile[:, None, None])


def interp_table(count, ratio, extra):
    indices = jnp.arange(count + 2 * extra) - extra
    coarse = indices // ratio
    within = indices % ratio
    lower = jnp.where(within < ratio // 2, coarse, coarse + 1) + 2
    weight = (within.astype(jnp.float32) + 0.5) / ratio + jnp.where(within < ratio // 2, 0.5, -0.5)
    columns = jnp.arange(count // ratio + 6)
    return (1.0 - weight)[:, None] * (columns[None, :] == lower[:, None]) + weight[:, None] * (
        columns[None, :] == lower[:, None] + 1
    )


def surface_winds(surface, fire_rows, fire_cols, extra_x, extra_y):
    table_x = interp_table(fire_rows, RF, extra_x)
    table_y = interp_table(fire_cols, RF, extra_y)
    along = jnp.einsum("ia,kab->kib", table_x, surface, precision=lax.Precision.HIGHEST)
    return jnp.einsum("kib,jb->kij", along, table_y, precision=lax.Precision.HIGHEST)


HALO_Y = 128


def shift(a, d, axis):
    return pltpu.roll(a, (-d) % a.shape[axis], axis)


def lookup(tab_ref, cat, row, default):
    ncat = tab_ref.shape[0] // 4
    out = jnp.full(cat.shape, default, jnp.float32)
    for category in range(ncat):
        out = jnp.where(cat == float(category), tab_ref[row * ncat + category], out)
    return out


def fire_kernel(tab_ref, ext_ref, wind_ref, fuel_ref, level_out, fuel_out, heat_out):
    rows, cols = fuel_ref.shape
    hx = (ext_ref.shape[1] - rows) // 2
    hy = (ext_ref.shape[2] - cols) // 2
    inner = (slice(hx, hx + rows), slice(hy, hy + cols))
    level = ext_ref[0]
    cat = ext_ref[1]
    nsteps = ext_ref[2]
    spread = lookup(tab_ref, cat, 0, 0.0)
    gain = lookup(tab_ref, cat, 1, 0.0)
    cat_in = cat[inner]
    burnout = lookup(tab_ref, cat_in, 2, 1.0)
    yields = lookup(tab_ref, cat_in, 3, 0.0)
    nsteps_in = nsteps[inner]
    wind_u = wind_ref[0]
    wind_v = wind_ref[1]
    remaining = fuel_ref[...]
    heating = jnp.zeros_like(remaining)
    for substep in range(SUBSTEPS):
        xm1 = shift(level, -1, 0)
        xp1 = shift(level, 1, 0)
        ym1 = shift(level, -1, 1)
        yp1 = shift(level, 1, 1)
        back_x = level - xm1
        ahead_x = xp1 - level
        back_y = level - ym1
        ahead_y = yp1 - level
        upwind = jnp.sqrt(
            jnp.maximum(back_x, 0.0) ** 2
            + jnp.minimum(ahead_x, 0.0) ** 2
            + jnp.maximum(back_y, 0.0) ** 2
            + jnp.minimum(ahead_y, 0.0) ** 2
        )
        slope_x = (shift(level, -2, 0) - 8.0 * xm1 + 8.0 * xp1 - shift(level, 2, 0)) / 12.0
        slope_y = (shift(level, -2, 1) - 8.0 * ym1 + 8.0 * yp1 - shift(level, 2, 1)) / 12.0
        pushing = jnp.maximum(wind_u * slope_x + wind_v * slope_y, 0.0)
        moved = level - spread * (upwind + gain * pushing)
        burned = remaining / (1.0 + jnp.exp(moved[inner])) / burnout
        active = float(substep) < nsteps_in
        remaining = jnp.where(active, remaining - burned, remaining)
        heating = heating + jnp.where(active, yields * burned, 0.0)
        level = jnp.where(float(substep) < nsteps, moved, level)
    level_out[...] = level[inner]
    fuel_out[...] = remaining
    heat_rows = heating.reshape(rows // RF, RF, cols).sum(axis=1)
    lane_in = lax.broadcasted_iota(jnp.int32, (cols, cols // RF), 0) // RF
    lane_out = lax.broadcasted_iota(jnp.int32, (cols, cols // RF), 1)
    blocks = (lane_in == lane_out).astype(jnp.float32)
    heat_out[...] = jnp.dot(
        heat_rows, blocks, precision=lax.Precision.HIGHEST, preferred_element_type=jnp.float32
    ) / (RF * RF)


def fire_step(tables, ext, winds, fuel_left):
    rows, cols = fuel_left.shape
    vmem = pl.BlockSpec(memory_space=pltpu.VMEM)
    return pl.pallas_call(
        fire_kernel,
        out_shape=(
            jax.ShapeDtypeStruct((rows, cols), jnp.float32),
            jax.ShapeDtypeStruct((rows, cols), jnp.float32),
            jax.ShapeDtypeStruct((rows // RF, cols // RF), jnp.float32),
        ),
        in_specs=[pl.BlockSpec(memory_space=pltpu.SMEM), vmem, vmem, vmem],
        out_specs=(vmem, vmem, vmem),
    )(tables, ext, winds, fuel_left)


def atmos_kernel(p_ref, q_ref, lo_ref, hi_ref, y_ref, u_ref, v_ref, h_ref, o_ref, ext_ref):
    rows, cols = o_ref.shape[2], o_ref.shape[3]
    halo = lo_ref.shape[2]
    centre = q_ref[0]
    ext_ref[:, 0:halo, :] = lo_ref[0]
    ext_ref[:, halo : halo + rows, :] = centre
    ext_ref[:, halo + rows : 2 * halo + rows, :] = hi_ref[0]
    ends = y_ref[0]
    lane = lax.broadcasted_iota(jnp.int32, centre.shape, 2)

    def ax(dx):
        return ext_ref[:, halo + dx : halo + dx + rows, :]

    def ay(dy):
        if dy > 0:
            turn = cols - dy
            return jnp.where(lane >= turn, pltpu.roll(ends, turn, 2), pltpu.roll(centre, turn, 2))
        return jnp.where(lane < -dy, pltpu.roll(ends, -dy, 2), pltpu.roll(centre, -dy, 2))

    deriv_x = (
        ax(3) - 9.0 * ax(2) + 45.0 * ax(1) - 45.0 * ax(-1) + 9.0 * ax(-2) - ax(-3)
    ) / 60.0
    deriv_y = (
        ay(3) - 9.0 * ay(2) + 45.0 * ay(1) - 45.0 * ay(-1) + 9.0 * ay(-2) - ay(-3)
    ) / 60.0
    laplace = ax(1) + ax(-1) + ay(1) + ay(-1) - 4.0 * centre
    updated = centre - COURANT * (u_ref[0] * deriv_x + v_ref[0] * deriv_y) + DIFFUSE * laplace
    heat = h_ref[...]
    profile_heat = jnp.stack([heat * p_ref[k] for k in range(updated.shape[0])])
    o_ref[0] = jnp.where(pl.program_id(0) == 3, updated + profile_heat, updated)


def atmos_call(atmos, x_lo, x_hi, y_ends, heat_atm):
    fields, depth, rows, cols = atmos.shape
    halo = x_lo.shape[2]
    profile = jnp.exp(-4.0 * jnp.arange(depth).astype(jnp.float32) / depth)
    block = (1, depth, rows, cols)
    edge = (1, depth, halo, cols)
    return pl.pallas_call(
        atmos_kernel,
        grid=(fields,),
        out_shape=jax.ShapeDtypeStruct((fields, depth, rows, cols), jnp.float32),
        in_specs=[
            pl.BlockSpec(memory_space=pltpu.SMEM),
            pl.BlockSpec(block, lambda f: (f, 0, 0, 0)),
            pl.BlockSpec(edge, lambda f: (f, 0, 0, 0)),
            pl.BlockSpec(edge, lambda f: (f, 0, 0, 0)),
            pl.BlockSpec(block, lambda f: (f, 0, 0, 0)),
            pl.BlockSpec(block, lambda f: (0, 0, 0, 0)),
            pl.BlockSpec(block, lambda f: (1, 0, 0, 0)),
            pl.BlockSpec((rows, cols), lambda f: (0, 0)),
        ],
        out_specs=pl.BlockSpec(block, lambda f: (f, 0, 0, 0)),
        scratch_shapes=[pltpu.VMEM((depth, -(-(rows + 2 * halo) // 8) * 8, cols), jnp.float32)],
    )(profile, atmos, x_lo, x_hi, y_ends, atmos, atmos, heat_atm)


def fire_halo(level):
    return extended(level, (("gx", 0), ("gy", 1)), 2)


def shards(
    atmos,
    level_set,
    fuel_left,
    fuel_map,
    spread_rate,
    wind_factor,
    burn_time,
    heat_yield,
    burn_tiles,
    burn_count,
    substep_count,
):
    fire_rows, fire_cols = level_set.shape
    atmos_rows, atmos_cols = (atmos.shape[2], atmos.shape[3])
    count_x = lax.axis_size("gx")
    x_lo = lax.ppermute(atmos[:, :, -3:], "gx", [(i, i + 1) for i in range(count_x - 1)])
    x_hi = lax.ppermute(atmos[:, :, :3], "gx", [(i + 1, i) for i in range(count_x - 1)])
    count = lax.axis_size("gy")
    from_lo = lax.ppermute(atmos[..., -3:], "gy", [(i, i + 1) for i in range(count - 1)])
    from_hi = lax.ppermute(atmos[..., :3], "gy", [(i + 1, i) for i in range(count - 1)])
    room = jnp.zeros(atmos.shape[:3] + (atmos_cols - 6,), jnp.float32)
    y_ends = jnp.concatenate([from_hi, room, from_lo], axis=3)
    along_x = jnp.concatenate([x_lo[0:2, 0:1], atmos[0:2, 0:1], x_hi[0:2, 0:1]], axis=2)
    surface = extended(along_x[:, 0], (("gy", 2),), 3)
    slots = burn_tiles.reshape(-1)
    listed = burn_count.reshape(())
    tiles_dev = substep_count.size
    slot_valid = jnp.arange(slots.shape[0]) < listed
    tile_on = jnp.any(
        (slots[:, None] == jnp.arange(tiles_dev)[None, :]) & slot_valid[:, None], axis=0
    )
    tile_on = tile_on.reshape(substep_count.shape)
    tiles_x, tiles_y = substep_count.shape
    halo = 2 * SUBSTEPS
    nsteps = jnp.where(tile_on, substep_count, 0).astype(jnp.float32)
    nsteps = jnp.broadcast_to(nsteps[:, None, :, None], (tiles_x, TILE, tiles_y, TILE)).reshape(
        fire_rows, fire_cols
    )
    stacked = jnp.stack([level_set, fuel_map.astype(jnp.float32), nsteps])
    stacked = extended(stacked, (("gx", 1), ("gy", 2)), halo)
    room = jnp.zeros(stacked.shape[:2] + (HALO_Y - halo,), jnp.float32)
    stacked = jnp.concatenate([room, stacked, room], axis=2)
    winds = surface_winds(surface, fire_rows, fire_cols, halo, HALO_Y)
    tables = jnp.concatenate([spread_rate, wind_factor, burn_time, heat_yield]).astype(jnp.float32)
    level, remaining, heat_atm = fire_step(tables, stacked, winds, fuel_left)
    return (atmos_call(atmos, x_lo, x_hi, y_ends, heat_atm), level, remaining)


def solution(mesh):
    return jax.shard_map(
        shards,
        mesh=mesh,
        in_specs=(
            P(None, None, "gx", "gy"),
            P("gx", "gy"),
            P("gx", "gy"),
            P("gx", "gy"),
            P(),
            P(),
            P(),
            P(),
            P("gx", "gy", None),
            P("gx", "gy"),
            P("gx", "gy"),
        ),
        out_specs=(P(None, None, "gx", "gy"), P("gx", "gy"), P("gx", "gy")),
        check_vma=False,
    )
```

```python
import jax
import jax.numpy as jnp
from jax import lax
from jax.sharding import PartitionSpec as P
from jax.experimental import pallas as pl
from jax.experimental.pallas import tpu as pltpu

RF = 8
TILE = 64
SUBSTEPS = 8


COURANT = 0.2
DIFFUSE = 0.05


def extended(cells, sides, width):
    for axis, dim in sides:
        count = lax.axis_size(axis)
        ends = count - 1
        head = lax.slice_in_dim(cells, 0, width, axis=dim)
        tail = lax.slice_in_dim(cells, cells.shape[dim] - width, cells.shape[dim], axis=dim)
        cells = jnp.concatenate(
            [
                lax.ppermute(tail, axis, [(i, (i + 1) % count) for i in range(ends)]),
                cells,
                lax.ppermute(head, axis, [((i + 1) % count, i) for i in range(ends)]),
            ],
            axis=dim,
        )
    return cells


def advance(
    padded, level, remaining, heating, spread, gain, burnout, yields, wind_u, wind_v, active
):
    back_x = level - padded[..., 1:-3, 2:-2]
    ahead_x = padded[..., 3:-1, 2:-2] - level
    back_y = level - padded[..., 2:-2, 1:-3]
    ahead_y = padded[..., 2:-2, 3:-1] - level
    upwind = jnp.sqrt(
        jnp.maximum(back_x, 0.0) ** 2
        + jnp.minimum(ahead_x, 0.0) ** 2
        + jnp.maximum(back_y, 0.0) ** 2
        + jnp.minimum(ahead_y, 0.0) ** 2
    )
    slope_x = (
        padded[..., :-4, 2:-2]
        - 8.0 * padded[..., 1:-3, 2:-2]
        + 8.0 * padded[..., 3:-1, 2:-2]
        - padded[..., 4:, 2:-2]
    ) / 12.0
    slope_y = (
        padded[..., 2:-2, :-4]
        - 8.0 * padded[..., 2:-2, 1:-3]
        + 8.0 * padded[..., 2:-2, 3:-1]
        - padded[..., 2:-2, 4:]
    ) / 12.0
    pushing = jnp.maximum(wind_u * slope_x + wind_v * slope_y, 0.0)
    advanced = level - spread * (upwind + gain * pushing)
    burned = remaining / (1.0 + jnp.exp(advanced)) / burnout
    return (
        jnp.where(active, advanced, level),
        jnp.where(active, remaining - burned, remaining),
        heating + jnp.where(active, yields * burned, 0.0),
    )


def spread_level(padded, level, spread, gain, wind_u, wind_v):
    back_x = level - padded[..., 1:-3, 2:-2]
    ahead_x = padded[..., 3:-1, 2:-2] - level
    back_y = level - padded[..., 2:-2, 1:-3]
    ahead_y = padded[..., 2:-2, 3:-1] - level
    upwind = jnp.sqrt(
        jnp.maximum(back_x, 0.0) ** 2
        + jnp.minimum(ahead_x, 0.0) ** 2
        + jnp.maximum(back_y, 0.0) ** 2
        + jnp.minimum(ahead_y, 0.0) ** 2
    )
    slope_x = (
        padded[..., :-4, 2:-2]
        - 8.0 * padded[..., 1:-3, 2:-2]
        + 8.0 * padded[..., 3:-1, 2:-2]
        - padded[..., 4:, 2:-2]
    ) / 12.0
    slope_y = (
        padded[..., 2:-2, :-4]
        - 8.0 * padded[..., 2:-2, 1:-3]
        + 8.0 * padded[..., 2:-2, 3:-1]
        - padded[..., 2:-2, 4:]
    ) / 12.0
    pushing = jnp.maximum(wind_u * slope_x + wind_v * slope_y, 0.0)
    return level - spread * (upwind + gain * pushing)


def atmos_step(padded, heat_atm):
    width_x = padded.shape[2] - 6
    width_y = padded.shape[3] - 6

    def shifted(along_x, along_y):
        return padded[
            :, :, 3 + along_x : 3 + along_x + width_x, 3 + along_y : 3 + along_y + width_y
        ]

    centre = shifted(0, 0)
    deriv_x = (
        shifted(3, 0)
        - 9.0 * shifted(2, 0)
        + 45.0 * shifted(1, 0)
        - 45.0 * shifted(-1, 0)
        + 9.0 * shifted(-2, 0)
        - shifted(-3, 0)
    ) / 60.0
    deriv_y = (
        shifted(0, 3)
        - 9.0 * shifted(0, 2)
        + 45.0 * shifted(0, 1)
        - 45.0 * shifted(0, -1)
        + 9.0 * shifted(0, -2)
        - shifted(0, -3)
    ) / 60.0
    laplace = shifted(1, 0) + shifted(-1, 0) + shifted(0, 1) + shifted(0, -1) - 4.0 * centre
    updated = centre - COURANT * (centre[0:1] * deriv_x + centre[1:2] * deriv_y) + DIFFUSE * laplace
    depth = padded.shape[1]
    profile = jnp.exp(-4.0 * jnp.arange(depth).astype(jnp.float32) / depth)
    return updated.at[3].add(heat_atm[None, :, :] * profile[:, None, None])


def interp_table(count, ratio, extra):
    indices = jnp.arange(count + 2 * extra) - extra
    coarse = indices // ratio
    within = indices % ratio
    lower = jnp.where(within < ratio // 2, coarse, coarse + 1) + 2
    weight = (within.astype(jnp.float32) + 0.5) / ratio + jnp.where(within < ratio // 2, 0.5, -0.5)
    columns = jnp.arange(count // ratio + 6)
    return (1.0 - weight)[:, None] * (columns[None, :] == lower[:, None]) + weight[:, None] * (
        columns[None, :] == lower[:, None] + 1
    )


def surface_winds(surface, fire_rows, fire_cols, extra_x, extra_y):
    table_x = interp_table(fire_rows, RF, extra_x)
    table_y = interp_table(fire_cols, RF, extra_y)
    along = jnp.einsum("ia,kab->kib", table_x, surface, precision=lax.Precision.HIGHEST)
    return jnp.einsum("kib,jb->kij", along, table_y, precision=lax.Precision.HIGHEST)


HALO_Y = 128


def shift(a, d, axis):
    return pltpu.roll(a, (-d) % a.shape[axis], axis)


def lookup(tab_ref, cat, row, default):
    ncat = tab_ref.shape[0] // 4
    out = jnp.full(cat.shape, default, jnp.float32)
    for category in range(ncat):
        out = jnp.where(cat == float(category), tab_ref[row * ncat + category], out)
    return out


def fire_kernel(tab_ref, ext_ref, wind_ref, fuel_ref, level_out, fuel_out, heat_out):
    rows, cols = fuel_ref.shape
    hx = (ext_ref.shape[1] - rows) // 2
    hy = (ext_ref.shape[2] - cols) // 2
    inner = (slice(hx, hx + rows), slice(hy, hy + cols))
    level = ext_ref[0]
    cat = ext_ref[1]
    nsteps = ext_ref[2]
    spread = lookup(tab_ref, cat, 0, 0.0)
    gain = lookup(tab_ref, cat, 1, 0.0)
    cat_in = cat[inner]
    burnout = lookup(tab_ref, cat_in, 2, 1.0)
    yields = lookup(tab_ref, cat_in, 3, 0.0)
    nsteps_in = nsteps[inner]
    wind_u = wind_ref[0]
    wind_v = wind_ref[1]
    remaining = fuel_ref[...]
    heating = jnp.zeros_like(remaining)
    for substep in range(SUBSTEPS):
        xm1 = shift(level, -1, 0)
        xp1 = shift(level, 1, 0)
        ym1 = shift(level, -1, 1)
        yp1 = shift(level, 1, 1)
        back_x = level - xm1
        ahead_x = xp1 - level
        back_y = level - ym1
        ahead_y = yp1 - level
        upwind = jnp.sqrt(
            jnp.maximum(back_x, 0.0) ** 2
            + jnp.minimum(ahead_x, 0.0) ** 2
            + jnp.maximum(back_y, 0.0) ** 2
            + jnp.minimum(ahead_y, 0.0) ** 2
        )
        slope_x = (shift(level, -2, 0) - 8.0 * xm1 + 8.0 * xp1 - shift(level, 2, 0)) / 12.0
        slope_y = (shift(level, -2, 1) - 8.0 * ym1 + 8.0 * yp1 - shift(level, 2, 1)) / 12.0
        pushing = jnp.maximum(wind_u * slope_x + wind_v * slope_y, 0.0)
        moved = level - spread * (upwind + gain * pushing)
        burned = remaining / (1.0 + jnp.exp(moved[inner])) / burnout
        active = float(substep) < nsteps_in
        remaining = jnp.where(active, remaining - burned, remaining)
        heating = heating + jnp.where(active, yields * burned, 0.0)
        level = jnp.where(float(substep) < nsteps, moved, level)
    level_out[...] = level[inner]
    fuel_out[...] = remaining
    heat_rows = heating.reshape(rows // RF, RF, cols).sum(axis=1)
    lane_in = lax.broadcasted_iota(jnp.int32, (cols, cols // RF), 0) // RF
    lane_out = lax.broadcasted_iota(jnp.int32, (cols, cols // RF), 1)
    blocks = (lane_in == lane_out).astype(jnp.float32)
    heat_out[...] = jnp.dot(
        heat_rows, blocks, precision=lax.Precision.HIGHEST, preferred_element_type=jnp.float32
    ) / (RF * RF)


def fire_step(tables, ext, winds, fuel_left):
    rows, cols = fuel_left.shape
    vmem = pl.BlockSpec(memory_space=pltpu.VMEM)
    return pl.pallas_call(
        fire_kernel,
        out_shape=(
            jax.ShapeDtypeStruct((rows, cols), jnp.float32),
            jax.ShapeDtypeStruct((rows, cols), jnp.float32),
            jax.ShapeDtypeStruct((rows // RF, cols // RF), jnp.float32),
        ),
        in_specs=[pl.BlockSpec(memory_space=pltpu.SMEM), vmem, vmem, vmem],
        out_specs=(vmem, vmem, vmem),
    )(tables, ext, winds, fuel_left)


def atmos_kernel(p_ref, q_ref, lo_ref, hi_ref, y_ref, u_ref, v_ref, h_ref, o_ref, ext_ref):
    rows, cols = o_ref.shape[2], o_ref.shape[3]
    halo = lo_ref.shape[2]
    centre = q_ref[0]
    ext_ref[:, 0:halo, :] = lo_ref[0]
    ext_ref[:, halo : halo + rows, :] = centre
    ext_ref[:, halo + rows : 2 * halo + rows, :] = hi_ref[0]
    ends = y_ref[0]
    lane = lax.broadcasted_iota(jnp.int32, centre.shape, 2)

    def ax(dx):
        return ext_ref[:, halo + dx : halo + dx + rows, :]

    def ay(dy):
        if dy > 0:
            turn = cols - dy
            return jnp.where(lane >= turn, pltpu.roll(ends, turn, 2), pltpu.roll(centre, turn, 2))
        return jnp.where(lane < -dy, pltpu.roll(ends, -dy, 2), pltpu.roll(centre, -dy, 2))

    deriv_x = (
        ax(3) - 9.0 * ax(2) + 45.0 * ax(1) - 45.0 * ax(-1) + 9.0 * ax(-2) - ax(-3)
    ) / 60.0
    deriv_y = (
        ay(3) - 9.0 * ay(2) + 45.0 * ay(1) - 45.0 * ay(-1) + 9.0 * ay(-2) - ay(-3)
    ) / 60.0
    laplace = ax(1) + ax(-1) + ay(1) + ay(-1) - 4.0 * centre
    updated = centre - COURANT * (u_ref[0] * deriv_x + v_ref[0] * deriv_y) + DIFFUSE * laplace
    heat = h_ref[...]
    profile_heat = jnp.stack([heat * p_ref[k] for k in range(updated.shape[0])])
    o_ref[0] = jnp.where(pl.program_id(0) == 3, updated + profile_heat, updated)


def atmos_call(atmos, x_lo, x_hi, y_ends, heat_atm):
    fields, depth, rows, cols = atmos.shape
    halo = x_lo.shape[2]
    profile = jnp.exp(-4.0 * jnp.arange(depth).astype(jnp.float32) / depth)
    block = (1, depth, rows, cols)
    edge = (1, depth, halo, cols)
    return pl.pallas_call(
        atmos_kernel,
        grid=(fields,),
        out_shape=jax.ShapeDtypeStruct((fields, depth, rows, cols), jnp.float32),
        in_specs=[
            pl.BlockSpec(memory_space=pltpu.SMEM),
            pl.BlockSpec(block, lambda f: (f, 0, 0, 0)),
            pl.BlockSpec(edge, lambda f: (f, 0, 0, 0)),
            pl.BlockSpec(edge, lambda f: (f, 0, 0, 0)),
            pl.BlockSpec(block, lambda f: (f, 0, 0, 0)),
            pl.BlockSpec(block, lambda f: (0, 0, 0, 0)),
            pl.BlockSpec(block, lambda f: (1, 0, 0, 0)),
            pl.BlockSpec((rows, cols), lambda f: (0, 0)),
        ],
        out_specs=pl.BlockSpec(block, lambda f: (f, 0, 0, 0)),
        scratch_shapes=[pltpu.VMEM((depth, -(-(rows + 2 * halo) // 8) * 8, cols), jnp.float32)],
    )(profile, atmos, x_lo, x_hi, y_ends, atmos, atmos, heat_atm)


def fire_halo(level):
    return extended(level, (("gx", 0), ("gy", 1)), 2)


def shards(
    atmos,
    level_set,
    fuel_left,
    fuel_map,
    spread_rate,
    wind_factor,
    burn_time,
    heat_yield,
    burn_tiles,
    burn_count,
    substep_count,
):
    fire_rows, fire_cols = level_set.shape
    atmos_rows, atmos_cols = (atmos.shape[2], atmos.shape[3])
    count_x = lax.axis_size("gx")
    x_lo = lax.ppermute(atmos[:, :, -3:], "gx", [(i, i + 1) for i in range(count_x - 1)])
    x_hi = lax.ppermute(atmos[:, :, :3], "gx", [(i + 1, i) for i in range(count_x - 1)])
    count = lax.axis_size("gy")
    from_lo = lax.ppermute(atmos[..., -3:], "gy", [(i, i + 1) for i in range(count - 1)])
    from_hi = lax.ppermute(atmos[..., :3], "gy", [(i + 1, i) for i in range(count - 1)])
    room = jnp.zeros(atmos.shape[:3] + (atmos_cols - 6,), jnp.float32)
    y_ends = jnp.concatenate([from_hi, room, from_lo], axis=3)
    along_x = jnp.concatenate([x_lo[0:2, 0:1], atmos[0:2, 0:1], x_hi[0:2, 0:1]], axis=2)
    slots = burn_tiles.reshape(-1)
    listed = burn_count.reshape(())
    tiles_dev = substep_count.size
    slot_valid = jnp.arange(slots.shape[0]) < listed
    tile_on = jnp.any(
        (slots[:, None] == jnp.arange(tiles_dev)[None, :]) & slot_valid[:, None], axis=0
    )
    tile_on = tile_on.reshape(substep_count.shape)
    tiles_x, tiles_y = substep_count.shape
    halo = 2 * SUBSTEPS
    nsteps = jnp.where(tile_on, substep_count, 0).astype(jnp.float32)
    nsteps = jnp.broadcast_to(nsteps[:, None, :, None], (tiles_x, TILE, tiles_y, TILE)).reshape(
        fire_rows, fire_cols
    )
    stacked = jnp.stack([level_set, fuel_map.astype(jnp.float32), nsteps])
    stacked = extended(stacked, (("gx", 1),), halo)
    surf = along_x[:, 0]
    fire_count = stacked.shape[0]

    def with_surface(fire_part, surf_part):
        room = (
            (0, 0),
            (0, fire_part.shape[1] - surf_part.shape[1]),
            (0, fire_part.shape[2] - surf_part.shape[2]),
        )
        return jnp.concatenate([fire_part, jnp.pad(surf_part, room)], axis=0)

    got_lo = lax.ppermute(
        with_surface(stacked[..., -halo:], surf[..., -3:]),
        "gy",
        [(i, i + 1) for i in range(count - 1)],
    )
    got_hi = lax.ppermute(
        with_surface(stacked[..., :halo], surf[..., :3]),
        "gy",
        [(i + 1, i) for i in range(count - 1)],
    )
    srows = surf.shape[1]
    stacked = jnp.concatenate([got_lo[:fire_count], stacked, got_hi[:fire_count]], axis=2)
    surface = jnp.concatenate(
        [got_lo[fire_count:, :srows, :3], surf, got_hi[fire_count:, :srows, :3]], axis=2
    )
    room = jnp.zeros(stacked.shape[:2] + (HALO_Y - halo,), jnp.float32)
    stacked = jnp.concatenate([room, stacked, room], axis=2)
    winds = surface_winds(surface, fire_rows, fire_cols, halo, HALO_Y)
    tables = jnp.concatenate([spread_rate, wind_factor, burn_time, heat_yield]).astype(jnp.float32)
    level, remaining, heat_atm = fire_step(tables, stacked, winds, fuel_left)
    return (atmos_call(atmos, x_lo, x_hi, y_ends, heat_atm), level, remaining)


def solution(mesh):
    return jax.shard_map(
        shards,
        mesh=mesh,
        in_specs=(
            P(None, None, "gx", "gy"),
            P("gx", "gy"),
            P("gx", "gy"),
            P("gx", "gy"),
            P(),
            P(),
            P(),
            P(),
            P("gx", "gy", None),
            P("gx", "gy"),
            P("gx", "gy"),
        ),
        out_specs=(P(None, None, "gx", "gy"), P("gx", "gy"), P("gx", "gy")),
        check_vma=False,
    )
```

```python
import jax
import jax.numpy as jnp
from jax import lax
from jax.sharding import PartitionSpec as P
from jax.experimental import pallas as pl
from jax.experimental.pallas import tpu as pltpu

RF = 8
TILE = 64
SUBSTEPS = 8


COURANT = 0.2
DIFFUSE = 0.05


def extended(cells, sides, width):
    for axis, dim in sides:
        count = lax.axis_size(axis)
        ends = count - 1
        head = lax.slice_in_dim(cells, 0, width, axis=dim)
        tail = lax.slice_in_dim(cells, cells.shape[dim] - width, cells.shape[dim], axis=dim)
        cells = jnp.concatenate(
            [
                lax.ppermute(tail, axis, [(i, (i + 1) % count) for i in range(ends)]),
                cells,
                lax.ppermute(head, axis, [((i + 1) % count, i) for i in range(ends)]),
            ],
            axis=dim,
        )
    return cells


def advance(
    padded, level, remaining, heating, spread, gain, burnout, yields, wind_u, wind_v, active
):
    back_x = level - padded[..., 1:-3, 2:-2]
    ahead_x = padded[..., 3:-1, 2:-2] - level
    back_y = level - padded[..., 2:-2, 1:-3]
    ahead_y = padded[..., 2:-2, 3:-1] - level
    upwind = jnp.sqrt(
        jnp.maximum(back_x, 0.0) ** 2
        + jnp.minimum(ahead_x, 0.0) ** 2
        + jnp.maximum(back_y, 0.0) ** 2
        + jnp.minimum(ahead_y, 0.0) ** 2
    )
    slope_x = (
        padded[..., :-4, 2:-2]
        - 8.0 * padded[..., 1:-3, 2:-2]
        + 8.0 * padded[..., 3:-1, 2:-2]
        - padded[..., 4:, 2:-2]
    ) / 12.0
    slope_y = (
        padded[..., 2:-2, :-4]
        - 8.0 * padded[..., 2:-2, 1:-3]
        + 8.0 * padded[..., 2:-2, 3:-1]
        - padded[..., 2:-2, 4:]
    ) / 12.0
    pushing = jnp.maximum(wind_u * slope_x + wind_v * slope_y, 0.0)
    advanced = level - spread * (upwind + gain * pushing)
    burned = remaining / (1.0 + jnp.exp(advanced)) / burnout
    return (
        jnp.where(active, advanced, level),
        jnp.where(active, remaining - burned, remaining),
        heating + jnp.where(active, yields * burned, 0.0),
    )


def spread_level(padded, level, spread, gain, wind_u, wind_v):
    back_x = level - padded[..., 1:-3, 2:-2]
    ahead_x = padded[..., 3:-1, 2:-2] - level
    back_y = level - padded[..., 2:-2, 1:-3]
    ahead_y = padded[..., 2:-2, 3:-1] - level
    upwind = jnp.sqrt(
        jnp.maximum(back_x, 0.0) ** 2
        + jnp.minimum(ahead_x, 0.0) ** 2
        + jnp.maximum(back_y, 0.0) ** 2
        + jnp.minimum(ahead_y, 0.0) ** 2
    )
    slope_x = (
        padded[..., :-4, 2:-2]
        - 8.0 * padded[..., 1:-3, 2:-2]
        + 8.0 * padded[..., 3:-1, 2:-2]
        - padded[..., 4:, 2:-2]
    ) / 12.0
    slope_y = (
        padded[..., 2:-2, :-4]
        - 8.0 * padded[..., 2:-2, 1:-3]
        + 8.0 * padded[..., 2:-2, 3:-1]
        - padded[..., 2:-2, 4:]
    ) / 12.0
    pushing = jnp.maximum(wind_u * slope_x + wind_v * slope_y, 0.0)
    return level - spread * (upwind + gain * pushing)


def atmos_step(padded, heat_atm):
    width_x = padded.shape[2] - 6
    width_y = padded.shape[3] - 6

    def shifted(along_x, along_y):
        return padded[
            :, :, 3 + along_x : 3 + along_x + width_x, 3 + along_y : 3 + along_y + width_y
        ]

    centre = shifted(0, 0)
    deriv_x = (
        shifted(3, 0)
        - 9.0 * shifted(2, 0)
        + 45.0 * shifted(1, 0)
        - 45.0 * shifted(-1, 0)
        + 9.0 * shifted(-2, 0)
        - shifted(-3, 0)
    ) / 60.0
    deriv_y = (
        shifted(0, 3)
        - 9.0 * shifted(0, 2)
        + 45.0 * shifted(0, 1)
        - 45.0 * shifted(0, -1)
        + 9.0 * shifted(0, -2)
        - shifted(0, -3)
    ) / 60.0
    laplace = shifted(1, 0) + shifted(-1, 0) + shifted(0, 1) + shifted(0, -1) - 4.0 * centre
    updated = centre - COURANT * (centre[0:1] * deriv_x + centre[1:2] * deriv_y) + DIFFUSE * laplace
    depth = padded.shape[1]
    profile = jnp.exp(-4.0 * jnp.arange(depth).astype(jnp.float32) / depth)
    return updated.at[3].add(heat_atm[None, :, :] * profile[:, None, None])


def interp_table(count, ratio, extra):
    indices = jnp.arange(count + 2 * extra) - extra
    coarse = indices // ratio
    within = indices % ratio
    lower = jnp.where(within < ratio // 2, coarse, coarse + 1) + 2
    weight = (within.astype(jnp.float32) + 0.5) / ratio + jnp.where(within < ratio // 2, 0.5, -0.5)
    columns = jnp.arange(count // ratio + 6)
    return (1.0 - weight)[:, None] * (columns[None, :] == lower[:, None]) + weight[:, None] * (
        columns[None, :] == lower[:, None] + 1
    )


def surface_winds(surface, fire_rows, fire_cols, extra_x, extra_y):
    table_x = interp_table(fire_rows, RF, extra_x)
    table_y = interp_table(fire_cols, RF, extra_y)
    along = jnp.einsum("ia,kab->kib", table_x, surface, precision=lax.Precision.HIGHEST)
    return jnp.einsum("kib,jb->kij", along, table_y, precision=lax.Precision.HIGHEST)


HALO_Y = 128


def shift(a, d, axis):
    return pltpu.roll(a, (-d) % a.shape[axis], axis)


def lookup(tab_ref, cat, row, default):
    ncat = tab_ref.shape[0] // 4
    out = jnp.full(cat.shape, default, jnp.float32)
    for category in range(ncat):
        out = jnp.where(cat == float(category), tab_ref[row * ncat + category], out)
    return out


def fire_kernel(
    tab_ref, mid_ref, xlo_ref, xhi_ref, ylo_ref, yhi_ref, wind_ref, fuel_ref,
    level_out, fuel_out, heat_out, ext_ref,
):
    rows, cols = fuel_ref.shape
    edge_x = xlo_ref.shape[1]
    edge_y = ylo_ref.shape[2]
    ext_ref[:, 0:edge_x, edge_y : edge_y + cols] = xlo_ref[...]
    ext_ref[:, edge_x : edge_x + rows, edge_y : edge_y + cols] = mid_ref[...]
    ext_ref[:, edge_x + rows :, edge_y : edge_y + cols] = xhi_ref[...]
    ext_ref[:, :, 0:edge_y] = ylo_ref[...]
    ext_ref[:, :, edge_y + cols :] = yhi_ref[...]
    hx = (ext_ref.shape[1] - rows) // 2
    hy = (ext_ref.shape[2] - cols) // 2
    inner = (slice(hx, hx + rows), slice(hy, hy + cols))
    level = ext_ref[0]
    cat = ext_ref[1]
    nsteps = ext_ref[2]
    spread = lookup(tab_ref, cat, 0, 0.0)
    gain = lookup(tab_ref, cat, 1, 0.0)
    cat_in = cat[inner]
    burnout = lookup(tab_ref, cat_in, 2, 1.0)
    yields = lookup(tab_ref, cat_in, 3, 0.0)
    nsteps_in = nsteps[inner]
    wind_u = wind_ref[0]
    wind_v = wind_ref[1]
    remaining = fuel_ref[...]
    heating = jnp.zeros_like(remaining)
    for substep in range(SUBSTEPS):
        xm1 = shift(level, -1, 0)
        xp1 = shift(level, 1, 0)
        ym1 = shift(level, -1, 1)
        yp1 = shift(level, 1, 1)
        back_x = level - xm1
        ahead_x = xp1 - level
        back_y = level - ym1
        ahead_y = yp1 - level
        upwind = jnp.sqrt(
            jnp.maximum(back_x, 0.0) ** 2
            + jnp.minimum(ahead_x, 0.0) ** 2
            + jnp.maximum(back_y, 0.0) ** 2
            + jnp.minimum(ahead_y, 0.0) ** 2
        )
        slope_x = (shift(level, -2, 0) - 8.0 * xm1 + 8.0 * xp1 - shift(level, 2, 0)) / 12.0
        slope_y = (shift(level, -2, 1) - 8.0 * ym1 + 8.0 * yp1 - shift(level, 2, 1)) / 12.0
        pushing = jnp.maximum(wind_u * slope_x + wind_v * slope_y, 0.0)
        moved = level - spread * (upwind + gain * pushing)
        burned = remaining / (1.0 + jnp.exp(moved[inner])) / burnout
        active = float(substep) < nsteps_in
        remaining = jnp.where(active, remaining - burned, remaining)
        heating = heating + jnp.where(active, yields * burned, 0.0)
        level = jnp.where(float(substep) < nsteps, moved, level)
    level_out[...] = level[inner]
    fuel_out[...] = remaining
    heat_rows = heating.reshape(rows // RF, RF, cols).sum(axis=1)
    lane_in = lax.broadcasted_iota(jnp.int32, (cols, cols // RF), 0) // RF
    lane_out = lax.broadcasted_iota(jnp.int32, (cols, cols // RF), 1)
    blocks = (lane_in == lane_out).astype(jnp.float32)
    heat_out[...] = jnp.dot(
        heat_rows, blocks, precision=lax.Precision.HIGHEST, preferred_element_type=jnp.float32
    ) / (RF * RF)


def fire_step(tables, mid, x_lo, x_hi, y_lo, y_hi, winds, fuel_left):
    rows, cols = fuel_left.shape
    vmem = pl.BlockSpec(memory_space=pltpu.VMEM)
    return pl.pallas_call(
        fire_kernel,
        out_shape=(
            jax.ShapeDtypeStruct((rows, cols), jnp.float32),
            jax.ShapeDtypeStruct((rows, cols), jnp.float32),
            jax.ShapeDtypeStruct((rows // RF, cols // RF), jnp.float32),
        ),
        in_specs=[pl.BlockSpec(memory_space=pltpu.SMEM)] + [vmem] * 7,
        scratch_shapes=[pltpu.VMEM(mid.shape[:1] + winds.shape[1:], jnp.float32)],
        out_specs=(vmem, vmem, vmem),
    )(tables, mid, x_lo, x_hi, y_lo, y_hi, winds, fuel_left)


def atmos_kernel(p_ref, q_ref, lo_ref, hi_ref, y_ref, u_ref, v_ref, h_ref, o_ref, ext_ref):
    rows, cols = o_ref.shape[2], o_ref.shape[3]
    halo = lo_ref.shape[2]
    centre = q_ref[0]
    ext_ref[:, 0:halo, :] = lo_ref[0]
    ext_ref[:, halo : halo + rows, :] = centre
    ext_ref[:, halo + rows : 2 * halo + rows, :] = hi_ref[0]
    ends = y_ref[0]
    lane = lax.broadcasted_iota(jnp.int32, centre.shape, 2)

    def ax(dx):
        return ext_ref[:, halo + dx : halo + dx + rows, :]

    def ay(dy):
        if dy > 0:
            turn = cols - dy
            return jnp.where(lane >= turn, pltpu.roll(ends, turn, 2), pltpu.roll(centre, turn, 2))
        return jnp.where(lane < -dy, pltpu.roll(ends, -dy, 2), pltpu.roll(centre, -dy, 2))

    deriv_x = (
        ax(3) - 9.0 * ax(2) + 45.0 * ax(1) - 45.0 * ax(-1) + 9.0 * ax(-2) - ax(-3)
    ) / 60.0
    deriv_y = (
        ay(3) - 9.0 * ay(2) + 45.0 * ay(1) - 45.0 * ay(-1) + 9.0 * ay(-2) - ay(-3)
    ) / 60.0
    laplace = ax(1) + ax(-1) + ay(1) + ay(-1) - 4.0 * centre
    updated = centre - COURANT * (u_ref[0] * deriv_x + v_ref[0] * deriv_y) + DIFFUSE * laplace
    heat = h_ref[...]
    profile_heat = jnp.stack([heat * p_ref[k] for k in range(updated.shape[0])])
    o_ref[0] = jnp.where(pl.program_id(0) == 3, updated + profile_heat, updated)


def atmos_call(atmos, x_lo, x_hi, y_ends, heat_atm):
    fields, depth, rows, cols = atmos.shape
    halo = x_lo.shape[2]
    profile = jnp.exp(-4.0 * jnp.arange(depth).astype(jnp.float32) / depth)
    block = (1, depth, rows, cols)
    edge = (1, depth, halo, cols)
    return pl.pallas_call(
        atmos_kernel,
        grid=(fields,),
        out_shape=jax.ShapeDtypeStruct((fields, depth, rows, cols), jnp.float32),
        in_specs=[
            pl.BlockSpec(memory_space=pltpu.SMEM),
            pl.BlockSpec(block, lambda f: (f, 0, 0, 0)),
            pl.BlockSpec(edge, lambda f: (f, 0, 0, 0)),
            pl.BlockSpec(edge, lambda f: (f, 0, 0, 0)),
            pl.BlockSpec(block, lambda f: (f, 0, 0, 0)),
            pl.BlockSpec(block, lambda f: (0, 0, 0, 0)),
            pl.BlockSpec(block, lambda f: (1, 0, 0, 0)),
            pl.BlockSpec((rows, cols), lambda f: (0, 0)),
        ],
        out_specs=pl.BlockSpec(block, lambda f: (f, 0, 0, 0)),
        scratch_shapes=[pltpu.VMEM((depth, -(-(rows + 2 * halo) // 8) * 8, cols), jnp.float32)],
    )(profile, atmos, x_lo, x_hi, y_ends, atmos, atmos, heat_atm)


def fire_halo(level):
    return extended(level, (("gx", 0), ("gy", 1)), 2)


def shards(
    atmos,
    level_set,
    fuel_left,
    fuel_map,
    spread_rate,
    wind_factor,
    burn_time,
    heat_yield,
    burn_tiles,
    burn_count,
    substep_count,
):
    fire_rows, fire_cols = level_set.shape
    atmos_rows, atmos_cols = (atmos.shape[2], atmos.shape[3])
    count_x = lax.axis_size("gx")
    x_lo = lax.ppermute(atmos[:, :, -3:], "gx", [(i, i + 1) for i in range(count_x - 1)])
    x_hi = lax.ppermute(atmos[:, :, :3], "gx", [(i + 1, i) for i in range(count_x - 1)])
    count = lax.axis_size("gy")
    from_lo = lax.ppermute(atmos[..., -3:], "gy", [(i, i + 1) for i in range(count - 1)])
    from_hi = lax.ppermute(atmos[..., :3], "gy", [(i + 1, i) for i in range(count - 1)])
    room = jnp.zeros(atmos.shape[:3] + (atmos_cols - 6,), jnp.float32)
    y_ends = jnp.concatenate([from_hi, room, from_lo], axis=3)
    along_x = jnp.concatenate([x_lo[0:2, 0:1], atmos[0:2, 0:1], x_hi[0:2, 0:1]], axis=2)
    surface = extended(along_x[:, 0], (("gy", 2),), 3)
    slots = burn_tiles.reshape(-1)
    listed = burn_count.reshape(())
    tiles_dev = substep_count.size
    slot_valid = jnp.arange(slots.shape[0]) < listed
    tile_on = jnp.any(
        (slots[:, None] == jnp.arange(tiles_dev)[None, :]) & slot_valid[:, None], axis=0
    )
    tile_on = tile_on.reshape(substep_count.shape)
    tiles_x, tiles_y = substep_count.shape
    halo = 2 * SUBSTEPS
    nsteps = jnp.where(tile_on, substep_count, 0).astype(jnp.float32)
    nsteps = jnp.broadcast_to(nsteps[:, None, :, None], (tiles_x, TILE, tiles_y, TILE)).reshape(
        fire_rows, fire_cols
    )
    stacked = jnp.stack([level_set, fuel_map.astype(jnp.float32), nsteps])
    f_lo = lax.ppermute(stacked[:, -halo:], "gx", [(i, i + 1) for i in range(count_x - 1)])
    f_hi = lax.ppermute(stacked[:, :halo], "gx", [(i + 1, i) for i in range(count_x - 1)])

    def column(lo, hi):
        return jnp.concatenate([f_lo[..., lo:hi], stacked[..., lo:hi], f_hi[..., lo:hi]], axis=1)

    y_lo = lax.ppermute(
        column(fire_cols - halo, fire_cols), "gy", [(i, i + 1) for i in range(count - 1)]
    )
    y_hi = lax.ppermute(column(0, halo), "gy", [(i + 1, i) for i in range(count - 1)])
    y_lo = jnp.pad(y_lo, ((0, 0), (0, 0), (HALO_Y - halo, 0)))
    y_hi = jnp.pad(y_hi, ((0, 0), (0, 0), (0, HALO_Y - halo)))
    winds = surface_winds(surface, fire_rows, fire_cols, halo, HALO_Y)
    tables = jnp.concatenate([spread_rate, wind_factor, burn_time, heat_yield]).astype(jnp.float32)
    level, remaining, heat_atm = fire_step(tables, stacked, f_lo, f_hi, y_lo, y_hi, winds, fuel_left)
    return (atmos_call(atmos, x_lo, x_hi, y_ends, heat_atm), level, remaining)


def solution(mesh):
    return jax.shard_map(
        shards,
        mesh=mesh,
        in_specs=(
            P(None, None, "gx", "gy"),
            P("gx", "gy"),
            P("gx", "gy"),
            P("gx", "gy"),
            P(),
            P(),
            P(),
            P(),
            P("gx", "gy", None),
            P("gx", "gy"),
            P("gx", "gy"),
        ),
        out_specs=(P(None, None, "gx", "gy"), P("gx", "gy"), P("gx", "gy")),
        check_vma=False,
    )
```

```python
import jax
import jax.numpy as jnp
from jax import lax
from jax.sharding import PartitionSpec as P
from jax.experimental import pallas as pl
from jax.experimental.pallas import tpu as pltpu

RF = 8
TILE = 64
SUBSTEPS = 8


COURANT = 0.2
DIFFUSE = 0.05


def extended(cells, sides, width):
    for axis, dim in sides:
        count = lax.axis_size(axis)
        ends = count - 1
        head = lax.slice_in_dim(cells, 0, width, axis=dim)
        tail = lax.slice_in_dim(cells, cells.shape[dim] - width, cells.shape[dim], axis=dim)
        cells = jnp.concatenate(
            [
                lax.ppermute(tail, axis, [(i, (i + 1) % count) for i in range(ends)]),
                cells,
                lax.ppermute(head, axis, [((i + 1) % count, i) for i in range(ends)]),
            ],
            axis=dim,
        )
    return cells


def advance(
    padded, level, remaining, heating, spread, gain, burnout, yields, wind_u, wind_v, active
):
    back_x = level - padded[..., 1:-3, 2:-2]
    ahead_x = padded[..., 3:-1, 2:-2] - level
    back_y = level - padded[..., 2:-2, 1:-3]
    ahead_y = padded[..., 2:-2, 3:-1] - level
    upwind = jnp.sqrt(
        jnp.maximum(back_x, 0.0) ** 2
        + jnp.minimum(ahead_x, 0.0) ** 2
        + jnp.maximum(back_y, 0.0) ** 2
        + jnp.minimum(ahead_y, 0.0) ** 2
    )
    slope_x = (
        padded[..., :-4, 2:-2]
        - 8.0 * padded[..., 1:-3, 2:-2]
        + 8.0 * padded[..., 3:-1, 2:-2]
        - padded[..., 4:, 2:-2]
    ) / 12.0
    slope_y = (
        padded[..., 2:-2, :-4]
        - 8.0 * padded[..., 2:-2, 1:-3]
        + 8.0 * padded[..., 2:-2, 3:-1]
        - padded[..., 2:-2, 4:]
    ) / 12.0
    pushing = jnp.maximum(wind_u * slope_x + wind_v * slope_y, 0.0)
    advanced = level - spread * (upwind + gain * pushing)
    burned = remaining / (1.0 + jnp.exp(advanced)) / burnout
    return (
        jnp.where(active, advanced, level),
        jnp.where(active, remaining - burned, remaining),
        heating + jnp.where(active, yields * burned, 0.0),
    )


def spread_level(padded, level, spread, gain, wind_u, wind_v):
    back_x = level - padded[..., 1:-3, 2:-2]
    ahead_x = padded[..., 3:-1, 2:-2] - level
    back_y = level - padded[..., 2:-2, 1:-3]
    ahead_y = padded[..., 2:-2, 3:-1] - level
    upwind = jnp.sqrt(
        jnp.maximum(back_x, 0.0) ** 2
        + jnp.minimum(ahead_x, 0.0) ** 2
        + jnp.maximum(back_y, 0.0) ** 2
        + jnp.minimum(ahead_y, 0.0) ** 2
    )
    slope_x = (
        padded[..., :-4, 2:-2]
        - 8.0 * padded[..., 1:-3, 2:-2]
        + 8.0 * padded[..., 3:-1, 2:-2]
        - padded[..., 4:, 2:-2]
    ) / 12.0
    slope_y = (
        padded[..., 2:-2, :-4]
        - 8.0 * padded[..., 2:-2, 1:-3]
        + 8.0 * padded[..., 2:-2, 3:-1]
        - padded[..., 2:-2, 4:]
    ) / 12.0
    pushing = jnp.maximum(wind_u * slope_x + wind_v * slope_y, 0.0)
    return level - spread * (upwind + gain * pushing)


def atmos_step(padded, heat_atm):
    width_x = padded.shape[2] - 6
    width_y = padded.shape[3] - 6

    def shifted(along_x, along_y):
        return padded[
            :, :, 3 + along_x : 3 + along_x + width_x, 3 + along_y : 3 + along_y + width_y
        ]

    centre = shifted(0, 0)
    deriv_x = (
        shifted(3, 0)
        - 9.0 * shifted(2, 0)
        + 45.0 * shifted(1, 0)
        - 45.0 * shifted(-1, 0)
        + 9.0 * shifted(-2, 0)
        - shifted(-3, 0)
    ) / 60.0
    deriv_y = (
        shifted(0, 3)
        - 9.0 * shifted(0, 2)
        + 45.0 * shifted(0, 1)
        - 45.0 * shifted(0, -1)
        + 9.0 * shifted(0, -2)
        - shifted(0, -3)
    ) / 60.0
    laplace = shifted(1, 0) + shifted(-1, 0) + shifted(0, 1) + shifted(0, -1) - 4.0 * centre
    updated = centre - COURANT * (centre[0:1] * deriv_x + centre[1:2] * deriv_y) + DIFFUSE * laplace
    depth = padded.shape[1]
    profile = jnp.exp(-4.0 * jnp.arange(depth).astype(jnp.float32) / depth)
    return updated.at[3].add(heat_atm[None, :, :] * profile[:, None, None])


def interp_table(count, ratio, extra):
    indices = jnp.arange(count + 2 * extra) - extra
    coarse = indices // ratio
    within = indices % ratio
    lower = jnp.where(within < ratio // 2, coarse, coarse + 1) + 2
    weight = (within.astype(jnp.float32) + 0.5) / ratio + jnp.where(within < ratio // 2, 0.5, -0.5)
    columns = jnp.arange(count // ratio + 6)
    return (1.0 - weight)[:, None] * (columns[None, :] == lower[:, None]) + weight[:, None] * (
        columns[None, :] == lower[:, None] + 1
    )


def surface_winds(surface, fire_rows, fire_cols, extra_x, extra_y):
    table_x = interp_table(fire_rows, RF, extra_x)
    table_y = interp_table(fire_cols, RF, extra_y)
    along = jnp.einsum("ia,kab->kib", table_x, surface, precision=lax.Precision.HIGHEST)
    return jnp.einsum("kib,jb->kij", along, table_y, precision=lax.Precision.HIGHEST)


HALO_Y = 64


def shift(a, d, axis):
    return pltpu.roll(a, (-d) % a.shape[axis], axis)


def lookup(tab_ref, cat, row, default):
    ncat = tab_ref.shape[0] // 4
    out = jnp.full(cat.shape, default, jnp.float32)
    for category in range(ncat):
        out = jnp.where(cat == float(category), tab_ref[row * ncat + category], out)
    return out


def fire_kernel(tab_ref, ext_ref, wind_ref, fuel_ref, level_out, fuel_out, heat_out):
    rows, cols = fuel_ref.shape
    hx = (ext_ref.shape[1] - rows) // 2
    hy = (ext_ref.shape[2] - cols) // 2
    width = ext_ref.shape[2]

    def interior(a):
        return pltpu.roll(a[hx : hx + rows], (width - hy) % width, 1)[:, :cols]
    level = ext_ref[0]
    cat = ext_ref[1]
    nsteps = ext_ref[2]
    spread = lookup(tab_ref, cat, 0, 0.0)
    gain = lookup(tab_ref, cat, 1, 0.0)
    cat_in = interior(cat)
    burnout = lookup(tab_ref, cat_in, 2, 1.0)
    yields = lookup(tab_ref, cat_in, 3, 0.0)
    nsteps_in = interior(nsteps)
    wind_u = wind_ref[0]
    wind_v = wind_ref[1]
    remaining = fuel_ref[...]
    heating = jnp.zeros_like(remaining)
    for substep in range(SUBSTEPS):
        xm1 = shift(level, -1, 0)
        xp1 = shift(level, 1, 0)
        ym1 = shift(level, -1, 1)
        yp1 = shift(level, 1, 1)
        back_x = level - xm1
        ahead_x = xp1 - level
        back_y = level - ym1
        ahead_y = yp1 - level
        upwind = jnp.sqrt(
            jnp.maximum(back_x, 0.0) ** 2
            + jnp.minimum(ahead_x, 0.0) ** 2
            + jnp.maximum(back_y, 0.0) ** 2
            + jnp.minimum(ahead_y, 0.0) ** 2
        )
        slope_x = (shift(level, -2, 0) - 8.0 * xm1 + 8.0 * xp1 - shift(level, 2, 0)) / 12.0
        slope_y = (shift(level, -2, 1) - 8.0 * ym1 + 8.0 * yp1 - shift(level, 2, 1)) / 12.0
        pushing = jnp.maximum(wind_u * slope_x + wind_v * slope_y, 0.0)
        moved = level - spread * (upwind + gain * pushing)
        burned = remaining / (1.0 + jnp.exp(interior(moved))) / burnout
        active = float(substep) < nsteps_in
        remaining = jnp.where(active, remaining - burned, remaining)
        heating = heating + jnp.where(active, yields * burned, 0.0)
        level = jnp.where(float(substep) < nsteps, moved, level)
    level_out[...] = interior(level)
    fuel_out[...] = remaining
    heat_rows = heating.reshape(rows // RF, RF, cols).sum(axis=1)
    lane_in = lax.broadcasted_iota(jnp.int32, (cols, cols // RF), 0) // RF
    lane_out = lax.broadcasted_iota(jnp.int32, (cols, cols // RF), 1)
    blocks = (lane_in == lane_out).astype(jnp.float32)
    heat_out[...] = jnp.dot(
        heat_rows, blocks, precision=lax.Precision.HIGHEST, preferred_element_type=jnp.float32
    ) / (RF * RF)


def fire_step(tables, ext, winds, fuel_left):
    rows, cols = fuel_left.shape
    vmem = pl.BlockSpec(memory_space=pltpu.VMEM)
    return pl.pallas_call(
        fire_kernel,
        out_shape=(
            jax.ShapeDtypeStruct((rows, cols), jnp.float32),
            jax.ShapeDtypeStruct((rows, cols), jnp.float32),
            jax.ShapeDtypeStruct((rows // RF, cols // RF), jnp.float32),
        ),
        in_specs=[pl.BlockSpec(memory_space=pltpu.SMEM), vmem, vmem, vmem],
        out_specs=(vmem, vmem, vmem),
    )(tables, ext, winds, fuel_left)


def atmos_kernel(p_ref, q_ref, lo_ref, hi_ref, y_ref, u_ref, v_ref, h_ref, o_ref, ext_ref):
    rows, cols = o_ref.shape[2], o_ref.shape[3]
    halo = lo_ref.shape[2]
    centre = q_ref[0]
    ext_ref[:, 0:halo, :] = lo_ref[0]
    ext_ref[:, halo : halo + rows, :] = centre
    ext_ref[:, halo + rows : 2 * halo + rows, :] = hi_ref[0]
    ends = y_ref[0]
    lane = lax.broadcasted_iota(jnp.int32, centre.shape, 2)

    def ax(dx):
        return ext_ref[:, halo + dx : halo + dx + rows, :]

    def ay(dy):
        if dy > 0:
            turn = cols - dy
            return jnp.where(lane >= turn, pltpu.roll(ends, turn, 2), pltpu.roll(centre, turn, 2))
        return jnp.where(lane < -dy, pltpu.roll(ends, -dy, 2), pltpu.roll(centre, -dy, 2))

    deriv_x = (
        ax(3) - 9.0 * ax(2) + 45.0 * ax(1) - 45.0 * ax(-1) + 9.0 * ax(-2) - ax(-3)
    ) / 60.0
    deriv_y = (
        ay(3) - 9.0 * ay(2) + 45.0 * ay(1) - 45.0 * ay(-1) + 9.0 * ay(-2) - ay(-3)
    ) / 60.0
    laplace = ax(1) + ax(-1) + ay(1) + ay(-1) - 4.0 * centre
    updated = centre - COURANT * (u_ref[0] * deriv_x + v_ref[0] * deriv_y) + DIFFUSE * laplace
    heat = h_ref[...]
    profile_heat = jnp.stack([heat * p_ref[k] for k in range(updated.shape[0])])
    o_ref[0] = jnp.where(pl.program_id(0) == 3, updated + profile_heat, updated)


def atmos_call(atmos, x_lo, x_hi, y_ends, heat_atm):
    fields, depth, rows, cols = atmos.shape
    halo = x_lo.shape[2]
    profile = jnp.exp(-4.0 * jnp.arange(depth).astype(jnp.float32) / depth)
    block = (1, depth, rows, cols)
    edge = (1, depth, halo, cols)
    return pl.pallas_call(
        atmos_kernel,
        grid=(fields,),
        out_shape=jax.ShapeDtypeStruct((fields, depth, rows, cols), jnp.float32),
        in_specs=[
            pl.BlockSpec(memory_space=pltpu.SMEM),
            pl.BlockSpec(block, lambda f: (f, 0, 0, 0)),
            pl.BlockSpec(edge, lambda f: (f, 0, 0, 0)),
            pl.BlockSpec(edge, lambda f: (f, 0, 0, 0)),
            pl.BlockSpec(block, lambda f: (f, 0, 0, 0)),
            pl.BlockSpec(block, lambda f: (0, 0, 0, 0)),
            pl.BlockSpec(block, lambda f: (1, 0, 0, 0)),
            pl.BlockSpec((rows, cols), lambda f: (0, 0)),
        ],
        out_specs=pl.BlockSpec(block, lambda f: (f, 0, 0, 0)),
        scratch_shapes=[pltpu.VMEM((depth, -(-(rows + 2 * halo) // 8) * 8, cols), jnp.float32)],
    )(profile, atmos, x_lo, x_hi, y_ends, atmos, atmos, heat_atm)


def fire_halo(level):
    return extended(level, (("gx", 0), ("gy", 1)), 2)


def shards(
    atmos,
    level_set,
    fuel_left,
    fuel_map,
    spread_rate,
    wind_factor,
    burn_time,
    heat_yield,
    burn_tiles,
    burn_count,
    substep_count,
):
    fire_rows, fire_cols = level_set.shape
    atmos_rows, atmos_cols = (atmos.shape[2], atmos.shape[3])
    count_x = lax.axis_size("gx")
    x_lo = lax.ppermute(atmos[:, :, -3:], "gx", [(i, i + 1) for i in range(count_x - 1)])
    x_hi = lax.ppermute(atmos[:, :, :3], "gx", [(i + 1, i) for i in range(count_x - 1)])
    count = lax.axis_size("gy")
    from_lo = lax.ppermute(atmos[..., -3:], "gy", [(i, i + 1) for i in range(count - 1)])
    from_hi = lax.ppermute(atmos[..., :3], "gy", [(i + 1, i) for i in range(count - 1)])
    room = jnp.zeros(atmos.shape[:3] + (atmos_cols - 6,), jnp.float32)
    y_ends = jnp.concatenate([from_hi, room, from_lo], axis=3)
    along_x = jnp.concatenate([x_lo[0:2, 0:1], atmos[0:2, 0:1], x_hi[0:2, 0:1]], axis=2)
    surface = extended(along_x[:, 0], (("gy", 2),), 3)
    slots = burn_tiles.reshape(-1)
    listed = burn_count.reshape(())
    tiles_dev = substep_count.size
    slot_valid = jnp.arange(slots.shape[0]) < listed
    tile_on = jnp.any(
        (slots[:, None] == jnp.arange(tiles_dev)[None, :]) & slot_valid[:, None], axis=0
    )
    tile_on = tile_on.reshape(substep_count.shape)
    tiles_x, tiles_y = substep_count.shape
    halo = 2 * SUBSTEPS
    nsteps = jnp.where(tile_on, substep_count, 0).astype(jnp.float32)
    nsteps = jnp.broadcast_to(nsteps[:, None, :, None], (tiles_x, TILE, tiles_y, TILE)).reshape(
        fire_rows, fire_cols
    )
    stacked = jnp.stack([level_set, fuel_map.astype(jnp.float32), nsteps])
    stacked = extended(stacked, (("gx", 1), ("gy", 2)), halo)
    room = jnp.zeros(stacked.shape[:2] + (HALO_Y - halo,), jnp.float32)
    stacked = jnp.concatenate([room, stacked, room], axis=2)
    winds = surface_winds(surface, fire_rows, fire_cols, halo, HALO_Y)
    tables = jnp.concatenate([spread_rate, wind_factor, burn_time, heat_yield]).astype(jnp.float32)
    level, remaining, heat_atm = fire_step(tables, stacked, winds, fuel_left)
    return (atmos_call(atmos, x_lo, x_hi, y_ends, heat_atm), level, remaining)


def solution(mesh):
    return jax.shard_map(
        shards,
        mesh=mesh,
        in_specs=(
            P(None, None, "gx", "gy"),
            P("gx", "gy"),
            P("gx", "gy"),
            P("gx", "gy"),
            P(),
            P(),
            P(),
            P(),
            P("gx", "gy", None),
            P("gx", "gy"),
            P("gx", "gy"),
        ),
        out_specs=(P(None, None, "gx", "gy"), P("gx", "gy"), P("gx", "gy")),
        check_vma=False,
    )
```

```python
import jax
import jax.numpy as jnp
from jax import lax
from jax.sharding import PartitionSpec as P
from jax.experimental import pallas as pl
from jax.experimental.pallas import tpu as pltpu

RF = 8
TILE = 64
SUBSTEPS = 8


COURANT = 0.2
DIFFUSE = 0.05


def extended(cells, sides, width):
    for axis, dim in sides:
        count = lax.axis_size(axis)
        ends = count - 1
        head = lax.slice_in_dim(cells, 0, width, axis=dim)
        tail = lax.slice_in_dim(cells, cells.shape[dim] - width, cells.shape[dim], axis=dim)
        cells = jnp.concatenate(
            [
                lax.ppermute(tail, axis, [(i, (i + 1) % count) for i in range(ends)]),
                cells,
                lax.ppermute(head, axis, [((i + 1) % count, i) for i in range(ends)]),
            ],
            axis=dim,
        )
    return cells


def advance(
    padded, level, remaining, heating, spread, gain, burnout, yields, wind_u, wind_v, active
):
    back_x = level - padded[..., 1:-3, 2:-2]
    ahead_x = padded[..., 3:-1, 2:-2] - level
    back_y = level - padded[..., 2:-2, 1:-3]
    ahead_y = padded[..., 2:-2, 3:-1] - level
    upwind = jnp.sqrt(
        jnp.maximum(back_x, 0.0) ** 2
        + jnp.minimum(ahead_x, 0.0) ** 2
        + jnp.maximum(back_y, 0.0) ** 2
        + jnp.minimum(ahead_y, 0.0) ** 2
    )
    slope_x = (
        padded[..., :-4, 2:-2]
        - 8.0 * padded[..., 1:-3, 2:-2]
        + 8.0 * padded[..., 3:-1, 2:-2]
        - padded[..., 4:, 2:-2]
    ) / 12.0
    slope_y = (
        padded[..., 2:-2, :-4]
        - 8.0 * padded[..., 2:-2, 1:-3]
        + 8.0 * padded[..., 2:-2, 3:-1]
        - padded[..., 2:-2, 4:]
    ) / 12.0
    pushing = jnp.maximum(wind_u * slope_x + wind_v * slope_y, 0.0)
    advanced = level - spread * (upwind + gain * pushing)
    burned = remaining / (1.0 + jnp.exp(advanced)) / burnout
    return (
        jnp.where(active, advanced, level),
        jnp.where(active, remaining - burned, remaining),
        heating + jnp.where(active, yields * burned, 0.0),
    )


def spread_level(padded, level, spread, gain, wind_u, wind_v):
    back_x = level - padded[..., 1:-3, 2:-2]
    ahead_x = padded[..., 3:-1, 2:-2] - level
    back_y = level - padded[..., 2:-2, 1:-3]
    ahead_y = padded[..., 2:-2, 3:-1] - level
    upwind = jnp.sqrt(
        jnp.maximum(back_x, 0.0) ** 2
        + jnp.minimum(ahead_x, 0.0) ** 2
        + jnp.maximum(back_y, 0.0) ** 2
        + jnp.minimum(ahead_y, 0.0) ** 2
    )
    slope_x = (
        padded[..., :-4, 2:-2]
        - 8.0 * padded[..., 1:-3, 2:-2]
        + 8.0 * padded[..., 3:-1, 2:-2]
        - padded[..., 4:, 2:-2]
    ) / 12.0
    slope_y = (
        padded[..., 2:-2, :-4]
        - 8.0 * padded[..., 2:-2, 1:-3]
        + 8.0 * padded[..., 2:-2, 3:-1]
        - padded[..., 2:-2, 4:]
    ) / 12.0
    pushing = jnp.maximum(wind_u * slope_x + wind_v * slope_y, 0.0)
    return level - spread * (upwind + gain * pushing)


def atmos_step(padded, heat_atm):
    width_x = padded.shape[2] - 6
    width_y = padded.shape[3] - 6

    def shifted(along_x, along_y):
        return padded[
            :, :, 3 + along_x : 3 + along_x + width_x, 3 + along_y : 3 + along_y + width_y
        ]

    centre = shifted(0, 0)
    deriv_x = (
        shifted(3, 0)
        - 9.0 * shifted(2, 0)
        + 45.0 * shifted(1, 0)
        - 45.0 * shifted(-1, 0)
        + 9.0 * shifted(-2, 0)
        - shifted(-3, 0)
    ) / 60.0
    deriv_y = (
        shifted(0, 3)
        - 9.0 * shifted(0, 2)
        + 45.0 * shifted(0, 1)
        - 45.0 * shifted(0, -1)
        + 9.0 * shifted(0, -2)
        - shifted(0, -3)
    ) / 60.0
    laplace = shifted(1, 0) + shifted(-1, 0) + shifted(0, 1) + shifted(0, -1) - 4.0 * centre
    updated = centre - COURANT * (centre[0:1] * deriv_x + centre[1:2] * deriv_y) + DIFFUSE * laplace
    depth = padded.shape[1]
    profile = jnp.exp(-4.0 * jnp.arange(depth).astype(jnp.float32) / depth)
    return updated.at[3].add(heat_atm[None, :, :] * profile[:, None, None])


def interp_table(count, ratio, extra):
    indices = jnp.arange(count + 2 * extra) - extra
    coarse = indices // ratio
    within = indices % ratio
    lower = jnp.where(within < ratio // 2, coarse, coarse + 1) + 2
    weight = (within.astype(jnp.float32) + 0.5) / ratio + jnp.where(within < ratio // 2, 0.5, -0.5)
    columns = jnp.arange(count // ratio + 6)
    return (1.0 - weight)[:, None] * (columns[None, :] == lower[:, None]) + weight[:, None] * (
        columns[None, :] == lower[:, None] + 1
    )


def surface_winds(surface, fire_rows, fire_cols, extra_x, extra_y):
    table_x = interp_table(fire_rows, RF, extra_x)
    table_y = interp_table(fire_cols, RF, extra_y)
    along = jnp.einsum("ia,kab->kib", table_x, surface, precision=lax.Precision.HIGHEST)
    return jnp.einsum("kib,jb->kij", along, table_y, precision=lax.Precision.HIGHEST)


HALO_Y = 64


def shift(a, d, axis):
    return pltpu.roll(a, (-d) % a.shape[axis], axis)


def lookup(tab_ref, cat, row, default):
    ncat = tab_ref.shape[0] // 4
    out = jnp.full(cat.shape, default, jnp.float32)
    for category in range(ncat):
        out = jnp.where(cat == float(category), tab_ref[row * ncat + category], out)
    return out


def fire_kernel(tab_ref, ext_ref, wind_ref, fuel_ref, level_out, fuel_out, heat_out):
    rows, cols = fuel_ref.shape
    hx = (ext_ref.shape[1] - rows) // 2
    hy = (ext_ref.shape[2] - cols) // 2
    width = ext_ref.shape[2]

    def interior(a, off=hx):
        return pltpu.roll(a[off : off + rows], (width - hy) % width, 1)[:, :cols]
    level = ext_ref[0]
    cat = ext_ref[1]
    nsteps = ext_ref[2]
    spread = lookup(tab_ref, cat, 0, 0.0)
    gain = lookup(tab_ref, cat, 1, 0.0)
    cat_in = interior(cat)
    burnout = lookup(tab_ref, cat_in, 2, 1.0)
    yields = lookup(tab_ref, cat_in, 3, 0.0)
    nsteps_in = interior(nsteps)
    wind_u = wind_ref[0]
    wind_v = wind_ref[1]
    remaining = fuel_ref[...]
    heating = jnp.zeros_like(remaining)
    off = hx
    for substep in range(SUBSTEPS):
        trim = (off - 2 * (SUBSTEPS - substep)) // 8 * 8
        if trim > 0:
            level, spread, gain, wind_u, wind_v, nsteps = (
                a[trim : a.shape[0] - trim] for a in (level, spread, gain, wind_u, wind_v, nsteps)
            )
            off -= trim
        xm1 = shift(level, -1, 0)
        xp1 = shift(level, 1, 0)
        ym1 = shift(level, -1, 1)
        yp1 = shift(level, 1, 1)
        back_x = level - xm1
        ahead_x = xp1 - level
        back_y = level - ym1
        ahead_y = yp1 - level
        upwind = jnp.sqrt(
            jnp.maximum(back_x, 0.0) ** 2
            + jnp.minimum(ahead_x, 0.0) ** 2
            + jnp.maximum(back_y, 0.0) ** 2
            + jnp.minimum(ahead_y, 0.0) ** 2
        )
        slope_x = (shift(level, -2, 0) - 8.0 * xm1 + 8.0 * xp1 - shift(level, 2, 0)) / 12.0
        slope_y = (shift(level, -2, 1) - 8.0 * ym1 + 8.0 * yp1 - shift(level, 2, 1)) / 12.0
        pushing = jnp.maximum(wind_u * slope_x + wind_v * slope_y, 0.0)
        moved = level - spread * (upwind + gain * pushing)
        burned = remaining / (1.0 + jnp.exp(interior(moved, off))) / burnout
        active = float(substep) < nsteps_in
        remaining = jnp.where(active, remaining - burned, remaining)
        heating = heating + jnp.where(active, yields * burned, 0.0)
        level = jnp.where(float(substep) < nsteps, moved, level)
    level_out[...] = interior(level, off)
    fuel_out[...] = remaining
    heat_rows = heating.reshape(rows // RF, RF, cols).sum(axis=1)
    lane_in = lax.broadcasted_iota(jnp.int32, (cols, cols // RF), 0) // RF
    lane_out = lax.broadcasted_iota(jnp.int32, (cols, cols // RF), 1)
    blocks = (lane_in == lane_out).astype(jnp.float32)
    heat_out[...] = jnp.dot(
        heat_rows, blocks, precision=lax.Precision.HIGHEST, preferred_element_type=jnp.float32
    ) / (RF * RF)


def fire_step(tables, ext, winds, fuel_left):
    rows, cols = fuel_left.shape
    vmem = pl.BlockSpec(memory_space=pltpu.VMEM)
    return pl.pallas_call(
        fire_kernel,
        out_shape=(
            jax.ShapeDtypeStruct((rows, cols), jnp.float32),
            jax.ShapeDtypeStruct((rows, cols), jnp.float32),
            jax.ShapeDtypeStruct((rows // RF, cols // RF), jnp.float32),
        ),
        in_specs=[pl.BlockSpec(memory_space=pltpu.SMEM), vmem, vmem, vmem],
        out_specs=(vmem, vmem, vmem),
    )(tables, ext, winds, fuel_left)


def atmos_kernel(p_ref, q_ref, lo_ref, hi_ref, y_ref, u_ref, v_ref, h_ref, o_ref, ext_ref):
    rows, cols = o_ref.shape[2], o_ref.shape[3]
    halo = lo_ref.shape[2]
    centre = q_ref[0]
    ext_ref[:, 0:halo, :] = lo_ref[0]
    ext_ref[:, halo : halo + rows, :] = centre
    ext_ref[:, halo + rows : 2 * halo + rows, :] = hi_ref[0]
    ends = y_ref[0]
    lane = lax.broadcasted_iota(jnp.int32, centre.shape, 2)

    def ax(dx):
        return ext_ref[:, halo + dx : halo + dx + rows, :]

    def ay(dy):
        if dy > 0:
            turn = cols - dy
            return jnp.where(lane >= turn, pltpu.roll(ends, turn, 2), pltpu.roll(centre, turn, 2))
        return jnp.where(lane < -dy, pltpu.roll(ends, -dy, 2), pltpu.roll(centre, -dy, 2))

    deriv_x = (
        ax(3) - 9.0 * ax(2) + 45.0 * ax(1) - 45.0 * ax(-1) + 9.0 * ax(-2) - ax(-3)
    ) / 60.0
    deriv_y = (
        ay(3) - 9.0 * ay(2) + 45.0 * ay(1) - 45.0 * ay(-1) + 9.0 * ay(-2) - ay(-3)
    ) / 60.0
    laplace = ax(1) + ax(-1) + ay(1) + ay(-1) - 4.0 * centre
    updated = centre - COURANT * (u_ref[0] * deriv_x + v_ref[0] * deriv_y) + DIFFUSE * laplace
    heat = h_ref[...]
    profile_heat = jnp.stack([heat * p_ref[k] for k in range(updated.shape[0])])
    o_ref[0] = jnp.where(pl.program_id(0) == 3, updated + profile_heat, updated)


def atmos_call(atmos, x_lo, x_hi, y_ends, heat_atm):
    fields, depth, rows, cols = atmos.shape
    halo = x_lo.shape[2]
    profile = jnp.exp(-4.0 * jnp.arange(depth).astype(jnp.float32) / depth)
    block = (1, depth, rows, cols)
    edge = (1, depth, halo, cols)
    return pl.pallas_call(
        atmos_kernel,
        grid=(fields,),
        out_shape=jax.ShapeDtypeStruct((fields, depth, rows, cols), jnp.float32),
        in_specs=[
            pl.BlockSpec(memory_space=pltpu.SMEM),
            pl.BlockSpec(block, lambda f: (f, 0, 0, 0)),
            pl.BlockSpec(edge, lambda f: (f, 0, 0, 0)),
            pl.BlockSpec(edge, lambda f: (f, 0, 0, 0)),
            pl.BlockSpec(block, lambda f: (f, 0, 0, 0)),
            pl.BlockSpec(block, lambda f: (0, 0, 0, 0)),
            pl.BlockSpec(block, lambda f: (1, 0, 0, 0)),
            pl.BlockSpec((rows, cols), lambda f: (0, 0)),
        ],
        out_specs=pl.BlockSpec(block, lambda f: (f, 0, 0, 0)),
        scratch_shapes=[pltpu.VMEM((depth, -(-(rows + 2 * halo) // 8) * 8, cols), jnp.float32)],
    )(profile, atmos, x_lo, x_hi, y_ends, atmos, atmos, heat_atm)


def fire_halo(level):
    return extended(level, (("gx", 0), ("gy", 1)), 2)


def shards(
    atmos,
    level_set,
    fuel_left,
    fuel_map,
    spread_rate,
    wind_factor,
    burn_time,
    heat_yield,
    burn_tiles,
    burn_count,
    substep_count,
):
    fire_rows, fire_cols = level_set.shape
    atmos_rows, atmos_cols = (atmos.shape[2], atmos.shape[3])
    count_x = lax.axis_size("gx")
    x_lo = lax.ppermute(atmos[:, :, -3:], "gx", [(i, i + 1) for i in range(count_x - 1)])
    x_hi = lax.ppermute(atmos[:, :, :3], "gx", [(i + 1, i) for i in range(count_x - 1)])
    count = lax.axis_size("gy")
    from_lo = lax.ppermute(atmos[..., -3:], "gy", [(i, i + 1) for i in range(count - 1)])
    from_hi = lax.ppermute(atmos[..., :3], "gy", [(i + 1, i) for i in range(count - 1)])
    room = jnp.zeros(atmos.shape[:3] + (atmos_cols - 6,), jnp.float32)
    y_ends = jnp.concatenate([from_hi, room, from_lo], axis=3)
    along_x = jnp.concatenate([x_lo[0:2, 0:1], atmos[0:2, 0:1], x_hi[0:2, 0:1]], axis=2)
    surface = extended(along_x[:, 0], (("gy", 2),), 3)
    slots = burn_tiles.reshape(-1)
    listed = burn_count.reshape(())
    tiles_dev = substep_count.size
    slot_valid = jnp.arange(slots.shape[0]) < listed
    tile_on = jnp.any(
        (slots[:, None] == jnp.arange(tiles_dev)[None, :]) & slot_valid[:, None], axis=0
    )
    tile_on = tile_on.reshape(substep_count.shape)
    tiles_x, tiles_y = substep_count.shape
    halo = 2 * SUBSTEPS
    nsteps = jnp.where(tile_on, substep_count, 0).astype(jnp.float32)
    nsteps = jnp.broadcast_to(nsteps[:, None, :, None], (tiles_x, TILE, tiles_y, TILE)).reshape(
        fire_rows, fire_cols
    )
    stacked = jnp.stack([level_set, fuel_map.astype(jnp.float32), nsteps])
    stacked = extended(stacked, (("gx", 1), ("gy", 2)), halo)
    room = jnp.zeros(stacked.shape[:2] + (HALO_Y - halo,), jnp.float32)
    stacked = jnp.concatenate([room, stacked, room], axis=2)
    winds = surface_winds(surface, fire_rows, fire_cols, halo, HALO_Y)
    tables = jnp.concatenate([spread_rate, wind_factor, burn_time, heat_yield]).astype(jnp.float32)
    level, remaining, heat_atm = fire_step(tables, stacked, winds, fuel_left)
    return (atmos_call(atmos, x_lo, x_hi, y_ends, heat_atm), level, remaining)


def solution(mesh):
    return jax.shard_map(
        shards,
        mesh=mesh,
        in_specs=(
            P(None, None, "gx", "gy"),
            P("gx", "gy"),
            P("gx", "gy"),
            P("gx", "gy"),
            P(),
            P(),
            P(),
            P(),
            P("gx", "gy", None),
            P("gx", "gy"),
            P("gx", "gy"),
        ),
        out_specs=(P(None, None, "gx", "gy"), P("gx", "gy"), P("gx", "gy")),
        check_vma=False,
    )
```
